256 devices in a mesh: req: 8 (over x, core), pg: 32 (over y, z).
Axes of the slice: x: 4, y: 4, z: 8, core: 2. Of those that a mesh axis runs over, the one named last changes fastest.
Arguments:
- tokens: bfloat16 [16384, 1024], P(('req', 'pg')), may hold values from -15 to 15
- variate_ids: int32 [16384], P('req'), may hold values from 0 to 3
- cache_pages: int32 [16], P('req'), may hold values from 1 to 96, 768 in all
- page_table: int32 [16, 96], P('req'), may hold values from 0 to 191, as said below
- kv_cache: bfloat16 [1536, 128, 2048], P(('req', 'pg')), may hold values from -104 to 104
- cache_variates: int32 [1536, 128], P(('req', 'pg')), may hold values from 0 to 3
- attn_gain: float32 [1024], replicated, may hold values from 0.25 to 1.75
- w_query: bfloat16 [1024, 1024], P('req', 'pg'), may hold values from -0.1875 to 0.1875
- w_keyval: bfloat16 [1024, 2048], P('req', 'pg'), may hold values from -0.1875 to 0.1875
- w_out: bfloat16 [1024, 1024], P('req', 'pg'), may hold values from -0.1875 to 0.1875
- variate_bias: float32 [2, 16], replicated, may hold values from -3 to 3
- head_gain: float32 [1024], replicated, may hold values from 0.25 to 1.75
- w_head: bfloat16 [1024, 256], P('req', 'pg'), may hold values from -0.1875 to 0.1875
Outputs:
- hidden_out: bfloat16 [16384, 1024], P(('req', 'pg'))
- appended_kv: bfloat16 [16384, 2048], P(('req', 'pg'))
- mix_logits: bfloat16 [16384, 256], P(('req', 'pg'))
- request_norm: float32 [16], P('req')
- request_peak: float32 [16], P('req')
The draws below stay inside these ranges and needn't reach their ends.
Inputs may be any that keep to these rules, and one draw needn't show every extreme that they name: Row r of page_table lists 96 entries; entry e places logical page n of request r in slot e mod 6 of the device with pg index e // 6 among the devices of r's req index. The rows of the 2 requests of one req index together hold every value once.
All inputs are finite; a program needn't handle non-finite values. No bound on the sum of `cache_pages` on one device may be relied on, other than what follows from the above.
Results may differ from the reference program's by a relative error of at most 0.017.
Values may be sent and summed in bfloat16 or wider, within the bound.
No kernel may reach another device: no remote copies, remote signals or barrier semaphores. Data moves between devices by JAX's collectives and lax.ppermute only.
A program may use at most 128 MiB of HBM per device.

```python
import math
import jax
import jax.numpy as jnp
import numpy as np
from jax import lax

D = 1024
H = 16
DH = 64
MIXW = 256
NVAR = 4
PAGE = 128
REQ_DEV = 2
TOK_DEV = 64
SLOTS = 6
REQUESTS = 16
FRESH = 1024
MAXPAGES = 96
TOKENS = 16384
CACHE_SLOTS = 1536
N_PG = 32


def draw_tokens(key, part):
    row_index = jnp.arange(TOKENS, dtype=jnp.int32) % FRESH
    ramp_rows = row_index.astype(jnp.float32) / FRESH
    base_draw = jnp.clip(jax.random.normal(key, (TOKENS, D), jnp.float32), -5.0, 5.0)
    row_scale = jnp.exp(jnp.log(3.0) * ramp_rows)
    return (base_draw * row_scale[:, None]).astype(jnp.bfloat16)


def draw_page_table(key, part):
    group_count = REQUESTS // REQ_DEV
    group_keys = jax.random.split(key, group_count)
    orders = jax.vmap(lambda group_key: jax.random.permutation(group_key, REQ_DEV * MAXPAGES))(group_keys)
    return orders.reshape(REQUESTS, MAXPAGES).astype(jnp.int32)


def draw_kv_cache(key, part):
    full_shape = (CACHE_SLOTS, PAGE, 2 * D)
    return jnp.clip(jax.random.normal(key, full_shape, jnp.float32), -6.0, 6.0).astype(jnp.bfloat16)


def touch_ends(drawn, key, low, largest):
    spot = [jax.random.randint(jax.random.fold_in(key, axis), (), 0, length) for axis, length in enumerate(drawn.shape)]
    widest = drawn.shape.index(max(drawn.shape))
    neighbour = spot[:widest] + [(spot[widest] + 1) % drawn.shape[widest]] + spot[widest + 1:]
    return drawn.at[tuple(spot)].set(low).at[tuple(neighbour)].set(largest)


def shard_levels(key, extent, shards, least, largest):
    level = 1.0
    for position, parts in shards:
        draws = jax.random.uniform(jax.random.fold_in(jax.random.fold_in(key, 6), position), (parts,), jnp.float32, least / len(shards), largest / len(shards))
        level = level * jnp.repeat(jnp.exp(draws), extent[position] // parts).reshape((-1,) + (1,) * (len(extent) - 1 - position))
    return level


def profile(number_of, total, bound, skew):
    portions = [(1 << 20) // math.isqrt(standing ** skew) + 1 for standing in range(2, number_of + 1)]
    surplus, given = total - bound - (number_of - 1), [1] * (number_of - 1)
    while surplus > 0:
        movable = [i for i in range(number_of - 1) if given[i] < bound]
        mass, left = sum([portions[i] for i in movable]), surplus
        for i in movable:
            extra = min(bound - given[i], max(1, left * portions[i] // mass), surplus)
            given[i] = given[i] + extra
            surplus = surplus - extra
    return np.array([bound] + given)


def ragged_sizes(key, count, total, limit, lean):
    if count == 2:
        one = jax.random.randint(key, (), max(1, total - limit), min(limit, total - 1) + 1)
        return jnp.stack([one, total - one])
    tallies = jnp.asarray(profile(count, total, limit, lean), jnp.int32)
    twos = (count - 1) // 2
    giver, sink = tallies[1:1 + 2 * twos:2], tallies[2:2 + 2 * twos:2]
    margin = jnp.minimum(giver - 1, limit - sink)
    moved = jax.random.randint(jax.random.fold_in(key, 1), (twos,), 0, 1 << 20) % (margin + 1)
    tallies = tallies.at[1:1 + 2 * twos:2].set(giver - moved).at[2:2 + 2 * twos:2].set(sink + moved)
    return tallies[jax.random.permutation(jax.random.fold_in(key, 2), count)]


def scatter_about(key, extent, scale, limit, shards=(), kind=jnp.bfloat16):
    values = jax.random.normal(key, extent, jnp.float32) * scale
    if len(shards) > 0:
        values = shard_levels(key, extent, shards, -0.22, 0.18) * values
    return jnp.clip(values, min=-limit, max=limit).astype(kind)


def setup_inputs(seed: int = 0) -> dict:
    key_list = jax.random.split(jax.random.key(seed), 14)
    return {
        "tokens": draw_tokens(jax.random.fold_in(key_list[13], 71), 0),
        "variate_ids": touch_ends(jax.random.randint(key_list[1], (TOKENS,), 0, NVAR), jax.random.fold_in(key_list[1], 1), 0, NVAR - 1).astype(jnp.int32),
        "cache_pages": ragged_sizes(key_list[2], REQUESTS, REQUESTS * MAXPAGES // 2, MAXPAGES, 2).astype(jnp.int32),
        "page_table": draw_page_table(jax.random.fold_in(key_list[13], 71), 0),
        "kv_cache": draw_kv_cache(jax.random.fold_in(key_list[13], 71), 0),
        "cache_variates": touch_ends(jax.random.randint(key_list[5], (CACHE_SLOTS, PAGE), 0, NVAR), jax.random.fold_in(key_list[5], 1), 0, NVAR - 1).astype(jnp.int32),
        "attn_gain": jnp.clip(1.0 + 0.15 * jax.random.normal(key_list[6], (D,), jnp.float32), 0.25, 1.75),
        "w_query": scatter_about(key_list[7], (D, D), D ** -0.5, 0.1875, ((0, 8), (1, 32))),
        "w_keyval": scatter_about(key_list[8], (D, 2 * D), D ** -0.5, 0.1875, ((0, 8), (1, 32))),
        "w_out": scatter_about(key_list[9], (D, D), D ** -0.5, 0.1875, ((0, 8), (1, 32))),
        "variate_bias": scatter_about(key_list[10], (2, H), 1.0, 3.0, (), jnp.float32),
        "head_gain": jnp.clip(1.0 + 0.15 * jax.random.normal(key_list[11], (D,), jnp.float32), 0.25, 1.75),
        "w_head": scatter_about(key_list[12], (D, MIXW), D ** -0.5, 0.1875, ((0, 8), (1, 32))),
    }


EPSILON = 1e-05
NEGATIVE = -1e+30

def rms_norm(values, gain):
    wide = values.astype(jnp.float32)
    power = lax.optimization_barrier(jnp.mean(wide * wide, axis=-1, keepdims=True))
    return (wide * lax.rsqrt(power + EPSILON) * gain.astype(jnp.float32)).astype(jnp.bfloat16)

def rope_angles(positions, half_width):
    steps = jnp.arange(half_width, dtype=jnp.float32) / half_width
    freqs = jnp.exp(-math.log(10000.0) * steps)
    angle = positions.astype(jnp.float32)[:, None] * freqs[None, :]
    return (jnp.cos(angle), jnp.sin(angle))

def rotate(values, cosine, sine_part, head_count):
    count = values.shape[0]
    halves = values.astype(jnp.float32).reshape(count, head_count, 2, -1)
    front_half = halves[:, :, 0, :]
    second = halves[:, :, 1, :]
    cosine_wide = cosine[:, None, :]
    sine_wide = sine_part[:, None, :]
    turned = jnp.stack([front_half * cosine_wide - second * sine_wide, second * cosine_wide + front_half * sine_wide], axis=2)
    return turned.reshape(count, -1).astype(jnp.bfloat16)

def lookup_small(table_rows, lookup_index, count):
    matches = lookup_index[:, None] == jnp.arange(count, dtype=jnp.int32)[None, :]
    return lax.optimization_barrier(jnp.sum(jnp.where(matches, table_rows[None, :], 0), axis=1)).astype(jnp.int32)

def slot_owners(table_rows, pages_held, slot_base, count):
    request_count, page_count = table_rows.shape
    slot_ids = slot_base + jnp.arange(count, dtype=jnp.int32)
    matches = table_rows[:, :, None] == slot_ids[None, None, :]
    live_pages = jnp.arange(page_count, dtype=jnp.int32)[None, :, None] < pages_held[:, None, None]
    live_hits = matches & live_pages
    used = jnp.any(live_hits, axis=(0, 1))
    request_ids = lax.optimization_barrier(jnp.sum(jnp.where(live_hits, jnp.arange(request_count, dtype=jnp.int32)[:, None, None], 0), axis=(0, 1))).astype(jnp.int32)
    return (used, request_ids)

def block_stats(query_rows, key_rows, value_rows, allowed, same_var, variate_bias, head_count):
    count = query_rows.shape[0]
    width = key_rows.shape[0]
    query_heads = query_rows.astype(jnp.float32).reshape(count, head_count, -1)
    key_heads = key_rows.astype(jnp.float32).reshape(width, head_count, -1)
    value_heads = value_rows.astype(jnp.float32).reshape(width, head_count, -1)
    scaling = 1.0 / math.sqrt(query_heads.shape[2])
    scores = jnp.einsum('qhd,khd->qhk', query_heads, key_heads) * scaling
    variate_term = jnp.where(same_var[:, None, :], variate_bias[0][None, :, None], variate_bias[1][None, :, None])
    masked = jnp.where(allowed[:, None, :], scores + variate_term, NEGATIVE)
    block_peak = lax.optimization_barrier(jnp.max(masked, axis=2))
    block_exps = jnp.where(allowed[:, None, :], jnp.exp(masked - block_peak[:, :, None]), 0.0)
    block_total = lax.optimization_barrier(jnp.sum(block_exps, axis=2))
    block_weights = block_exps.astype(jnp.bfloat16).astype(jnp.float32)
    summed = jnp.einsum('qhk,khd->qhd', block_weights, value_heads)
    return (block_peak, block_total, summed)

def merge_state(carry_state, block_part):
    old_peak, old_total, old_summed = carry_state
    new_peak, new_total, new_summed = block_part
    running_peak = jnp.maximum(old_peak, new_peak)
    keep_factor = jnp.exp(old_peak - running_peak)
    take_factor = jnp.exp(new_peak - running_peak)
    return (running_peak, old_total * keep_factor + new_total * take_factor, old_summed * keep_factor[..., None] + new_summed * take_factor[..., None])

def keep_same(carry_state):
    return carry_state

def group_attention(queries, new_pairs, group_ids, pages_held, table_rows, cache_group, cache_ids, variate_bias):
    used, slot_request = slot_owners(table_rows, pages_held, 0, N_PG * SLOTS)

    def one_request(request):
        query_rows = lax.dynamic_slice_in_dim(queries, request * FRESH, FRESH, 0)
        query_ids = lax.dynamic_slice_in_dim(group_ids, request * FRESH, FRESH, 0)
        start_state = (jnp.full((FRESH, H), NEGATIVE, jnp.float32), jnp.zeros((FRESH, H), jnp.float32), jnp.zeros((FRESH, H, DH), jnp.float32))

        def visit(carry_state, entry):

            def work(inner_state):
                page = lax.dynamic_index_in_dim(cache_group, entry, 0, keepdims=False)
                page_ids = lax.dynamic_index_in_dim(cache_ids, entry, 0, keepdims=False)
                allowed = jnp.ones((FRESH, PAGE), dtype=jnp.bool_)
                same_var = query_ids[:, None] == page_ids[None, :]
                return merge_state(inner_state, block_stats(query_rows, page[:, :D], page[:, D:], allowed, same_var, variate_bias, H))
            take = used[entry] & (slot_request[entry] == request)
            return (lax.cond(take, work, keep_same, carry_state), None)
        state, _ = lax.scan(visit, start_state, jnp.arange(N_PG * SLOTS, dtype=jnp.int32))

        def fresh_step(inner_state, block):
            begin_row = block * TOK_DEV

            def fresh_block(block_state):
                block_rows = lax.dynamic_slice_in_dim(new_pairs, begin_row, TOK_DEV, 0)
                block_ids = lax.dynamic_slice_in_dim(group_ids, begin_row, TOK_DEV, 0)
                offset = begin_row % FRESH
                allowed = (offset + jnp.arange(TOK_DEV, dtype=jnp.int32))[None, :] <= jnp.arange(FRESH, dtype=jnp.int32)[:, None]
                same_var = query_ids[:, None] == block_ids[None, :]
                return merge_state(block_state, block_stats(query_rows, block_rows[:, :D], block_rows[:, D:], allowed, same_var, variate_bias, H))
            return (lax.cond(begin_row // FRESH == request, fresh_block, keep_same, inner_state), None)
        state, _ = lax.scan(fresh_step, state, jnp.arange(N_PG, dtype=jnp.int32))
        return (state[2] / state[1][..., None]).reshape(FRESH, D).astype(jnp.bfloat16)
    return lax.map(one_request, jnp.arange(REQ_DEV, dtype=jnp.int32))

def reference(tokens, variate_ids, cache_pages, page_table, kv_cache, cache_variates, attn_gain, w_query, w_keyval, w_out, variate_bias, head_gain, w_head):
    normed = rms_norm(tokens, attn_gain)
    query_raw = jnp.dot(normed, w_query, preferred_element_type=jnp.float32).astype(jnp.bfloat16)
    keyval_raw = jnp.dot(normed, w_keyval, preferred_element_type=jnp.float32).astype(jnp.bfloat16)
    row_index = jnp.arange(TOKENS, dtype=jnp.int32)
    positions = lookup_small(cache_pages, row_index // FRESH, REQUESTS) * PAGE + row_index % FRESH
    cosine, sine_part = rope_angles(positions, DH // 2)
    queries = rotate(query_raw, cosine, sine_part, H)
    new_keys = rotate(keyval_raw[:, :D], cosine, sine_part, H)
    appended = jnp.concatenate([new_keys, keyval_raw[:, D:]], axis=1)
    group_count = REQUESTS // REQ_DEV
    span = REQ_DEV * FRESH
    group_slots = N_PG * SLOTS

    def per_group(group_index):
        return group_attention(lax.dynamic_slice_in_dim(queries, group_index * span, span, 0), lax.dynamic_slice_in_dim(appended, group_index * span, span, 0), lax.dynamic_slice_in_dim(variate_ids, group_index * span, span, 0), lax.dynamic_slice_in_dim(cache_pages, group_index * REQ_DEV, REQ_DEV, 0), lax.dynamic_slice_in_dim(page_table, group_index * REQ_DEV, REQ_DEV, 0), lax.dynamic_slice_in_dim(kv_cache, group_index * group_slots, group_slots, 0), lax.dynamic_slice_in_dim(cache_variates, group_index * group_slots, group_slots, 0), variate_bias)
    attention = lax.map(per_group, jnp.arange(group_count, dtype=jnp.int32)).reshape(TOKENS, D)
    hidden = (tokens.astype(jnp.float32) + jnp.dot(attention, w_out, preferred_element_type=jnp.float32)).astype(jnp.bfloat16)
    head_in = rms_norm(hidden, head_gain)
    logits = jnp.dot(head_in, w_head, preferred_element_type=jnp.float32)
    wide = hidden.astype(jnp.float32)
    energy = lax.optimization_barrier(jnp.sum((wide * wide).reshape(REQUESTS, FRESH * D), axis=1))
    peaks = lax.optimization_barrier(jnp.max(logits.reshape(REQUESTS, FRESH * MIXW), axis=1))
    return (hidden, appended, logits.astype(jnp.bfloat16), jnp.sqrt(energy), peaks)
```

```python
import math

import jax
import jax.numpy as jnp
from jax import lax
from jax.experimental import pallas as pl
from jax.experimental.pallas import tpu as pltpu
from jax.sharding import Mesh
from jax.sharding import PartitionSpec as P

PAGE = 128
EPSILON = 1e-05
NEGATIVE = -1e30
NY = 4
NZ = 8
NR = 8
SLOTS = 6
ROWS = 64
HEADS = 4
DH = 64
F32 = jnp.float32
BF16 = jnp.bfloat16
VMEM_LIMIT = 48 * 1024 * 1024


def shift(axis, size, step):
    return lambda value: lax.ppermute(
        value, axis, [(i, (i + step) % size) for i in range(size)]
    )


def rms_norm(values, gain):
    wide = values.astype(F32)
    power = jnp.mean(wide * wide, axis=-1, keepdims=True)
    return (wide * lax.rsqrt(power + EPSILON) * gain).astype(BF16)


def vmem():
    return pl.BlockSpec(memory_space=pltpu.VMEM)


def smem():
    return pl.BlockSpec(memory_space=pltpu.SMEM)


def anym():
    return pl.BlockSpec(memory_space=pl.ANY)


def params():
    return pltpu.CompilerParams(vmem_limit_bytes=VMEM_LIMIT)


def dot_last(a, b):
    return lax.dot_general(a, b, (((1,), (1,)), ((), ())), preferred_element_type=F32)


def carve_kernel(idx, kv, variates, *refs):
    outs = refs[0:3]
    side, sem = refs[3:5]
    y = idx[1]
    rows = SLOTS * PAGE
    side[...] = jnp.zeros(side.shape, BF16)
    side[0:8, 0:128] = jnp.concatenate(
        [variates[...].astype(F32), jnp.zeros((2, 128), F32)], axis=0
    ).astype(BF16)
    copies = []
    for d in range(1, NY):
        yd = lax.rem(y + d, NY)
        for half in range(2):
            low = pl.multiple_of(half * 1024 + yd * 256, 256)
            copies.append(
                pltpu.make_async_copy(
                    kv.at[:, pl.ds(low, 256)],
                    outs[d - 1].at[pl.ds(0, rows), pl.ds(half * 256, 256)],
                    sem.at[2 * d - 2 + half],
                )
            )
    for c in copies:
        c.start()
    for d in range(1, NY):
        outs[d - 1][rows : rows + 16, :] = side[...]
    for c in copies:
        c.wait()


def carve(idx, kv, variates):
    return pl.pallas_call(
        carve_kernel,
        out_shape=[jax.ShapeDtypeStruct((SLOTS * PAGE + 16, 512), BF16)] * 3,
        in_specs=[smem(), anym(), vmem()],
        out_specs=[vmem()] * 3,
        scratch_shapes=[pltpu.VMEM((16, 512), BF16), pltpu.SemaphoreType.DMA((6,))],
        compiler_params=params(),
    )(idx, kv, variates)


def qkv_kernel(tok, w, cos_ref, sin_ref, q_out, app_out, acc, feats):
    for r in range(NR):
        part = dot_last(w[r].reshape(NZ * 96, 128), tok[:, r * 128 : (r + 1) * 128])
        if r == 0:
            acc[...] = part
        else:
            acc[...] += part
    cos = cos_ref[...]
    sin = sin_ref[...]

    def rounded(zs, low, high):
        return acc[zs * 96 + low : zs * 96 + high, :].astype(BF16).astype(F32)

    for h in range(HEADS):
        a = rounded(2 * h, 0, 32)
        b = rounded(2 * h + 1, 0, 32)
        first = ((a * cos - b * sin).astype(BF16).astype(F32) * 0.125).astype(BF16)
        second = ((b * cos + a * sin).astype(BF16).astype(F32) * 0.125).astype(BF16)
        for zs in range(NZ):
            q_out[zs, h * 64 : h * 64 + 32, :] = first
            q_out[zs, h * 64 + 32 : h * 64 + 64, :] = second
        a = rounded(h, 32, 64)
        b = rounded(h, 64, 96)
        feats[h * 64 : h * 64 + 32, :] = a * cos - b * sin
        feats[h * 64 + 32 : h * 64 + 64, :] = b * cos + a * sin
        feats[256 + h * 64 : 256 + h * 64 + 64, :] = acc[(HEADS + h) * 96 + 32 : (HEADS + h) * 96 + 96, :]
    app_out[:, 0:256] = feats[0:256, :].T.astype(BF16)
    app_out[:, 256:512] = feats[256:512, :].T.astype(BF16)


def project(tok, w, cos, sin):
    return pl.pallas_call(
        qkv_kernel,
        out_shape=[
            jax.ShapeDtypeStruct((NZ, 256, 256), BF16),
            jax.ShapeDtypeStruct((256, 512), BF16),
        ],
        in_specs=[vmem()] * 4,
        out_specs=[vmem()] * 2,
        scratch_shapes=[pltpu.VMEM((NZ * 96, 256), F32), pltpu.VMEM((512, 256), F32)],
        compiler_params=params(),
    )(tok, w, cos, sin)


def attn_kernel(idx, used, owner, bias, *refs):
    q, kv, p1, p2, p3, app, own_vars, fresh_vars, qvar = refs[0:9]
    out = refs[9]
    pg, qb, top, acc, side, kvs, causal, sem = refs[10:18]
    y, z = idx[1], idx[2]
    rows = SLOTS * PAGE
    copies = []
    for half in range(2):
        low = pl.multiple_of(half * 1024 + y * 256, 256)
        copies.append(
            pltpu.make_async_copy(
                kv.at[:, pl.ds(low, 256)],
                pg.at[pl.ds(0, rows), pl.ds(half * 256, 256)],
                sem.at[half],
            )
        )
    for d, piece in enumerate((p1, p2, p3)):
        copies.append(
            pltpu.make_async_copy(
                piece.at[pl.ds(0, rows)], pg.at[pl.ds((d + 1) * rows, rows)], sem.at[2 + d]
            )
        )
        copies.append(
            pltpu.make_async_copy(
                piece.at[pl.ds(rows, 16), pl.ds(0, 128)], side.at[d], sem.at[5 + d]
            )
        )
    copies.append(pltpu.make_async_copy(app, pg.at[pl.ds(NY * rows, 256)], sem.at[8]))
    for c in copies:
        c.start()

    row16 = lax.broadcasted_iota(jnp.int32, (16, 128), 0)
    vsel = row16 & 3
    level = row16 >> 2
    zero = jnp.zeros((48, 128), BF16)

    def fill(zs, carry):
        lanes = pl.ds(pl.multiple_of(zs * 128, 128), 128)
        qv_row = qvar[zs]
        for j in range(2):
            same = jnp.broadcast_to(qv_row[:, j * 128 : (j + 1) * 128], (16, 128)) == vsel
            for h in range(HEADS):
                hh = y * HEADS + h
                b = jnp.where(same, bias[0, hh], bias[1, hh])
                hi = b.astype(BF16).astype(F32)
                mid = (b - hi).astype(BF16).astype(F32)
                lo = (b - hi - mid).astype(BF16).astype(F32)
                extra = jnp.where(
                    level == 0, hi, jnp.where(level == 1, mid, jnp.where(level == 2, lo, 0.0))
                ).astype(BF16)
                q_rows = q[zs, h * 64 : (h + 1) * 64, j * 128 : (j + 1) * 128]
                if h % 2 == 0:
                    qb[j, h, 0:64, lanes] = q_rows
                    qb[j, h, 64:80, lanes] = extra
                    qb[j, h, 80:128, lanes] = zero
                else:
                    qb[j, h, 0:16, lanes] = extra
                    qb[j, h, 16:64, lanes] = zero
                    qb[j, h, 64:128, lanes] = q_rows
        key_row = lax.broadcasted_iota(jnp.int32, (128, 128), 0)
        q_lane = lax.broadcasted_iota(jnp.int32, (128, 128), 1)
        key_pos = ((key_row >> 6) * NZ + z) * ROWS + (key_row & 63)
        q_pos = ((q_lane >> 6) * NZ + zs) * ROWS + (q_lane & 63)
        causal[:, lanes] = jnp.where(key_pos <= q_pos, 0.0, NEGATIVE)
        return carry

    lax.fori_loop(0, NZ, fill, 0)
    top[...] = jnp.full(top.shape, NEGATIVE, F32)
    acc[...] = jnp.zeros(acc.shape, F32)
    for s in range(SLOTS):
        kvs[s] = own_vars[s : s + 1, :].astype(F32)
    for j in range(2):
        kvs[NY * SLOTS + j] = fresh_vars[j : j + 1, :].astype(F32)
    for c in copies:
        c.wait()
    for d in range(3):
        block = side[d].astype(F32)
        for s in range(SLOTS):
            kvs[(d + 1) * SLOTS + s] = block[s : s + 1, :]

    sub = lax.broadcasted_iota(jnp.int32, (128, 128), 0)
    variate = (sub & 3).astype(F32)
    hot_rows = (sub & 63) < 12
    low_lanes = lax.broadcasted_iota(jnp.int32, (128, 128), 1) < 64
    ones = jnp.ones((16, 128), BF16)

    def visit(slot, j, fresh):
        page = pg[pl.ds(pl.multiple_of(slot * PAGE, PAGE), PAGE), :]
        kvals = jnp.broadcast_to(kvs[slot], (128, 128))
        hot = jnp.where(hot_rows & (variate == kvals), 1.0, 0.0).T
        keys = page[:, 0:256].astype(F32)
        vals = page[:, 256:512].astype(F32).T.astype(BF16)
        kaug = []
        vaug = []
        for h in range(HEADS):
            pair = keys[:, (h // 2) * 128 : (h // 2) * 128 + 128]
            both = (pair, hot) if h % 2 == 0 else (hot, pair)
            kaug.append(jnp.where(low_lanes, both[0], both[1]).astype(BF16))
            vaug.append(jnp.concatenate([vals[h * 64 : (h + 1) * 64, :], ones], axis=0))
        olds = [top[j, h] for h in range(HEADS)]
        scores = {}
        weights = {}
        for i in range(HEADS + 2):
            if i < HEADS:
                s = jnp.dot(kaug[i], qb[j, i], preferred_element_type=F32)
                scores[i] = s + causal[...] if fresh else s
            if 1 <= i <= HEADS:
                k = i - 1
                s = scores.pop(k)
                new = jnp.maximum(olds[k], jnp.max(s, axis=0, keepdims=True))
                weights[k] = (jnp.exp(s - new).astype(BF16), new, jnp.exp(olds[k] - new))
            if i >= 2:
                k = i - 2
                p, new, keep = weights.pop(k)
                top[j, k] = new
                acc[j, k] = acc[j, k] * keep + jnp.dot(vaug[k], p, preferred_element_type=F32)

    def body(slot, carry):
        @pl.when(used[slot] > 0)
        def _():
            visit(slot, owner[slot], False)

        return carry

    lax.fori_loop(0, NY * SLOTS, body, 0)

    def last(j, carry):
        visit(NY * SLOTS + j, j, True)
        return carry

    lax.fori_loop(0, 2, last, 0)

    low64 = lax.broadcasted_iota(jnp.int32, (64, 128), 1) < 64
    low8 = lax.broadcasted_iota(jnp.int32, (8, 128), 1) < 64

    def send(zs, carry):
        lanes = pl.ds(pl.multiple_of(zs * 128, 128), 128)
        for j in range(2):
            values = []
            parts = []
            for h in range(HEADS):
                total = acc[j, h, 64:65, lanes]
                values.append(acc[j, h, 0:64, lanes] * (1.0 / total))
                lse = top[j, h, :, lanes] + jnp.log(total)
                hi = lse.astype(BF16).astype(F32)
                mid = (lse - hi).astype(BF16).astype(F32)
                parts.append(jnp.concatenate([hi, mid, lse - hi - mid], axis=0))
            blank = jnp.zeros((2, 128), F32)
            stat_a = jnp.concatenate([parts[0], parts[1], blank], axis=0)
            stat_b = jnp.concatenate([parts[2], parts[3], blank], axis=0)
            for side_row in range(2):
                p = (2 * j + side_row) * NZ + zs

                def pick(left, right, mask):
                    if side_row == 0:
                        return jnp.where(mask, left, pltpu.roll(right, 64, 1)).astype(BF16)
                    return jnp.where(mask, pltpu.roll(left, 64, 1), right).astype(BF16)

                out[p, 0:64, :] = pick(values[0], values[2], low64)
                out[p, 64:128, :] = pick(values[1], values[3], low64)
                out[p, 128:136, :] = pick(stat_a, stat_b, low8)
        return carry

    lax.fori_loop(0, NZ, send, 0)


def attend(idx, used, owner, bias, q, kv, pieces, app, own_vars, fresh_vars, qvar):
    return pl.pallas_call(
        attn_kernel,
        out_shape=jax.ShapeDtypeStruct((NY * NZ, 136, 128), BF16),
        in_specs=[smem()] * 4 + [vmem()] + [anym()] * 5 + [vmem()] * 3,
        out_specs=vmem(),
        scratch_shapes=[
            pltpu.VMEM((26 * PAGE, 512), BF16),
            pltpu.VMEM((2, HEADS, 128, 1024), BF16),
            pltpu.VMEM((2, HEADS, 1, 1024), F32),
            pltpu.VMEM((2, HEADS, 80, 1024), F32),
            pltpu.VMEM((3, 16, 128), BF16),
            pltpu.VMEM((26, 1, 128), F32),
            pltpu.VMEM((128, 1024), F32),
            pltpu.SemaphoreType.DMA((9,)),
        ],
        compiler_params=params(),
    )(idx, used, owner, bias, q, kv, *pieces, app, own_vars, fresh_vars, qvar)


def final_kernel(idx, parts, tokens, late, app_all, gain, hidden_out, logits_out, stats_out, app_out, wo, wh, head_in, sem):
    y = idx[1]
    copies = [
        pltpu.make_async_copy(late.at[:, :, pl.ds(0, 32), :], wo, sem.at[0]),
        pltpu.make_async_copy(late.at[:, :, pl.ds(32, 8), :], wh, sem.at[1]),
    ]
    own = pl.ds(pl.multiple_of(y * ROWS, ROWS), ROWS)
    for ys in range(NY):
        for half in range(2):
            copies.append(
                pltpu.make_async_copy(
                    app_all.at[ys, own, pl.ds(half * 256, 256)],
                    app_out.at[:, pl.ds(half * 1024 + ys * 256, 256)],
                    sem.at[2 + 2 * ys + half],
                )
            )
    for c in copies:
        c.start()
    chunks = []
    for ys in range(NY):
        lses = [[], []]
        for zs in range(NZ):
            stat = parts[ys * NZ + zs, 128:136, :].astype(F32)
            for k in range(2):
                lses[k].append(stat[3 * k : 3 * k + 1] + stat[3 * k + 1 : 3 * k + 2] + stat[3 * k + 2 : 3 * k + 3])
        merged = []
        for k in range(2):
            best = lses[k][0]
            for v in lses[k][1:]:
                best = jnp.maximum(best, v)
            ws = [jnp.exp(v - best) for v in lses[k]]
            total = ws[0]
            for w in ws[1:]:
                total = total + w
            inverse = 1.0 / total
            value = None
            for zs in range(NZ):
                term = parts[ys * NZ + zs, k * 64 : (k + 1) * 64, :].astype(F32) * (ws[zs] * inverse)
                value = term if value is None else value + term
            merged.append(value)
        turned = jnp.concatenate(merged, axis=0).T.astype(BF16)
        chunks.append(turned[0:64, :])
        chunks.append(turned[64:128, :])
    for c in copies:
        c.wait()
    total = tokens[...].astype(F32)
    for r in range(NR):
        total = total + dot_last(chunks[r], wo[r].reshape(1024, 128))
    hidden = total.astype(BF16)
    hidden_out[...] = hidden
    wide = hidden.astype(F32)
    square = wide * wide
    power = jnp.sum(square, axis=1, keepdims=True)
    head_in[...] = (wide * lax.rsqrt(power * (1.0 / 1024) + EPSILON) * gain[...]).astype(BF16)
    logits = None
    for r in range(NR):
        part = dot_last(head_in[:, r * 128 : (r + 1) * 128], wh[r].reshape(256, 128))
        logits = part if logits is None else logits + part
    logits_out[...] = logits.astype(BF16)
    energy = jnp.sum(power, axis=0, keepdims=True)
    peak = jnp.max(jnp.max(logits, axis=1, keepdims=True), axis=0, keepdims=True)
    row = lax.broadcasted_iota(jnp.int32, (8, 128), 0)
    tile = jnp.where(row == 0, energy, jnp.where(row == 1, peak, 0.0))
    for p in range(NY * NZ):
        stats_out[p * 8 : (p + 1) * 8, :] = tile


def finish(idx, parts, tokens, late, app_all, gain):
    return pl.pallas_call(
        final_kernel,
        out_shape=[
            jax.ShapeDtypeStruct((ROWS, 1024), BF16),
            jax.ShapeDtypeStruct((ROWS, 256), BF16),
            jax.ShapeDtypeStruct((NY * NZ * 8, 128), F32),
            jax.ShapeDtypeStruct((ROWS, 2048), BF16),
        ],
        in_specs=[smem(), vmem(), vmem(), anym(), anym(), vmem()],
        out_specs=[vmem()] * 4,
        scratch_shapes=[
            pltpu.VMEM((NR, NY * NZ, 32, 128), BF16),
            pltpu.VMEM((NR, NY * NZ, 8, 128), BF16),
            pltpu.VMEM((ROWS, 1024), BF16),
            pltpu.SemaphoreType.DMA((10,)),
        ],
        compiler_params=params(),
    )(idx, parts, tokens, late, app_all, gain)


def stats_kernel(stats, norm_out, peak_out):
    half = NY * NZ * 4
    for j in range(2):
        block = stats[j * half : (j + 1) * half, :].reshape(NY * NZ // 2, 8, 128)
        norm_out[j] = jnp.sqrt(jnp.sum(block, axis=0))[0, 0]
        peak_out[j] = jnp.max(block, axis=0)[1, 0]


def gather_stats(stats):
    return pl.pallas_call(
        stats_kernel,
        out_shape=[jax.ShapeDtypeStruct((2,), F32)] * 2,
        in_specs=[vmem()],
        out_specs=[smem()] * 2,
        compiler_params=params(),
    )(stats)


def slot_table(table_rows, pages_held, slot_ids):
    request_count, page_count = table_rows.shape
    matches = table_rows[:, :, None] == slot_ids[None, None, :]
    live = jnp.arange(page_count, dtype=jnp.int32)[None, :, None] < pages_held[:, None, None]
    hits = jnp.any(matches & live, axis=1)
    used = jnp.any(hits, axis=0).astype(jnp.int32)
    owner = jnp.sum(
        jnp.where(hits, jnp.arange(request_count, dtype=jnp.int32)[:, None], 0), axis=0
    )
    return used, owner


def kv_target(p):
    head = p % 16
    return (head // 4) * NZ + head % 4 + (4 if p >= 16 else 0)


def per_device(
    tokens,
    variate_ids,
    cache_pages,
    page_table,
    kv_cache,
    cache_variates,
    attn_gain,
    w_query,
    w_keyval,
    w_out,
    variate_bias,
    head_gain,
    w_head,
):
    r = lax.axis_index("req")
    y = lax.axis_index("y")
    z = lax.axis_index("z")
    idx = jnp.stack([r, y, z]).astype(jnp.int32)

    kv_cols = lax.ppermute(w_keyval.T, ("y", "z"), [(p, kv_target(p)) for p in range(NY * NZ)])
    w_local = jnp.concatenate([w_query.T, kv_cols, w_out.T, w_head.T], axis=0)
    w_z = lax.all_to_all(
        jnp.broadcast_to(w_local[None], (NZ, 136, 128)), "z", 0, 0, tiled=True
    )
    w_all = lax.all_to_all(
        jnp.broadcast_to(w_z[None, :, 0:96, :], (NR, NZ, 96, 128)), "req", 0, 0, tiled=True
    )
    late = lax.all_gather(w_z[:, 96:136, :], ("req", "y"), axis=0).reshape(NR, NY * NZ, 40, 128)

    tok = lax.all_gather(rms_norm(tokens, attn_gain), "y", axis=0, tiled=True)

    kv_rows = kv_cache.reshape(SLOTS * PAGE, 2048)
    pieces = carve(idx, kv_rows, cache_variates)
    pieces = [shift("y", NY, d)(pieces[d - 1]) for d in range(1, NY)]
    columns = jnp.transpose(variate_ids.reshape(NY, NZ, ROWS), (1, 0, 2)).reshape(NZ, 1, 256)
    fresh_vars = lax.dynamic_index_in_dim(columns, z, 0, keepdims=False).reshape(2, 128)
    order = (y + NY - jnp.arange(NY, dtype=jnp.int32)) % NY
    slot_ids = (
        (order[:, None] * NZ + z) * SLOTS + jnp.arange(SLOTS, dtype=jnp.int32)[None, :]
    ).reshape(-1)
    used, owner = slot_table(page_table, cache_pages, slot_ids)

    lane = jnp.arange(256, dtype=jnp.int32)
    source = lane // ROWS
    positions = (
        jnp.where(source // 2 == 0, cache_pages[0], cache_pages[1]) * PAGE
        + ((source % 2) * NZ + z) * ROWS
        + lane % ROWS
    )
    steps = jnp.arange(32, dtype=F32) / 32
    freqs = jnp.exp(-math.log(10000.0) * steps)
    angle = positions.astype(F32)[None, :] * freqs[:, None]

    q_copies, app = project(tok, w_all, jnp.cos(angle), jnp.sin(angle))
    app_all = lax.all_gather(app, "y", axis=0)
    q = lax.all_to_all(q_copies, "z", 0, 0, tiled=True)
    sent = attend(
        idx, used, owner, variate_bias, q, kv_rows, pieces, app, cache_variates, fresh_vars, columns
    )
    parts = lax.all_to_all(sent, ("y", "z"), 0, 0, tiled=True)
    hidden, logits, stats, appended = finish(
        idx, parts, tokens, late, app_all, head_gain.reshape(1, -1)
    )
    norm, peak = gather_stats(lax.all_to_all(stats, ("y", "z"), 0, 0, tiled=True))
    return hidden, appended, logits, norm, peak


def solution(mesh):
    grid = Mesh(mesh.devices.reshape(NR, NY, NZ), ("req", "y", "z"))
    every = ("req", "y", "z")
    pg = ("y", "z")
    placed = (
        P(every, None),
        P("req"),
        P("req"),
        P("req", None),
        P(every, None, None),
        P(every, None),
        P(),
        P("req", pg),
        P("req", pg),
        P("req", pg),
        P(),
        P(),
        P("req", pg),
    )
    return jax.shard_map(
        per_device,
        mesh=grid,
        in_specs=placed,
        out_specs=(P(every, None), P(every, None), P(every, None), P("req"), P("req")),
        check_vma=False,
    )
```

```python
import math

import jax
import jax.numpy as jnp
from jax import lax
from jax.experimental import pallas as pl
from jax.experimental.pallas import tpu as pltpu
from jax.sharding import Mesh
from jax.sharding import PartitionSpec as P

PAGE = 128
EPSILON = 1e-05
NEGATIVE = -1e30
NY = 4
NZ = 8
NR = 8
SLOTS = 6
ROWS = 64
HEADS = 4
DH = 64
F32 = jnp.float32
BF16 = jnp.bfloat16


def shift(axis, size, step):
    return lambda value: lax.ppermute(
        value, axis, [(i, (i + step) % size) for i in range(size)]
    )


def rms_norm(values, gain):
    wide = values.astype(F32)
    power = jnp.mean(wide * wide, axis=-1, keepdims=True)
    return (wide * lax.rsqrt(power + EPSILON) * gain).astype(BF16)


def vmem():
    return pl.BlockSpec(memory_space=pltpu.VMEM)


def smem():
    return pl.BlockSpec(memory_space=pltpu.SMEM)


def hbm():
    return pl.BlockSpec(memory_space=pltpu.HBM)


def params(mib):
    return pltpu.CompilerParams(vmem_limit_bytes=mib * 1024 * 1024)


def dot_last(a, b):
    return lax.dot_general(a, b, (((1,), (1,)), ((), ())), preferred_element_type=F32)


def carve_kernel(idx, kv, variates, *refs):
    outs = refs[0:3]
    side, sem = refs[3:5]
    y = idx[1]
    rows = SLOTS * PAGE
    side[...] = jnp.zeros(side.shape, BF16)
    side[0:8, 0:128] = jnp.concatenate(
        [variates[...].astype(F32), jnp.zeros((2, 128), F32)], axis=0
    ).astype(BF16)
    copies = []
    for d in range(1, NY):
        yd = lax.rem(y + d, NY)
        for half in range(2):
            low = pl.multiple_of(half * 1024 + yd * 256, 256)
            copies.append(
                pltpu.make_async_copy(
                    kv.at[:, pl.ds(low, 256)],
                    outs[d - 1].at[pl.ds(0, rows), pl.ds(half * 256, 256)],
                    sem.at[2 * d - 2 + half],
                )
            )
    for c in copies:
        c.start()
    for d in range(1, NY):
        outs[d - 1][rows : rows + 16, :] = side[...]
    for c in copies:
        c.wait()


def carve(idx, kv, variates):
    return pl.pallas_call(
        carve_kernel,
        out_shape=[jax.ShapeDtypeStruct((SLOTS * PAGE + 16, 512), BF16)] * 3,
        in_specs=[smem(), hbm(), vmem()],
        out_specs=[vmem()] * 3,
        scratch_shapes=[pltpu.VMEM((16, 512), BF16), pltpu.SemaphoreType.DMA((6,))],
        compiler_params=params(56),
    )(idx, kv, variates)


def qkv_kernel(tok_hbm, w_hbm, cos_ref, sin_ref, q_out, app_out, tok, w, acc, feats, sem):
    copies = [pltpu.make_async_copy(tok_hbm, tok, sem.at[NR])] + [
        pltpu.make_async_copy(w_hbm.at[r], w.at[r], sem.at[r]) for r in range(NR)
    ]
    for c in copies:
        c.start()
    copies[0].wait()
    for r in range(NR):
        copies[1 + r].wait()
        part = dot_last(w[r], tok[:, r * 128 : (r + 1) * 128])
        if r == 0:
            acc[...] = part
        else:
            acc[...] += part
    cos = cos_ref[...]
    sin = sin_ref[...]

    def rounded(zs, low, high):
        return acc[zs * 96 + low : zs * 96 + high, :].astype(BF16).astype(F32)

    for h in range(HEADS):
        a = rounded(2 * h, 0, 32)
        b = rounded(2 * h + 1, 0, 32)
        first = ((a * cos - b * sin).astype(BF16).astype(F32) * 0.125).astype(BF16)
        second = ((b * cos + a * sin).astype(BF16).astype(F32) * 0.125).astype(BF16)
        for zs in range(NZ):
            q_out[zs, h * 64 : h * 64 + 32, :] = first
            q_out[zs, h * 64 + 32 : h * 64 + 64, :] = second
        a = rounded(h, 32, 64)
        b = rounded(h, 64, 96)
        feats[h * 64 : h * 64 + 32, :] = a * cos - b * sin
        feats[h * 64 + 32 : h * 64 + 64, :] = b * cos + a * sin
        feats[256 + h * 64 : 256 + h * 64 + 64, :] = acc[(HEADS + h) * 96 + 32 : (HEADS + h) * 96 + 96, :]
    app_out[:, 0:256] = feats[0:256, :].T.astype(BF16)
    app_out[:, 256:512] = feats[256:512, :].T.astype(BF16)


def project(tok, w, cos, sin):
    return pl.pallas_call(
        qkv_kernel,
        out_shape=[
            jax.ShapeDtypeStruct((NZ, 256, 256), BF16),
            jax.ShapeDtypeStruct((256, 512), BF16),
        ],
        in_specs=[hbm()] * 2 + [vmem()] * 2,
        out_specs=[vmem()] * 2,
        scratch_shapes=[
            pltpu.VMEM((256, 1024), BF16),
            pltpu.VMEM((NR, NZ * 96, 128), BF16),
            pltpu.VMEM((NZ * 96, 256), F32),
            pltpu.VMEM((512, 256), F32),
            pltpu.SemaphoreType.DMA((NR + 1,)),
        ],
        compiler_params=params(56),
    )(tok, w, cos, sin)


def attn_kernel(idx, used, owner, bias, *refs):
    q, kv, p1, p2, p3, app, own_vars, fresh_vars, qvar = refs[0:9]
    out = refs[9]
    pg, qb, top, acc, side, kvs, causal, sem = refs[10:18]
    y, z = idx[1], idx[2]
    rows = SLOTS * PAGE
    copies = []
    for half in range(2):
        low = pl.multiple_of(half * 1024 + y * 256, 256)
        copies.append(
            pltpu.make_async_copy(
                kv.at[:, pl.ds(low, 256)],
                pg.at[pl.ds(0, rows), pl.ds(half * 256, 256)],
                sem.at[half],
            )
        )
    for d, piece in enumerate((p1, p2, p3)):
        copies.append(
            pltpu.make_async_copy(
                piece.at[pl.ds(0, rows)], pg.at[pl.ds((d + 1) * rows, rows)], sem.at[2 + d]
            )
        )
        copies.append(
            pltpu.make_async_copy(
                piece.at[pl.ds(rows, 16), pl.ds(0, 128)], side.at[d], sem.at[5 + d]
            )
        )
    copies.append(pltpu.make_async_copy(app, pg.at[pl.ds(NY * rows, 256)], sem.at[8]))
    for c in copies:
        c.start()

    row16 = lax.broadcasted_iota(jnp.int32, (16, 128), 0)
    vsel = row16 & 3
    level = row16 >> 2
    zero = jnp.zeros((48, 128), BF16)

    def fill(zs, carry):
        lanes = pl.ds(pl.multiple_of(zs * 128, 128), 128)
        qv_row = qvar[zs]
        for j in range(2):
            same = jnp.broadcast_to(qv_row[:, j * 128 : (j + 1) * 128], (16, 128)) == vsel
            for h in range(HEADS):
                hh = y * HEADS + h
                b = jnp.where(same, bias[0, hh], bias[1, hh])
                hi = b.astype(BF16).astype(F32)
                mid = (b - hi).astype(BF16).astype(F32)
                lo = (b - hi - mid).astype(BF16).astype(F32)
                extra = jnp.where(
                    level == 0, hi, jnp.where(level == 1, mid, jnp.where(level == 2, lo, 0.0))
                ).astype(BF16)
                q_rows = q[zs, h * 64 : (h + 1) * 64, j * 128 : (j + 1) * 128]
                if h % 2 == 0:
                    qb[j, h, 0:64, lanes] = q_rows
                    qb[j, h, 64:80, lanes] = extra
                    qb[j, h, 80:128, lanes] = zero
                else:
                    qb[j, h, 0:16, lanes] = extra
                    qb[j, h, 16:64, lanes] = zero
                    qb[j, h, 64:128, lanes] = q_rows
        key_row = lax.broadcasted_iota(jnp.int32, (128, 128), 0)
        q_lane = lax.broadcasted_iota(jnp.int32, (128, 128), 1)
        key_pos = ((key_row >> 6) * NZ + z) * ROWS + (key_row & 63)
        q_pos = ((q_lane >> 6) * NZ + zs) * ROWS + (q_lane & 63)
        causal[:, lanes] = jnp.where(key_pos <= q_pos, 0.0, NEGATIVE)
        return carry

    lax.fori_loop(0, NZ, fill, 0)
    top[...] = jnp.full(top.shape, NEGATIVE, F32)
    acc[...] = jnp.zeros(acc.shape, F32)
    for s in range(SLOTS):
        kvs[s] = own_vars[s : s + 1, :].astype(F32)
    for j in range(2):
        kvs[NY * SLOTS + j] = fresh_vars[j : j + 1, :].astype(F32)
    for c in copies:
        c.wait()
    for d in range(3):
        block = side[d].astype(F32)
        for s in range(SLOTS):
            kvs[(d + 1) * SLOTS + s] = block[s : s + 1, :]

    sub = lax.broadcasted_iota(jnp.int32, (128, 128), 0)
    variate = (sub & 3).astype(F32)
    hot_rows = (sub & 63) < 12
    low_lanes = lax.broadcasted_iota(jnp.int32, (128, 128), 1) < 64
    ones = jnp.ones((16, 128), BF16)

    def visit(slot, j, fresh):
        page = pg[pl.ds(pl.multiple_of(slot * PAGE, PAGE), PAGE), :]
        kvals = jnp.broadcast_to(kvs[slot], (128, 128))
        hot = jnp.where(hot_rows & (variate == kvals), 1.0, 0.0).T
        keys = page[:, 0:256].astype(F32)
        vals = page[:, 256:512].astype(F32).T.astype(BF16)
        kaug = []
        vaug = []
        for h in range(HEADS):
            pair = keys[:, (h // 2) * 128 : (h // 2) * 128 + 128]
            both = (pair, hot) if h % 2 == 0 else (hot, pair)
            kaug.append(jnp.where(low_lanes, both[0], both[1]).astype(BF16))
            vaug.append(jnp.concatenate([vals[h * 64 : (h + 1) * 64, :], ones], axis=0))
        olds = [top[j, h] for h in range(HEADS)]
        scores = {}
        weights = {}
        for i in range(HEADS + 2):
            if i < HEADS:
                s = jnp.dot(kaug[i], qb[j, i], preferred_element_type=F32)
                scores[i] = s + causal[...] if fresh else s
            if 1 <= i <= HEADS:
                k = i - 1
                s = scores.pop(k)
                new = jnp.maximum(olds[k], jnp.max(s, axis=0, keepdims=True))
                weights[k] = (jnp.exp(s - new).astype(BF16), new, jnp.exp(olds[k] - new))
            if i >= 2:
                k = i - 2
                p, new, keep = weights.pop(k)
                top[j, k] = new
                acc[j, k] = acc[j, k] * keep + jnp.dot(vaug[k], p, preferred_element_type=F32)

    def body(slot, carry):
        @pl.when(used[slot] > 0)
        def _():
            visit(slot, owner[slot], False)

        return carry

    lax.fori_loop(0, NY * SLOTS, body, 0)

    def last(j, carry):
        visit(NY * SLOTS + j, j, True)
        return carry

    lax.fori_loop(0, 2, last, 0)

    low64 = lax.broadcasted_iota(jnp.int32, (64, 128), 1) < 64
    low8 = lax.broadcasted_iota(jnp.int32, (8, 128), 1) < 64

    def send(zs, carry):
        lanes = pl.ds(pl.multiple_of(zs * 128, 128), 128)
        for j in range(2):
            values = []
            parts = []
            for h in range(HEADS):
                total = acc[j, h, 64:65, lanes]
                values.append(acc[j, h, 0:64, lanes] * (1.0 / total))
                lse = top[j, h, :, lanes] + jnp.log(total)
                hi = lse.astype(BF16).astype(F32)
                mid = (lse - hi).astype(BF16).astype(F32)
                parts.append(jnp.concatenate([hi, mid, lse - hi - mid], axis=0))
            blank = jnp.zeros((2, 128), F32)
            stat_a = jnp.concatenate([parts[0], parts[1], blank], axis=0)
            stat_b = jnp.concatenate([parts[2], parts[3], blank], axis=0)
            for side_row in range(2):
                p = (2 * j + side_row) * NZ + zs

                def pick(left, right, mask):
                    if side_row == 0:
                        return jnp.where(mask, left, pltpu.roll(right, 64, 1)).astype(BF16)
                    return jnp.where(mask, pltpu.roll(left, 64, 1), right).astype(BF16)

                out[p, 0:64, :] = pick(values[0], values[2], low64)
                out[p, 64:128, :] = pick(values[1], values[3], low64)
                out[p, 128:136, :] = pick(stat_a, stat_b, low8)
        return carry

    lax.fori_loop(0, NZ, send, 0)


def attend(idx, used, owner, bias, q, kv, pieces, app, own_vars, fresh_vars, qvar):
    return pl.pallas_call(
        attn_kernel,
        out_shape=jax.ShapeDtypeStruct((NY * NZ, 136, 128), BF16),
        in_specs=[smem()] * 4 + [vmem()] + [hbm()] * 5 + [vmem()] * 3,
        out_specs=vmem(),
        scratch_shapes=[
            pltpu.VMEM((26 * PAGE, 512), BF16),
            pltpu.VMEM((2, HEADS, 128, 1024), BF16),
            pltpu.VMEM((2, HEADS, 1, 1024), F32),
            pltpu.VMEM((2, HEADS, 80, 1024), F32),
            pltpu.VMEM((3, 16, 128), BF16),
            pltpu.VMEM((26, 1, 128), F32),
            pltpu.VMEM((128, 1024), F32),
            pltpu.SemaphoreType.DMA((9,)),
        ],
        compiler_params=params(56),
    )(idx, used, owner, bias, q, kv, *pieces, app, own_vars, fresh_vars, qvar)


def final_kernel(parts, tokens, late, app_all, gain, hidden_out, logits_out, stats_out, app_out, wo, wh, head_in, sem):
    copies = [
        pltpu.make_async_copy(late.at[:, :, pl.ds(0, 32), :], wo, sem.at[0]),
        pltpu.make_async_copy(late.at[:, :, pl.ds(32, 8), :], wh, sem.at[1]),
    ]
    for ys in range(NY):
        for half in range(2):
            copies.append(
                pltpu.make_async_copy(
                    app_all.at[ys, :, pl.ds(half * 256, 256)],
                    app_out.at[:, pl.ds(half * 1024 + ys * 256, 256)],
                    sem.at[2 + 2 * ys + half],
                )
            )
    for c in copies:
        c.start()
    chunks = []
    for ys in range(NY):
        lses = [[], []]
        for zs in range(NZ):
            stat = parts[ys * NZ + zs, 128:136, :].astype(F32)
            for k in range(2):
                lses[k].append(stat[3 * k : 3 * k + 1] + stat[3 * k + 1 : 3 * k + 2] + stat[3 * k + 2 : 3 * k + 3])
        merged = []
        for k in range(2):
            best = lses[k][0]
            for v in lses[k][1:]:
                best = jnp.maximum(best, v)
            ws = [jnp.exp(v - best) for v in lses[k]]
            total = ws[0]
            for w in ws[1:]:
                total = total + w
            inverse = 1.0 / total
            value = None
            for zs in range(NZ):
                term = parts[ys * NZ + zs, k * 64 : (k + 1) * 64, :].astype(F32) * (ws[zs] * inverse)
                value = term if value is None else value + term
            merged.append(value)
        turned = jnp.concatenate(merged, axis=0).T.astype(BF16)
        chunks.append(turned[0:64, :])
        chunks.append(turned[64:128, :])
    for c in copies:
        c.wait()
    total = tokens[...].astype(F32)
    for r in range(NR):
        total = total + dot_last(chunks[r], wo[r].reshape(1024, 128))
    hidden = total.astype(BF16)
    hidden_out[...] = hidden
    wide = hidden.astype(F32)
    square = wide * wide
    power = jnp.sum(square, axis=1, keepdims=True)
    head_in[...] = (wide * lax.rsqrt(power * (1.0 / 1024) + EPSILON) * gain[...]).astype(BF16)
    logits = None
    for r in range(NR):
        part = dot_last(head_in[:, r * 128 : (r + 1) * 128], wh[r].reshape(256, 128))
        logits = part if logits is None else logits + part
    logits_out[...] = logits.astype(BF16)
    energy = jnp.sum(power, axis=0, keepdims=True)
    peak = jnp.max(jnp.max(logits, axis=1, keepdims=True), axis=0, keepdims=True)
    row = lax.broadcasted_iota(jnp.int32, (8, 128), 0)
    tile = jnp.where(row == 0, energy, jnp.where(row == 1, peak, 0.0))
    for p in range(NY * NZ):
        stats_out[p * 8 : (p + 1) * 8, :] = tile


def finish(parts, tokens, late, app_all, gain):
    return pl.pallas_call(
        final_kernel,
        out_shape=[
            jax.ShapeDtypeStruct((ROWS, 1024), BF16),
            jax.ShapeDtypeStruct((ROWS, 256), BF16),
            jax.ShapeDtypeStruct((NY * NZ * 8, 128), F32),
            jax.ShapeDtypeStruct((ROWS, 2048), BF16),
        ],
        in_specs=[vmem(), vmem(), hbm(), hbm(), vmem()],
        out_specs=[vmem()] * 4,
        scratch_shapes=[
            pltpu.VMEM((NR, NY * NZ, 32, 128), BF16),
            pltpu.VMEM((NR, NY * NZ, 8, 128), BF16),
            pltpu.VMEM((ROWS, 1024), BF16),
            pltpu.SemaphoreType.DMA((10,)),
        ],
        compiler_params=params(56),
    )(parts, tokens, late, app_all, gain)


def stats_kernel(stats, norm_out, peak_out):
    half = NY * NZ * 4
    for j in range(2):
        block = stats[j * half : (j + 1) * half, :].reshape(NY * NZ // 2, 8, 128)
        norm_out[j] = jnp.sqrt(jnp.sum(block, axis=0))[0, 0]
        peak_out[j] = jnp.max(block, axis=0)[1, 0]


def gather_stats(stats):
    return pl.pallas_call(
        stats_kernel,
        out_shape=[jax.ShapeDtypeStruct((2,), F32)] * 2,
        in_specs=[vmem()],
        out_specs=[smem()] * 2,
        compiler_params=params(4),
    )(stats)


def slot_table(table_rows, pages_held, slot_ids):
    request_count, page_count = table_rows.shape
    matches = table_rows[:, :, None] == slot_ids[None, None, :]
    live = jnp.arange(page_count, dtype=jnp.int32)[None, :, None] < pages_held[:, None, None]
    hits = jnp.any(matches & live, axis=1)
    used = jnp.any(hits, axis=0).astype(jnp.int32)
    owner = jnp.sum(
        jnp.where(hits, jnp.arange(request_count, dtype=jnp.int32)[:, None], 0), axis=0
    )
    return used, owner


def kv_target(p):
    head = p % 16
    return (head // 4) * NZ + head % 4 + (4 if p >= 16 else 0)


def per_device(
    tokens,
    variate_ids,
    cache_pages,
    page_table,
    kv_cache,
    cache_variates,
    attn_gain,
    w_query,
    w_keyval,
    w_out,
    variate_bias,
    head_gain,
    w_head,
):
    r = lax.axis_index("req")
    y = lax.axis_index("y")
    z = lax.axis_index("z")
    idx = jnp.stack([r, y, z]).astype(jnp.int32)

    kv_rows = kv_cache.reshape(SLOTS * PAGE, 2048)
    carved = carve(idx, kv_rows, cache_variates)
    pieces = [shift("y", NY, d)(carved[d - 1]) for d in range(1, NY)]

    kv_cols = lax.ppermute(w_keyval.T, ("y", "z"), [(p, kv_target(p)) for p in range(NY * NZ)])
    w_local = jnp.concatenate([w_query.T, kv_cols, w_out.T, w_head.T], axis=0)
    w_local, _ = lax.optimization_barrier((w_local, carved))
    w_z = lax.all_to_all(
        jnp.broadcast_to(w_local[None], (NZ, 136, 128)), "z", 0, 0, tiled=True
    )
    w_z, pieces[0], pieces[2] = lax.optimization_barrier((w_z, pieces[0], pieces[2]))
    w_all = lax.all_to_all(
        jnp.broadcast_to(w_z[None, :, 0:96, :], (NR, NZ, 96, 128)), "req", 0, 0, tiled=True
    )
    late = lax.all_gather(w_z[:, 96:136, :], ("req", "y"), axis=0).reshape(NR, NY * NZ, 40, 128)

    tok = lax.all_gather(rms_norm(tokens, attn_gain), "y", axis=0, tiled=True)
    tok, pieces[1] = lax.optimization_barrier((tok, pieces[1]))

    columns = jnp.transpose(variate_ids.reshape(NY, NZ, ROWS), (1, 0, 2)).reshape(NZ, 1, 256)
    fresh_vars = lax.dynamic_index_in_dim(columns, z, 0, keepdims=False).reshape(2, 128)
    order = (y + NY - jnp.arange(NY, dtype=jnp.int32)) % NY
    slot_ids = (
        (order[:, None] * NZ + z) * SLOTS + jnp.arange(SLOTS, dtype=jnp.int32)[None, :]
    ).reshape(-1)
    used, owner = slot_table(page_table, cache_pages, slot_ids)

    lane = jnp.arange(256, dtype=jnp.int32)
    source = lane // ROWS
    positions = (
        jnp.where(source // 2 == 0, cache_pages[0], cache_pages[1]) * PAGE
        + ((source % 2) * NZ + z) * ROWS
        + lane % ROWS
    )
    steps = jnp.arange(32, dtype=F32) / 32
    freqs = jnp.exp(-math.log(10000.0) * steps)
    angle = positions.astype(F32)[None, :] * freqs[:, None]

    q_copies, app = project(tok, w_all.reshape(NR, NZ * 96, 128), jnp.cos(angle), jnp.sin(angle))
    app_all = lax.all_to_all(app.reshape(NY, ROWS, 512), "y", 0, 0, tiled=True)
    q = lax.all_to_all(q_copies, "z", 0, 0, tiled=True)
    sent = attend(
        idx, used, owner, variate_bias, q, kv_rows, pieces, app, cache_variates, fresh_vars, columns
    )
    parts = lax.all_to_all(sent, ("y", "z"), 0, 0, tiled=True)
    hidden, logits, stats, appended = finish(
        parts, tokens, late, app_all, head_gain.reshape(1, -1)
    )
    norm, peak = gather_stats(lax.all_to_all(stats, ("y", "z"), 0, 0, tiled=True))
    return hidden, appended, logits, norm, peak


def solution(mesh):
    grid = Mesh(mesh.devices.reshape(NR, NY, NZ), ("req", "y", "z"))
    every = ("req", "y", "z")
    pg = ("y", "z")
    placed = (
        P(every, None),
        P("req"),
        P("req"),
        P("req", None),
        P(every, None, None),
        P(every, None),
        P(),
        P("req", pg),
        P("req", pg),
        P("req", pg),
        P(),
        P(),
        P("req", pg),
    )
    return jax.shard_map(
        per_device,
        mesh=grid,
        in_specs=placed,
        out_specs=(P(every, None), P(every, None), P(every, None), P("req"), P("req")),
        check_vma=False,
    )
```

```python
import math

import jax
import jax.numpy as jnp
from jax import lax
from jax.experimental import pallas as pl
from jax.experimental.pallas import tpu as pltpu
from jax.sharding import Mesh
from jax.sharding import PartitionSpec as P

PAGE = 128
EPSILON = 1e-05
NEGATIVE = -1e30
NY = 4
NZ = 8
NR = 8
SLOTS = 6
ROWS = 64
HEADS = 4
PIECE = SLOTS * 128 + 16 + 2 * ROWS
DH = 64
F32 = jnp.float32
BF16 = jnp.bfloat16


def shift(axis, size, step):
    return lambda value: lax.ppermute(
        value, axis, [(i, (i + step) % size) for i in range(size)]
    )


def vmem():
    return pl.BlockSpec(memory_space=pltpu.VMEM)


def smem():
    return pl.BlockSpec(memory_space=pltpu.SMEM)


def hbm():
    return pl.BlockSpec(memory_space=pltpu.HBM)


def params(mib):
    return pltpu.CompilerParams(vmem_limit_bytes=mib * 1024 * 1024)


def dot_last(a, b):
    return lax.dot_general(a, b, (((1,), (1,)), ((), ())), preferred_element_type=F32)


def carve_kernel(idx, kv, variates, tokens, gain, *refs):
    outs = refs[0:3]
    own = refs[3]
    side, sem = refs[4:6]
    y = idx[1]
    rows = SLOTS * PAGE
    side[...] = jnp.zeros(side.shape, BF16)
    side[0:8, 0:128] = jnp.concatenate(
        [variates[...].astype(F32), jnp.zeros((2, 128), F32)], axis=0
    ).astype(BF16)
    copies = []
    for d in range(1, NY):
        yd = lax.rem(y + d, NY)
        for half in range(2):
            low = pl.multiple_of(half * 1024 + yd * 256, 256)
            copies.append(
                pltpu.make_async_copy(
                    kv.at[:, pl.ds(low, 256)],
                    outs[d - 1].at[pl.ds(0, rows), pl.ds(half * 256, 256)],
                    sem.at[2 * d - 2 + half],
                )
            )
    for c in copies:
        c.start()
    wide = tokens[...].astype(F32)
    power = jnp.sum(wide * wide, axis=1, keepdims=True) * (1.0 / 1024)
    normed = (wide * lax.rsqrt(power + EPSILON) * gain[...]).astype(BF16)
    own[...] = normed
    for d in range(1, NY):
        outs[d - 1][rows : rows + 16, :] = side[...]
        outs[d - 1][rows + 16 : rows + 80, :] = normed[:, 0:512]
        outs[d - 1][rows + 80 : rows + 144, :] = normed[:, 512:1024]
    for c in copies:
        c.wait()


def carve(idx, kv, variates, tokens, gain):
    return pl.pallas_call(
        carve_kernel,
        out_shape=[jax.ShapeDtypeStruct((PIECE, 512), BF16)] * 3
        + [jax.ShapeDtypeStruct((ROWS, 1024), BF16)],
        in_specs=[smem(), hbm()] + [vmem()] * 3,
        out_specs=[vmem()] * 4,
        scratch_shapes=[pltpu.VMEM((16, 512), BF16), pltpu.SemaphoreType.DMA((6,))],
        compiler_params=params(56),
    )(idx, kv, variates, tokens, gain)


def qkv_kernel(idx, own, p1, p2, p3, w_hbm, cos_ref, sin_ref, q_out, app_out, tok, w, acc, feats, sem):
    y = idx[1]
    base = SLOTS * PAGE + 16
    copies = [
        pltpu.make_async_copy(
            own, tok.at[pl.ds(pl.multiple_of(y * ROWS, ROWS), ROWS), :], sem.at[NR]
        )
    ]
    for d, piece in enumerate((p1, p2, p3)):
        ys = lax.rem(y + NY - d - 1, NY)
        for half in range(2):
            copies.append(
                pltpu.make_async_copy(
                    piece.at[pl.ds(base + half * ROWS, ROWS)],
                    tok.at[
                        pl.ds(pl.multiple_of(ys * ROWS, ROWS), ROWS), pl.ds(half * 512, 512)
                    ],
                    sem.at[NR + 1 + 2 * d + half],
                )
            )
    blocks = [pltpu.make_async_copy(w_hbm.at[r], w.at[r], sem.at[r]) for r in range(NR)]
    for c in copies + blocks:
        c.start()
    for c in copies:
        c.wait()
    for r in range(NR):
        blocks[r].wait()
        part = dot_last(w[r], tok[:, r * 128 : (r + 1) * 128])
        if r == 0:
            acc[...] = part
        else:
            acc[...] += part
    cos = cos_ref[...]
    sin = sin_ref[...]

    def rounded(zs, low, high):
        return acc[zs * 96 + low : zs * 96 + high, :].astype(BF16).astype(F32)

    for h in range(HEADS):
        a = rounded(2 * h, 0, 32)
        b = rounded(2 * h + 1, 0, 32)
        first = ((a * cos - b * sin).astype(BF16).astype(F32) * 0.125).astype(BF16)
        second = ((b * cos + a * sin).astype(BF16).astype(F32) * 0.125).astype(BF16)
        for zs in range(NZ):
            q_out[zs, h * 64 : h * 64 + 32, :] = first
            q_out[zs, h * 64 + 32 : h * 64 + 64, :] = second
        a = rounded(h, 32, 64)
        b = rounded(h, 64, 96)
        feats[h * 64 : h * 64 + 32, :] = a * cos - b * sin
        feats[h * 64 + 32 : h * 64 + 64, :] = b * cos + a * sin
        feats[256 + h * 64 : 256 + h * 64 + 64, :] = acc[(HEADS + h) * 96 + 32 : (HEADS + h) * 96 + 96, :]
    app_out[:, 0:256] = feats[0:256, :].T.astype(BF16)
    app_out[:, 256:512] = feats[256:512, :].T.astype(BF16)


def project(idx, own, pieces, w, cos, sin):
    return pl.pallas_call(
        qkv_kernel,
        out_shape=[
            jax.ShapeDtypeStruct((NZ, 256, 256), BF16),
            jax.ShapeDtypeStruct((256, 512), BF16),
        ],
        in_specs=[smem()] + [hbm()] * 5 + [vmem()] * 2,
        out_specs=[vmem()] * 2,
        scratch_shapes=[
            pltpu.VMEM((256, 1024), BF16),
            pltpu.VMEM((NR, NZ * 96, 128), BF16),
            pltpu.VMEM((NZ * 96, 256), F32),
            pltpu.VMEM((512, 256), F32),
            pltpu.SemaphoreType.DMA((NR + 7,)),
        ],
        compiler_params=params(56),
    )(idx, own, *pieces, w, cos, sin)


def attn_kernel(idx, used, owner, bias, *refs):
    q, kv, p1, p2, p3, app, own_vars, fresh_vars, qvar = refs[0:9]
    out = refs[9]
    pg, qb, top, acc, side, kvs, causal, sem = refs[10:18]
    y, z = idx[1], idx[2]
    rows = SLOTS * PAGE
    copies = []
    for half in range(2):
        low = pl.multiple_of(half * 1024 + y * 256, 256)
        copies.append(
            pltpu.make_async_copy(
                kv.at[:, pl.ds(low, 256)],
                pg.at[pl.ds(0, rows), pl.ds(half * 256, 256)],
                sem.at[half],
            )
        )
    for d, piece in enumerate((p1, p2, p3)):
        copies.append(
            pltpu.make_async_copy(
                piece.at[pl.ds(0, rows)], pg.at[pl.ds((d + 1) * rows, rows)], sem.at[2 + d]
            )
        )
        copies.append(
            pltpu.make_async_copy(
                piece.at[pl.ds(rows, 16), pl.ds(0, 128)], side.at[d], sem.at[5 + d]
            )
        )
    copies.append(pltpu.make_async_copy(app, pg.at[pl.ds(NY * rows, 256)], sem.at[8]))
    for c in copies:
        c.start()

    row16 = lax.broadcasted_iota(jnp.int32, (16, 128), 0)
    vsel = row16 & 3
    level = row16 >> 2
    zero = jnp.zeros((48, 128), BF16)

    def fill(zs, carry):
        lanes = pl.ds(pl.multiple_of(zs * 128, 128), 128)
        qv_row = qvar[zs]
        for j in range(2):
            same = jnp.broadcast_to(qv_row[:, j * 128 : (j + 1) * 128], (16, 128)) == vsel
            for h in range(HEADS):
                hh = y * HEADS + h
                b = jnp.where(same, bias[0, hh], bias[1, hh])
                hi = b.astype(BF16).astype(F32)
                mid = (b - hi).astype(BF16).astype(F32)
                lo = (b - hi - mid).astype(BF16).astype(F32)
                extra = jnp.where(
                    level == 0, hi, jnp.where(level == 1, mid, jnp.where(level == 2, lo, 0.0))
                ).astype(BF16)
                q_rows = q[zs, h * 64 : (h + 1) * 64, j * 128 : (j + 1) * 128]
                if h % 2 == 0:
                    qb[j, h, 0:64, lanes] = q_rows
                    qb[j, h, 64:80, lanes] = extra
                    qb[j, h, 80:128, lanes] = zero
                else:
                    qb[j, h, 0:16, lanes] = extra
                    qb[j, h, 16:64, lanes] = zero
                    qb[j, h, 64:128, lanes] = q_rows
        key_row = lax.broadcasted_iota(jnp.int32, (128, 128), 0)
        q_lane = lax.broadcasted_iota(jnp.int32, (128, 128), 1)
        key_pos = ((key_row >> 6) * NZ + z) * ROWS + (key_row & 63)
        q_pos = ((q_lane >> 6) * NZ + zs) * ROWS + (q_lane & 63)
        causal[:, lanes] = jnp.where(key_pos <= q_pos, 0.0, NEGATIVE)
        return carry

    lax.fori_loop(0, NZ, fill, 0)
    top[...] = jnp.full(top.shape, NEGATIVE, F32)
    acc[...] = jnp.zeros(acc.shape, F32)
    for s in range(SLOTS):
        kvs[s] = own_vars[s : s + 1, :].astype(F32)
    for j in range(2):
        kvs[NY * SLOTS + j] = fresh_vars[j : j + 1, :].astype(F32)
    for c in copies:
        c.wait()
    for d in range(3):
        block = side[d].astype(F32)
        for s in range(SLOTS):
            kvs[(d + 1) * SLOTS + s] = block[s : s + 1, :]

    sub = lax.broadcasted_iota(jnp.int32, (128, 128), 0)
    variate = (sub & 3).astype(F32)
    hot_rows = (sub & 63) < 12
    low_lanes = lax.broadcasted_iota(jnp.int32, (128, 128), 1) < 64
    ones = jnp.ones((16, 128), BF16)

    def visit(slot, j, fresh):
        page = pg[pl.ds(pl.multiple_of(slot * PAGE, PAGE), PAGE), :]
        kvals = jnp.broadcast_to(kvs[slot], (128, 128))
        hot = jnp.where(hot_rows & (variate == kvals), 1.0, 0.0).T
        keys = page[:, 0:256].astype(F32)
        vals = page[:, 256:512].astype(F32).T.astype(BF16)
        kaug = []
        vaug = []
        for h in range(HEADS):
            pair = keys[:, (h // 2) * 128 : (h // 2) * 128 + 128]
            both = (pair, hot) if h % 2 == 0 else (hot, pair)
            kaug.append(jnp.where(low_lanes, both[0], both[1]).astype(BF16))
            vaug.append(jnp.concatenate([vals[h * 64 : (h + 1) * 64, :], ones], axis=0))
        olds = [top[j, h] for h in range(HEADS)]
        scores = {}
        weights = {}
        for i in range(HEADS + 2):
            if i < HEADS:
                s = jnp.dot(kaug[i], qb[j, i], preferred_element_type=F32)
                scores[i] = s + causal[...] if fresh else s
            if 1 <= i <= HEADS:
                k = i - 1
                s = scores.pop(k)
                new = jnp.maximum(olds[k], jnp.max(s, axis=0, keepdims=True))
                weights[k] = (jnp.exp(s - new).astype(BF16), new, jnp.exp(olds[k] - new))
            if i >= 2:
                k = i - 2
                p, new, keep = weights.pop(k)
                top[j, k] = new
                acc[j, k] = acc[j, k] * keep + jnp.dot(vaug[k], p, preferred_element_type=F32)

    def body(slot, carry):
        @pl.when(used[slot] > 0)
        def _():
            visit(slot, owner[slot], False)

        return carry

    lax.fori_loop(0, NY * SLOTS, body, 0)

    def last(j, carry):
        visit(NY * SLOTS + j, j, True)
        return carry

    lax.fori_loop(0, 2, last, 0)

    low64 = lax.broadcasted_iota(jnp.int32, (64, 128), 1) < 64
    low8 = lax.broadcasted_iota(jnp.int32, (8, 128), 1) < 64

    def send(zs, carry):
        lanes = pl.ds(pl.multiple_of(zs * 128, 128), 128)
        for j in range(2):
            values = []
            parts = []
            for h in range(HEADS):
                total = acc[j, h, 64:65, lanes]
                values.append(acc[j, h, 0:64, lanes] * (1.0 / total))
                lse = top[j, h, :, lanes] + jnp.log(total)
                hi = lse.astype(BF16).astype(F32)
                mid = (lse - hi).astype(BF16).astype(F32)
                parts.append(jnp.concatenate([hi, mid, lse - hi - mid], axis=0))
            blank = jnp.zeros((2, 128), F32)
            stat_a = jnp.concatenate([parts[0], parts[1], blank], axis=0)
            stat_b = jnp.concatenate([parts[2], parts[3], blank], axis=0)
            for side_row in range(2):
                p = (2 * j + side_row) * NZ + zs

                def pick(left, right, mask):
                    if side_row == 0:
                        return jnp.where(mask, left, pltpu.roll(right, 64, 1)).astype(BF16)
                    return jnp.where(mask, pltpu.roll(left, 64, 1), right).astype(BF16)

                out[p, 0:64, :] = pick(values[0], values[2], low64)
                out[p, 64:128, :] = pick(values[1], values[3], low64)
                out[p, 128:136, :] = pick(stat_a, stat_b, low8)
        return carry

    lax.fori_loop(0, NZ, send, 0)


def attend(idx, used, owner, bias, q, kv, pieces, app, own_vars, fresh_vars, qvar):
    return pl.pallas_call(
        attn_kernel,
        out_shape=jax.ShapeDtypeStruct((NY * NZ, 136, 128), BF16),
        in_specs=[smem()] * 4 + [vmem()] + [hbm()] * 5 + [vmem()] * 3,
        out_specs=vmem(),
        scratch_shapes=[
            pltpu.VMEM((26 * PAGE, 512), BF16),
            pltpu.VMEM((2, HEADS, 128, 1024), BF16),
            pltpu.VMEM((2, HEADS, 1, 1024), F32),
            pltpu.VMEM((2, HEADS, 80, 1024), F32),
            pltpu.VMEM((3, 16, 128), BF16),
            pltpu.VMEM((26, 1, 128), F32),
            pltpu.VMEM((128, 1024), F32),
            pltpu.SemaphoreType.DMA((9,)),
        ],
        compiler_params=params(56),
    )(idx, used, owner, bias, q, kv, *pieces, app, own_vars, fresh_vars, qvar)


def final_kernel(idx, parts, tokens, late, app_all, gain, hidden_out, logits_out, stats_out, app_out, wo, wh, head_in, sem):
    copies = [
        pltpu.make_async_copy(late.at[:, :, pl.ds(0, 32), :], wo, sem.at[0]),
        pltpu.make_async_copy(late.at[:, :, pl.ds(32, 8), :], wh, sem.at[1]),
    ]
    own = pl.ds(pl.multiple_of(idx[1] * ROWS, ROWS), ROWS)
    for ys in range(NY):
        for half in range(2):
            copies.append(
                pltpu.make_async_copy(
                    app_all.at[ys, own, pl.ds(half * 256, 256)],
                    app_out.at[:, pl.ds(half * 1024 + ys * 256, 256)],
                    sem.at[2 + 2 * ys + half],
                )
            )
    for c in copies:
        c.start()
    chunks = []
    for ys in range(NY):
        lses = [[], []]
        for zs in range(NZ):
            stat = parts[ys * NZ + zs, 128:136, :].astype(F32)
            for k in range(2):
                lses[k].append(stat[3 * k : 3 * k + 1] + stat[3 * k + 1 : 3 * k + 2] + stat[3 * k + 2 : 3 * k + 3])
        merged = []
        for k in range(2):
            best = lses[k][0]
            for v in lses[k][1:]:
                best = jnp.maximum(best, v)
            ws = [jnp.exp(v - best) for v in lses[k]]
            total = ws[0]
            for w in ws[1:]:
                total = total + w
            inverse = 1.0 / total
            value = None
            for zs in range(NZ):
                term = parts[ys * NZ + zs, k * 64 : (k + 1) * 64, :].astype(F32) * (ws[zs] * inverse)
                value = term if value is None else value + term
            merged.append(value)
        turned = jnp.concatenate(merged, axis=0).T.astype(BF16)
        chunks.append(turned[0:64, :])
        chunks.append(turned[64:128, :])
    for c in copies:
        c.wait()
    total = tokens[...].astype(F32)
    for r in range(NR):
        total = total + dot_last(chunks[r], wo[r].reshape(1024, 128))
    hidden = total.astype(BF16)
    hidden_out[...] = hidden
    wide = hidden.astype(F32)
    square = wide * wide
    power = jnp.sum(square, axis=1, keepdims=True)
    head_in[...] = (wide * lax.rsqrt(power * (1.0 / 1024) + EPSILON) * gain[...]).astype(BF16)
    logits = None
    for r in range(NR):
        part = dot_last(head_in[:, r * 128 : (r + 1) * 128], wh[r].reshape(256, 128))
        logits = part if logits is None else logits + part
    logits_out[...] = logits.astype(BF16)
    energy = jnp.sum(power, axis=0, keepdims=True)
    peak = jnp.max(jnp.max(logits, axis=1, keepdims=True), axis=0, keepdims=True)
    row = lax.broadcasted_iota(jnp.int32, (8, 128), 0)
    tile = jnp.where(row == 0, energy, jnp.where(row == 1, peak, 0.0))
    for p in range(NY * NZ):
        stats_out[p * 8 : (p + 1) * 8, :] = tile


def finish(idx, parts, tokens, late, app_all, gain):
    return pl.pallas_call(
        final_kernel,
        out_shape=[
            jax.ShapeDtypeStruct((ROWS, 1024), BF16),
            jax.ShapeDtypeStruct((ROWS, 256), BF16),
            jax.ShapeDtypeStruct((NY * NZ * 8, 128), F32),
            jax.ShapeDtypeStruct((ROWS, 2048), BF16),
        ],
        in_specs=[smem(), vmem(), vmem(), hbm(), hbm(), vmem()],
        out_specs=[vmem()] * 4,
        scratch_shapes=[
            pltpu.VMEM((NR, NY * NZ, 32, 128), BF16),
            pltpu.VMEM((NR, NY * NZ, 8, 128), BF16),
            pltpu.VMEM((ROWS, 1024), BF16),
            pltpu.SemaphoreType.DMA((10,)),
        ],
        compiler_params=params(56),
    )(idx, parts, tokens, late, app_all, gain)


def stats_kernel(stats, norm_out, peak_out):
    half = NY * NZ * 4
    for j in range(2):
        block = stats[j * half : (j + 1) * half, :].reshape(NY * NZ // 2, 8, 128)
        norm_out[j] = jnp.sqrt(jnp.sum(block, axis=0))[0, 0]
        peak_out[j] = jnp.max(block, axis=0)[1, 0]


def gather_stats(stats):
    return pl.pallas_call(
        stats_kernel,
        out_shape=[jax.ShapeDtypeStruct((2,), F32)] * 2,
        in_specs=[vmem()],
        out_specs=[smem()] * 2,
        compiler_params=params(4),
    )(stats)


def slot_table(table_rows, pages_held, slot_ids):
    request_count, page_count = table_rows.shape
    matches = table_rows[:, :, None] == slot_ids[None, None, :]
    live = jnp.arange(page_count, dtype=jnp.int32)[None, :, None] < pages_held[:, None, None]
    hits = jnp.any(matches & live, axis=1)
    used = jnp.any(hits, axis=0).astype(jnp.int32)
    owner = jnp.sum(
        jnp.where(hits, jnp.arange(request_count, dtype=jnp.int32)[:, None], 0), axis=0
    )
    return used, owner


def kv_target(p):
    head = p % 16
    return (head // 4) * NZ + head % 4 + (4 if p >= 16 else 0)


def per_device(
    tokens,
    variate_ids,
    cache_pages,
    page_table,
    kv_cache,
    cache_variates,
    attn_gain,
    w_query,
    w_keyval,
    w_out,
    variate_bias,
    head_gain,
    w_head,
):
    r = lax.axis_index("req")
    y = lax.axis_index("y")
    z = lax.axis_index("z")
    idx = jnp.stack([r, y, z]).astype(jnp.int32)

    kv_cols = lax.ppermute(w_keyval.T, ("y", "z"), [(p, kv_target(p)) for p in range(NY * NZ)])

    kv_rows = kv_cache.reshape(SLOTS * PAGE, 2048)
    *carved, own = carve(idx, kv_rows, cache_variates, tokens, attn_gain.reshape(1, -1))
    carved, kv_cols = lax.optimization_barrier((carved, kv_cols))
    pieces = [shift("y", NY, d)(carved[d - 1]) for d in range(1, NY)]

    w_local = jnp.concatenate([w_query.T, kv_cols, w_out.T, w_head.T], axis=0)
    w_z = lax.all_to_all(
        jnp.broadcast_to(w_local[None], (NZ, 136, 128)), "z", 0, 0, tiled=True
    )
    w_z, pieces[0], pieces[2] = lax.optimization_barrier((w_z, pieces[0], pieces[2]))
    w_all = lax.all_to_all(
        jnp.broadcast_to(w_z[None, :, 0:96, :], (NR, NZ, 96, 128)), "req", 0, 0, tiled=True
    )
    late = lax.all_gather(w_z[:, 96:136, :], ("req", "y"), axis=0).reshape(NR, NY * NZ, 40, 128)

    columns = jnp.transpose(variate_ids.reshape(NY, NZ, ROWS), (1, 0, 2)).reshape(NZ, 1, 256)
    fresh_vars = lax.dynamic_index_in_dim(columns, z, 0, keepdims=False).reshape(2, 128)
    order = (y + NY - jnp.arange(NY, dtype=jnp.int32)) % NY
    slot_ids = (
        (order[:, None] * NZ + z) * SLOTS + jnp.arange(SLOTS, dtype=jnp.int32)[None, :]
    ).reshape(-1)
    used, owner = slot_table(page_table, cache_pages, slot_ids)

    lane = jnp.arange(256, dtype=jnp.int32)
    source = lane // ROWS
    positions = (
        jnp.where(source // 2 == 0, cache_pages[0], cache_pages[1]) * PAGE
        + ((source % 2) * NZ + z) * ROWS
        + lane % ROWS
    )
    steps = jnp.arange(32, dtype=F32) / 32
    freqs = jnp.exp(-math.log(10000.0) * steps)
    angle = positions.astype(F32)[None, :] * freqs[:, None]

    q_copies, app = project(
        idx, own, pieces, w_all.reshape(NR, NZ * 96, 128), jnp.cos(angle), jnp.sin(angle)
    )
    app_all = lax.all_gather(app, "y", axis=0)
    q = lax.all_to_all(q_copies, "z", 0, 0, tiled=True)
    q, late = lax.optimization_barrier((q, late))
    sent = attend(
        idx, used, owner, variate_bias, q, kv_rows, pieces, app, cache_variates, fresh_vars, columns
    )
    parts = lax.all_to_all(sent, ("y", "z"), 0, 0, tiled=True)
    hidden, logits, stats, appended = finish(
        idx, parts, tokens, late, app_all, head_gain.reshape(1, -1)
    )
    norm, peak = gather_stats(lax.all_to_all(stats, ("y", "z"), 0, 0, tiled=True))
    return hidden, appended, logits, norm, peak


def solution(mesh):
    grid = Mesh(mesh.devices.reshape(NR, NY, NZ), ("req", "y", "z"))
    every = ("req", "y", "z")
    pg = ("y", "z")
    placed = (
        P(every, None),
        P("req"),
        P("req"),
        P("req", None),
        P(every, None, None),
        P(every, None),
        P(),
        P("req", pg),
        P("req", pg),
        P("req", pg),
        P(),
        P(),
        P("req", pg),
    )
    return jax.shard_map(
        per_device,
        mesh=grid,
        in_specs=placed,
        out_specs=(P(every, None), P(every, None), P(every, None), P("req"), P("req")),
        check_vma=False,
    )
```

```python
import math

import jax
import jax.numpy as jnp
from jax import lax
from jax.experimental import pallas as pl
from jax.experimental.pallas import tpu as pltpu
from jax.sharding import Mesh
from jax.sharding import PartitionSpec as P

PAGE = 128
EPSILON = 1e-05
NEGATIVE = -1e30
NY = 4
NZ = 8
NR = 8
SLOTS = 6
ROWS = 64
HEADS = 4
PIECE = SLOTS * 128 + 16 + 2 * ROWS
DH = 64
F32 = jnp.float32
BF16 = jnp.bfloat16


def shift(axis, size, step):
    return lambda value: lax.ppermute(
        value, axis, [(i, (i + step) % size) for i in range(size)]
    )


def vmem():
    return pl.BlockSpec(memory_space=pltpu.VMEM)


def smem():
    return pl.BlockSpec(memory_space=pltpu.SMEM)


def hbm():
    return pl.BlockSpec(memory_space=pltpu.HBM)


def params(mib):
    return pltpu.CompilerParams(vmem_limit_bytes=mib * 1024 * 1024)


def dot_last(a, b):
    return lax.dot_general(a, b, (((1,), (1,)), ((), ())), preferred_element_type=F32)


def carve_kernel(idx, kv, variates, tokens, gain, *refs):
    outs = refs[0:3]
    own = refs[3]
    side, sem = refs[4:6]
    y = idx[1]
    rows = SLOTS * PAGE
    side[...] = jnp.zeros(side.shape, BF16)
    side[0:8, 0:128] = jnp.concatenate(
        [variates[...].astype(F32), jnp.zeros((2, 128), F32)], axis=0
    ).astype(BF16)
    copies = []
    for d in range(1, NY):
        yd = lax.rem(y + d, NY)
        for half in range(2):
            low = pl.multiple_of(half * 1024 + yd * 256, 256)
            copies.append(
                pltpu.make_async_copy(
                    kv.at[:, pl.ds(low, 256)],
                    outs[d - 1].at[pl.ds(0, rows), pl.ds(half * 256, 256)],
                    sem.at[2 * d - 2 + half],
                )
            )
    for c in copies:
        c.start()
    wide = tokens[...].astype(F32)
    power = jnp.sum(wide * wide, axis=1, keepdims=True) * (1.0 / 1024)
    normed = (wide * lax.rsqrt(power + EPSILON) * gain[...]).astype(BF16)
    own[...] = normed
    for d in range(1, NY):
        outs[d - 1][rows : rows + 16, :] = side[...]
        if d != 2:
            outs[d - 1][rows + 16 : rows + 80, :] = normed[:, 0:512]
            outs[d - 1][rows + 80 : rows + 144, :] = normed[:, 512:1024]
    for c in copies:
        c.wait()


def carve(idx, kv, variates, tokens, gain):
    return pl.pallas_call(
        carve_kernel,
        out_shape=[
            jax.ShapeDtypeStruct((PIECE if d != 2 else SLOTS * PAGE + 16, 512), BF16)
            for d in range(1, NY)
        ]
        + [jax.ShapeDtypeStruct((ROWS, 1024), BF16)],
        in_specs=[smem(), hbm()] + [vmem()] * 3,
        out_specs=[vmem()] * 4,
        scratch_shapes=[pltpu.VMEM((16, 512), BF16), pltpu.SemaphoreType.DMA((6,))],
        compiler_params=params(56),
    )(idx, kv, variates, tokens, gain)


def qkv_kernel(idx, own, p1, opposite, p3, w_hbm, cos_ref, sin_ref, q_out, app_out, tok, w, acc, feats, sem):
    y = idx[1]
    base = SLOTS * PAGE + 16
    copies = [
        pltpu.make_async_copy(
            own, tok.at[pl.ds(pl.multiple_of(y * ROWS, ROWS), ROWS), :], sem.at[NR]
        ),
        pltpu.make_async_copy(
            opposite,
            tok.at[pl.ds(pl.multiple_of(lax.rem(y + 2, NY) * ROWS, ROWS), ROWS), :],
            sem.at[NR + 3],
        ),
    ]
    for d, piece in ((0, p1), (2, p3)):
        ys = lax.rem(y + NY - d - 1, NY)
        for half in range(2):
            copies.append(
                pltpu.make_async_copy(
                    piece.at[pl.ds(base + half * ROWS, ROWS)],
                    tok.at[
                        pl.ds(pl.multiple_of(ys * ROWS, ROWS), ROWS), pl.ds(half * 512, 512)
                    ],
                    sem.at[NR + 1 + 2 * d + half],
                )
            )
    blocks = [pltpu.make_async_copy(w_hbm.at[r], w.at[r], sem.at[r]) for r in range(NR)]
    for c in copies + blocks:
        c.start()
    for c in copies:
        c.wait()
    for r in range(NR):
        blocks[r].wait()
        part = dot_last(w[r], tok[:, r * 128 : (r + 1) * 128])
        if r == 0:
            acc[...] = part
        else:
            acc[...] += part
    cos = cos_ref[...]
    sin = sin_ref[...]

    def rounded(zs, low, high):
        return acc[zs * 96 + low : zs * 96 + high, :].astype(BF16).astype(F32)

    for h in range(HEADS):
        a = rounded(2 * h, 0, 32)
        b = rounded(2 * h + 1, 0, 32)
        first = ((a * cos - b * sin).astype(BF16).astype(F32) * 0.125).astype(BF16)
        second = ((b * cos + a * sin).astype(BF16).astype(F32) * 0.125).astype(BF16)
        for zs in range(NZ):
            q_out[zs, h * 64 : h * 64 + 32, :] = first
            q_out[zs, h * 64 + 32 : h * 64 + 64, :] = second
        a = rounded(h, 32, 64)
        b = rounded(h, 64, 96)
        feats[h * 64 : h * 64 + 32, :] = a * cos - b * sin
        feats[h * 64 + 32 : h * 64 + 64, :] = b * cos + a * sin
        feats[256 + h * 64 : 256 + h * 64 + 64, :] = acc[(HEADS + h) * 96 + 32 : (HEADS + h) * 96 + 96, :]
    app_out[:, 0:256] = feats[0:256, :].T.astype(BF16)
    app_out[:, 256:512] = feats[256:512, :].T.astype(BF16)


def project(idx, own, p1, opposite, p3, w, cos, sin):
    return pl.pallas_call(
        qkv_kernel,
        out_shape=[
            jax.ShapeDtypeStruct((NZ, 256, 256), BF16),
            jax.ShapeDtypeStruct((256, 512), BF16),
        ],
        in_specs=[smem()] + [hbm()] * 5 + [vmem()] * 2,
        out_specs=[vmem()] * 2,
        scratch_shapes=[
            pltpu.VMEM((256, 1024), BF16),
            pltpu.VMEM((NR, NZ * 96, 128), BF16),
            pltpu.VMEM((NZ * 96, 256), F32),
            pltpu.VMEM((512, 256), F32),
            pltpu.SemaphoreType.DMA((NR + 7,)),
        ],
        compiler_params=params(56),
    )(idx, own, p1, opposite, p3, w, cos, sin)


def attn_kernel(idx, used, owner, bias, *refs):
    q, kv, p1, p2, p3, app, own_vars, fresh_vars, qvar = refs[0:9]
    out = refs[9]
    pg, qb, top, acc, side, kvs, causal, sem = refs[10:18]
    y, z = idx[1], idx[2]
    rows = SLOTS * PAGE
    copies = []
    for half in range(2):
        low = pl.multiple_of(half * 1024 + y * 256, 256)
        copies.append(
            pltpu.make_async_copy(
                kv.at[:, pl.ds(low, 256)],
                pg.at[pl.ds(0, rows), pl.ds(half * 256, 256)],
                sem.at[half],
            )
        )
    for d, piece in enumerate((p1, p2, p3)):
        copies.append(
            pltpu.make_async_copy(
                piece.at[pl.ds(0, rows)], pg.at[pl.ds((d + 1) * rows, rows)], sem.at[2 + d]
            )
        )
        copies.append(
            pltpu.make_async_copy(
                piece.at[pl.ds(rows, 16), pl.ds(0, 128)], side.at[d], sem.at[5 + d]
            )
        )
    copies.append(pltpu.make_async_copy(app, pg.at[pl.ds(NY * rows, 256)], sem.at[8]))
    for c in copies:
        c.start()

    row16 = lax.broadcasted_iota(jnp.int32, (16, 128), 0)
    vsel = row16 & 3
    level = row16 >> 2
    zero = jnp.zeros((48, 128), BF16)

    def fill(zs, carry):
        lanes = pl.ds(pl.multiple_of(zs * 128, 128), 128)
        qv_row = qvar[zs]
        for j in range(2):
            same = jnp.broadcast_to(qv_row[:, j * 128 : (j + 1) * 128], (16, 128)) == vsel
            for h in range(HEADS):
                hh = y * HEADS + h
                b = jnp.where(same, bias[0, hh], bias[1, hh])
                hi = b.astype(BF16).astype(F32)
                mid = (b - hi).astype(BF16).astype(F32)
                lo = (b - hi - mid).astype(BF16).astype(F32)
                extra = jnp.where(
                    level == 0, hi, jnp.where(level == 1, mid, jnp.where(level == 2, lo, 0.0))
                ).astype(BF16)
                q_rows = q[zs, h * 64 : (h + 1) * 64, j * 128 : (j + 1) * 128]
                if h % 2 == 0:
                    qb[j, h, 0:64, lanes] = q_rows
                    qb[j, h, 64:80, lanes] = extra
                    qb[j, h, 80:128, lanes] = zero
                else:
                    qb[j, h, 0:16, lanes] = extra
                    qb[j, h, 16:64, lanes] = zero
                    qb[j, h, 64:128, lanes] = q_rows
        key_row = lax.broadcasted_iota(jnp.int32, (128, 128), 0)
        q_lane = lax.broadcasted_iota(jnp.int32, (128, 128), 1)
        key_pos = ((key_row >> 6) * NZ + z) * ROWS + (key_row & 63)
        q_pos = ((q_lane >> 6) * NZ + zs) * ROWS + (q_lane & 63)
        causal[:, lanes] = jnp.where(key_pos <= q_pos, 0.0, NEGATIVE)
        return carry

    lax.fori_loop(0, NZ, fill, 0)
    top[...] = jnp.full(top.shape, NEGATIVE, F32)
    acc[...] = jnp.zeros(acc.shape, F32)
    for s in range(SLOTS):
        kvs[s] = own_vars[s : s + 1, :].astype(F32)
    for j in range(2):
        kvs[NY * SLOTS + j] = fresh_vars[j : j + 1, :].astype(F32)
    for c in copies:
        c.wait()
    for d in range(3):
        block = side[d].astype(F32)
        for s in range(SLOTS):
            kvs[(d + 1) * SLOTS + s] = block[s : s + 1, :]

    sub = lax.broadcasted_iota(jnp.int32, (128, 128), 0)
    variate = (sub & 3).astype(F32)
    hot_rows = (sub & 63) < 12
    low_lanes = lax.broadcasted_iota(jnp.int32, (128, 128), 1) < 64
    ones = jnp.ones((16, 128), BF16)

    def visit(slot, j, fresh):
        page = pg[pl.ds(pl.multiple_of(slot * PAGE, PAGE), PAGE), :]
        kvals = jnp.broadcast_to(kvs[slot], (128, 128))
        hot = jnp.where(hot_rows & (variate == kvals), 1.0, 0.0).T
        keys = page[:, 0:256].astype(F32)
        vals = page[:, 256:512].astype(F32).T.astype(BF16)
        kaug = []
        vaug = []
        for h in range(HEADS):
            pair = keys[:, (h // 2) * 128 : (h // 2) * 128 + 128]
            both = (pair, hot) if h % 2 == 0 else (hot, pair)
            kaug.append(jnp.where(low_lanes, both[0], both[1]).astype(BF16))
            vaug.append(jnp.concatenate([vals[h * 64 : (h + 1) * 64, :], ones], axis=0))
        olds = [top[j, h] for h in range(HEADS)]
        scores = {}
        weights = {}
        for i in range(HEADS + 2):
            if i < HEADS:
                s = jnp.dot(kaug[i], qb[j, i], preferred_element_type=F32)
                scores[i] = s + causal[...] if fresh else s
            if 1 <= i <= HEADS:
                k = i - 1
                s = scores.pop(k)
                new = jnp.maximum(olds[k], jnp.max(s, axis=0, keepdims=True))
                weights[k] = (jnp.exp(s - new).astype(BF16), new, jnp.exp(olds[k] - new))
            if i >= 2:
                k = i - 2
                p, new, keep = weights.pop(k)
                top[j, k] = new
                acc[j, k] = acc[j, k] * keep + jnp.dot(vaug[k], p, preferred_element_type=F32)

    def body(slot, carry):
        @pl.when(used[slot] > 0)
        def _():
            visit(slot, owner[slot], False)

        return carry

    lax.fori_loop(0, NY * SLOTS, body, 0)

    def last(j, carry):
        visit(NY * SLOTS + j, j, True)
        return carry

    lax.fori_loop(0, 2, last, 0)

    low64 = lax.broadcasted_iota(jnp.int32, (64, 128), 1) < 64
    low8 = lax.broadcasted_iota(jnp.int32, (8, 128), 1) < 64

    def send(zs, carry):
        lanes = pl.ds(pl.multiple_of(zs * 128, 128), 128)
        for j in range(2):
            values = []
            parts = []
            for h in range(HEADS):
                total = acc[j, h, 64:65, lanes]
                values.append(acc[j, h, 0:64, lanes] * (1.0 / total))
                lse = top[j, h, :, lanes] + jnp.log(total)
                hi = lse.astype(BF16).astype(F32)
                mid = (lse - hi).astype(BF16).astype(F32)
                parts.append(jnp.concatenate([hi, mid, lse - hi - mid], axis=0))
            blank = jnp.zeros((2, 128), F32)
            stat_a = jnp.concatenate([parts[0], parts[1], blank], axis=0)
            stat_b = jnp.concatenate([parts[2], parts[3], blank], axis=0)
            for side_row in range(2):
                p = (2 * j + side_row) * NZ + zs

                def pick(left, right, mask):
                    if side_row == 0:
                        return jnp.where(mask, left, pltpu.roll(right, 64, 1)).astype(BF16)
                    return jnp.where(mask, pltpu.roll(left, 64, 1), right).astype(BF16)

                out[p, 0:64, :] = pick(values[0], values[2], low64)
                out[p, 64:128, :] = pick(values[1], values[3], low64)
                out[p, 128:136, :] = pick(stat_a, stat_b, low8)
        return carry

    lax.fori_loop(0, NZ, send, 0)


def attend(idx, used, owner, bias, q, kv, pieces, app, own_vars, fresh_vars, qvar):
    return pl.pallas_call(
        attn_kernel,
        out_shape=jax.ShapeDtypeStruct((NY * NZ, 136, 128), BF16),
        in_specs=[smem()] * 4 + [vmem()] + [hbm()] * 5 + [vmem()] * 3,
        out_specs=vmem(),
        scratch_shapes=[
            pltpu.VMEM((26 * PAGE, 512), BF16),
            pltpu.VMEM((2, HEADS, 128, 1024), BF16),
            pltpu.VMEM((2, HEADS, 1, 1024), F32),
            pltpu.VMEM((2, HEADS, 80, 1024), F32),
            pltpu.VMEM((3, 16, 128), BF16),
            pltpu.VMEM((26, 1, 128), F32),
            pltpu.VMEM((128, 1024), F32),
            pltpu.SemaphoreType.DMA((9,)),
        ],
        compiler_params=params(56),
    )(idx, used, owner, bias, q, kv, *pieces, app, own_vars, fresh_vars, qvar)


def final_kernel(idx, parts, tokens, late, app_all, gain, hidden_out, logits_out, stats_out, app_out, wo, wh, head_in, sem):
    copies = [
        pltpu.make_async_copy(late.at[:, :, pl.ds(0, 32), :], wo, sem.at[0]),
        pltpu.make_async_copy(late.at[:, :, pl.ds(32, 8), :], wh, sem.at[1]),
    ]
    own = pl.ds(pl.multiple_of(idx[1] * ROWS, ROWS), ROWS)
    for ys in range(NY):
        for half in range(2):
            copies.append(
                pltpu.make_async_copy(
                    app_all.at[ys, own, pl.ds(half * 256, 256)],
                    app_out.at[:, pl.ds(half * 1024 + ys * 256, 256)],
                    sem.at[2 + 2 * ys + half],
                )
            )
    for c in copies:
        c.start()
    chunks = []
    for ys in range(NY):
        lses = [[], []]
        for zs in range(NZ):
            stat = parts[ys * NZ + zs, 128:136, :].astype(F32)
            for k in range(2):
                lses[k].append(stat[3 * k : 3 * k + 1] + stat[3 * k + 1 : 3 * k + 2] + stat[3 * k + 2 : 3 * k + 3])
        merged = []
        for k in range(2):
            best = lses[k][0]
            for v in lses[k][1:]:
                best = jnp.maximum(best, v)
            ws = [jnp.exp(v - best) for v in lses[k]]
            total = ws[0]
            for w in ws[1:]:
                total = total + w
            inverse = 1.0 / total
            value = None
            for zs in range(NZ):
                term = parts[ys * NZ + zs, k * 64 : (k + 1) * 64, :].astype(F32) * (ws[zs] * inverse)
                value = term if value is None else value + term
            merged.append(value)
        turned = jnp.concatenate(merged, axis=0).T.astype(BF16)
        chunks.append(turned[0:64, :])
        chunks.append(turned[64:128, :])
    for c in copies:
        c.wait()
    total = tokens[...].astype(F32)
    for r in range(NR):
        total = total + dot_last(chunks[r], wo[r].reshape(1024, 128))
    hidden = total.astype(BF16)
    hidden_out[...] = hidden
    wide = hidden.astype(F32)
    square = wide * wide
    power = jnp.sum(square, axis=1, keepdims=True)
    head_in[...] = (wide * lax.rsqrt(power * (1.0 / 1024) + EPSILON) * gain[...]).astype(BF16)
    logits = None
    for r in range(NR):
        part = dot_last(head_in[:, r * 128 : (r + 1) * 128], wh[r].reshape(256, 128))
        logits = part if logits is None else logits + part
    logits_out[...] = logits.astype(BF16)
    energy = jnp.sum(power, axis=0, keepdims=True)
    peak = jnp.max(jnp.max(logits, axis=1, keepdims=True), axis=0, keepdims=True)
    row = lax.broadcasted_iota(jnp.int32, (8, 128), 0)
    tile = jnp.where(row == 0, energy, jnp.where(row == 1, peak, 0.0))
    for p in range(NY * NZ):
        stats_out[p * 8 : (p + 1) * 8, :] = tile


def finish(idx, parts, tokens, late, app_all, gain):
    return pl.pallas_call(
        final_kernel,
        out_shape=[
            jax.ShapeDtypeStruct((ROWS, 1024), BF16),
            jax.ShapeDtypeStruct((ROWS, 256), BF16),
            jax.ShapeDtypeStruct((NY * NZ * 8, 128), F32),
            jax.ShapeDtypeStruct((ROWS, 2048), BF16),
        ],
        in_specs=[smem(), vmem(), vmem(), hbm(), hbm(), vmem()],
        out_specs=[vmem()] * 4,
        scratch_shapes=[
            pltpu.VMEM((NR, NY * NZ, 32, 128), BF16),
            pltpu.VMEM((NR, NY * NZ, 8, 128), BF16),
            pltpu.VMEM((ROWS, 1024), BF16),
            pltpu.SemaphoreType.DMA((10,)),
        ],
        compiler_params=params(56),
    )(idx, parts, tokens, late, app_all, gain)


def stats_kernel(stats, norm_out, peak_out):
    half = NY * NZ * 4
    for j in range(2):
        block = stats[j * half : (j + 1) * half, :].reshape(NY * NZ // 2, 8, 128)
        norm_out[j] = jnp.sqrt(jnp.sum(block, axis=0))[0, 0]
        peak_out[j] = jnp.max(block, axis=0)[1, 0]


def gather_stats(stats):
    return pl.pallas_call(
        stats_kernel,
        out_shape=[jax.ShapeDtypeStruct((2,), F32)] * 2,
        in_specs=[vmem()],
        out_specs=[smem()] * 2,
        compiler_params=params(4),
    )(stats)


def slot_table(table_rows, pages_held, slot_ids):
    request_count, page_count = table_rows.shape
    matches = table_rows[:, :, None] == slot_ids[None, None, :]
    live = jnp.arange(page_count, dtype=jnp.int32)[None, :, None] < pages_held[:, None, None]
    hits = jnp.any(matches & live, axis=1)
    used = jnp.any(hits, axis=0).astype(jnp.int32)
    owner = jnp.sum(
        jnp.where(hits, jnp.arange(request_count, dtype=jnp.int32)[:, None], 0), axis=0
    )
    return used, owner


def kv_target(p):
    head = p % 16
    return (head // 4) * NZ + head % 4 + (4 if p >= 16 else 0)


def per_device(
    tokens,
    variate_ids,
    cache_pages,
    page_table,
    kv_cache,
    cache_variates,
    attn_gain,
    w_query,
    w_keyval,
    w_out,
    variate_bias,
    head_gain,
    w_head,
):
    r = lax.axis_index("req")
    y = lax.axis_index("y")
    z = lax.axis_index("z")
    idx = jnp.stack([r, y, z]).astype(jnp.int32)

    kv_cols = lax.ppermute(w_keyval.T, ("y", "z"), [(p, kv_target(p)) for p in range(NY * NZ)])

    kv_rows = kv_cache.reshape(SLOTS * PAGE, 2048)
    *carved, own = carve(idx, kv_rows, cache_variates, tokens, attn_gain.reshape(1, -1))
    pieces = [shift("y", NY, d)(carved[d - 1]) for d in range(1, NY)]
    opposite = shift("y", NY, 2)(own)

    w_local = jnp.concatenate([w_query.T, kv_cols, w_out.T, w_head.T], axis=0)
    w_z = lax.all_to_all(
        jnp.broadcast_to(w_local[None], (NZ, 136, 128)), "z", 0, 0, tiled=True
    )
    w_all = lax.all_to_all(
        jnp.broadcast_to(w_z[None, :, 0:96, :], (NR, NZ, 96, 128)), "req", 0, 0, tiled=True
    )
    late = lax.all_gather(w_z[:, 96:136, :], ("req", "y"), axis=0).reshape(NR, NY * NZ, 40, 128)

    columns = jnp.transpose(variate_ids.reshape(NY, NZ, ROWS), (1, 0, 2)).reshape(NZ, 1, 256)
    fresh_vars = lax.dynamic_index_in_dim(columns, z, 0, keepdims=False).reshape(2, 128)
    order = (y + NY - jnp.arange(NY, dtype=jnp.int32)) % NY
    slot_ids = (
        (order[:, None] * NZ + z) * SLOTS + jnp.arange(SLOTS, dtype=jnp.int32)[None, :]
    ).reshape(-1)
    used, owner = slot_table(page_table, cache_pages, slot_ids)

    lane = jnp.arange(256, dtype=jnp.int32)
    source = lane // ROWS
    positions = (
        jnp.where(source // 2 == 0, cache_pages[0], cache_pages[1]) * PAGE
        + ((source % 2) * NZ + z) * ROWS
        + lane % ROWS
    )
    steps = jnp.arange(32, dtype=F32) / 32
    freqs = jnp.exp(-math.log(10000.0) * steps)
    angle = positions.astype(F32)[None, :] * freqs[:, None]

    q_copies, app = project(
        idx, own, pieces[0], opposite, pieces[2], w_all.reshape(NR, NZ * 96, 128), jnp.cos(angle), jnp.sin(angle)
    )
    app_all = lax.all_gather(app, "y", axis=0)
    q = lax.all_to_all(q_copies, "z", 0, 0, tiled=True)
    q, late = lax.optimization_barrier((q, late))
    sent = attend(
        idx, used, owner, variate_bias, q, kv_rows, pieces, app, cache_variates, fresh_vars, columns
    )
    sent, app_all = lax.optimization_barrier((sent, app_all))
    parts = lax.all_to_all(sent, ("y", "z"), 0, 0, tiled=True)
    hidden, logits, stats, appended = finish(
        idx, parts, tokens, late, app_all, head_gain.reshape(1, -1)
    )
    norm, peak = gather_stats(lax.all_to_all(stats, ("y", "z"), 0, 0, tiled=True))
    return hidden, appended, logits, norm, peak


def solution(mesh):
    grid = Mesh(mesh.devices.reshape(NR, NY, NZ), ("req", "y", "z"))
    every = ("req", "y", "z")
    pg = ("y", "z")
    placed = (
        P(every, None),
        P("req"),
        P("req"),
        P("req", None),
        P(every, None, None),
        P(every, None),
        P(),
        P("req", pg),
        P("req", pg),
        P("req", pg),
        P(),
        P(),
        P("req", pg),
    )
    return jax.shard_map(
        per_device,
        mesh=grid,
        in_specs=placed,
        out_specs=(P(every, None), P(every, None), P(every, None), P("req"), P("req")),
        check_vma=False,
    )
```

```python
import math

import jax
import jax.numpy as jnp
from jax import lax
from jax.experimental import pallas as pl
from jax.experimental.pallas import tpu as pltpu
from jax.sharding import Mesh
from jax.sharding import PartitionSpec as P

PAGE = 128
EPSILON = 1e-05
NEGATIVE = -1e30
NY = 4
NZ = 8
NR = 8
NH = 4
NG = 8
SLOTS = 6
ROWS = 64
HEADS = 2
CACHED = SLOTS * PAGE
PIECE = CACHED + 16
STEPS = [(dy, dz) for dy in range(NY) for dz in range(2)]
DH = 64
F32 = jnp.float32
BF16 = jnp.bfloat16


def partner_permute(value, dy, dz):
    pairs = []
    for g in range(NG):
        pairs.append((g, ((g // 2 + dy) % NY) * 2 + (g % 2 + dz) % 2))
    return lax.ppermute(value, ("y", "z0"), pairs)


def vmem():
    return pl.BlockSpec(memory_space=pltpu.VMEM)


def smem():
    return pl.BlockSpec(memory_space=pltpu.SMEM)


def hbm():
    return pl.BlockSpec(memory_space=pltpu.HBM)


def params(mib):
    return pltpu.CompilerParams(vmem_limit_bytes=mib * 1024 * 1024)


def dot_last(a, b):
    return lax.dot_general(a, b, (((1,), (1,)), ((), ())), preferred_element_type=F32)


def carve_kernel(idx, kv, variates, *refs):
    outs = refs[0:7]
    side, sem = refs[7:9]
    y, z0 = idx[1], idx[3]
    side[...] = jnp.zeros(side.shape, BF16)
    side[0:8, 0:128] = jnp.concatenate(
        [variates[...].astype(F32), jnp.zeros((2, 128), F32)], axis=0
    ).astype(BF16)
    copies = []
    for o, (dy, dz) in enumerate(STEPS[1:]):
        target = lax.rem(y + dy, NY) * 2 + lax.rem(z0 + dz, 2)
        for half in range(2):
            low = pl.multiple_of(half * 1024 + target * 128, 128)
            copies.append(
                pltpu.make_async_copy(
                    kv.at[:, pl.ds(low, 128)],
                    outs[o].at[pl.ds(0, CACHED), pl.ds(half * 128, 128)],
                    sem.at[2 * o + half],
                )
            )
    for c in copies:
        c.start()
    for o in range(7):
        outs[o][CACHED:PIECE, :] = side[...]
    for c in copies:
        c.wait()


def carve(idx, kv, variates):
    return pl.pallas_call(
        carve_kernel,
        out_shape=[jax.ShapeDtypeStruct((PIECE, 256), BF16)] * 7,
        in_specs=[smem(), hbm(), vmem()],
        out_specs=[vmem()] * 7,
        scratch_shapes=[pltpu.VMEM((16, 256), BF16), pltpu.SemaphoreType.DMA((14,))],
        compiler_params=params(56),
    )(idx, kv, variates)


def qkv_kernel(
    idx, t0, t1, t2, t3, w_hbm, cos_ref, sin_ref, q_out, app_out, tok, w, acc, feats, sem
):
    y, z0 = idx[1], idx[3]
    copies = []
    for dy, pair in enumerate((t0, t1, t2, t3)):
        ys = lax.rem(y + NY - dy, NY)
        for dz in range(2):
            row = pl.multiple_of((ys * 2 + lax.rem(z0 + dz, 2)) * ROWS, ROWS)
            copies.append(
                pltpu.make_async_copy(
                    pair.at[pl.ds(dz * ROWS, ROWS)],
                    tok.at[pl.ds(row, ROWS)],
                    sem.at[NR + 2 * dy + dz],
                )
            )
    blocks = [pltpu.make_async_copy(w_hbm.at[r], w.at[r], sem.at[r]) for r in range(NR)]
    for c in copies + blocks:
        c.start()
    for c in copies:
        c.wait()
    for r in range(NR):
        blocks[r].wait()
        part = dot_last(w[r], tok[:, r * 128 : (r + 1) * 128])
        if r == 0:
            acc[...] = part
        else:
            acc[...] += part
    cos = cos_ref[...]
    sin = sin_ref[...]

    def rounded(block, low, high):
        return acc[block * 96 + low : block * 96 + high, :].astype(BF16).astype(F32)

    for h in range(HEADS):
        a = rounded(2 * h, 0, 32)
        b = rounded(2 * h + 1, 0, 32)
        first = ((a * cos - b * sin).astype(BF16).astype(F32) * 0.125).astype(BF16)
        second = ((b * cos + a * sin).astype(BF16).astype(F32) * 0.125).astype(BF16)
        for zs in range(NH):
            q_out[zs, h * 64 : h * 64 + 32, :] = first
            q_out[zs, h * 64 + 32 : h * 64 + 64, :] = second
        a = rounded(h, 32, 64)
        b = rounded(h, 64, 96)
        feats[h * 64 : h * 64 + 32, :] = a * cos - b * sin
        feats[h * 64 + 32 : h * 64 + 64, :] = b * cos + a * sin
        feats[128 + h * 64 : 128 + h * 64 + 64, :] = acc[
            (HEADS + h) * 96 + 32 : (HEADS + h) * 96 + 96, :
        ]
    app_out[...] = feats[...].T.astype(BF16)


def project(idx, toks, w, cos, sin):
    return pl.pallas_call(
        qkv_kernel,
        out_shape=[
            jax.ShapeDtypeStruct((NH, 128, 512), BF16),
            jax.ShapeDtypeStruct((512, 256), BF16),
        ],
        in_specs=[smem()] + [hbm()] * 5 + [vmem()] * 2,
        out_specs=[vmem()] * 2,
        scratch_shapes=[
            pltpu.VMEM((512, 1024), BF16),
            pltpu.VMEM((NR, NH * 96, 128), BF16),
            pltpu.VMEM((NH * 96, 512), F32),
            pltpu.VMEM((256, 512), F32),
            pltpu.SemaphoreType.DMA((2 * NR,)),
        ],
        compiler_params=params(56),
    )(idx, *toks, w, cos, sin)


def attn_kernel(idx, used, owner, bias, *refs):
    q, kv = refs[0:2]
    pieces = refs[2:9]
    app, own_vars, fresh_vars, qvar = refs[9:13]
    out = refs[13]
    pg, qb, top, acc, side, kvs, causal, order, sem = refs[14:23]
    y, z1, z0 = idx[1], idx[2], idx[3]
    group = y * 2 + z0
    fresh_base = NG * SLOTS
    copies = []
    for half in range(2):
        low = pl.multiple_of(half * 1024 + group * 128, 128)
        copies.append(
            pltpu.make_async_copy(
                kv.at[:, pl.ds(low, 128)],
                pg.at[pl.ds(0, CACHED), pl.ds(half * 128, 128)],
                sem.at[half],
            )
        )
    for o in range(7):
        copies.append(
            pltpu.make_async_copy(
                pieces[o].at[pl.ds(0, CACHED)],
                pg.at[pl.ds((o + 1) * CACHED, CACHED)],
                sem.at[2 + 2 * o],
            )
        )
        copies.append(
            pltpu.make_async_copy(
                pieces[o].at[pl.ds(CACHED, 16), pl.ds(0, 128)], side.at[o], sem.at[3 + 2 * o]
            )
        )
    copies.append(pltpu.make_async_copy(app, pg.at[pl.ds(NG * CACHED, 512)], sem.at[16]))
    for c in copies:
        c.start()

    def collect(slot, count):
        order[count] = slot
        return count + used[slot]

    count = lax.fori_loop(0, fresh_base, collect, 0)

    row16 = lax.broadcasted_iota(jnp.int32, (16, 256), 0)
    vsel = row16 & 3
    level = row16 >> 2
    zero = jnp.zeros((48, 256), BF16)

    def fill(zs, carry):
        lanes = pl.ds(pl.multiple_of(zs * 256, 256), 256)
        qv_row = qvar[zs]
        for j in range(2):
            same = jnp.broadcast_to(qv_row[:, j * 256 : (j + 1) * 256], (16, 256)) == vsel
            for h in range(HEADS):
                hh = group * HEADS + h
                b = jnp.where(same, bias[0, hh], bias[1, hh])
                hi = b.astype(BF16).astype(F32)
                mid = (b - hi).astype(BF16).astype(F32)
                lo = (b - hi - mid).astype(BF16).astype(F32)
                extra = jnp.where(
                    level == 0, hi, jnp.where(level == 1, mid, jnp.where(level == 2, lo, 0.0))
                ).astype(BF16)
                q_rows = q[zs, h * 64 : (h + 1) * 64, j * 256 : (j + 1) * 256]
                if h % 2 == 0:
                    qb[j, h, 0:64, lanes] = q_rows
                    qb[j, h, 64:80, lanes] = extra
                    qb[j, h, 80:128, lanes] = zero
                else:
                    qb[j, h, 0:16, lanes] = extra
                    qb[j, h, 16:64, lanes] = zero
                    qb[j, h, 64:128, lanes] = q_rows
        key_row = lax.broadcasted_iota(jnp.int32, (128, 256), 0)
        q_lane = lax.broadcasted_iota(jnp.int32, (128, 256), 1)
        q_pos = ((q_lane >> 7) * NZ + zs * 2 + ((q_lane >> 6) & 1)) * ROWS + (q_lane & 63)
        for f in range(2):
            key_pos = (f * NZ + z1 * 2 + (key_row >> 6)) * ROWS + (key_row & 63)
            causal[f, :, lanes] = jnp.where(key_pos <= q_pos, 0.0, NEGATIVE)
        return carry

    lax.fori_loop(0, NH, fill, 0)
    top[...] = jnp.full(top.shape, NEGATIVE, F32)
    acc[...] = jnp.zeros(acc.shape, F32)
    for s in range(SLOTS):
        kvs[s] = own_vars[s : s + 1, :].astype(F32)
    for f in range(4):
        kvs[fresh_base + f] = fresh_vars[f : f + 1, :].astype(F32)
    for c in copies:
        c.wait()
    for o in range(7):
        block = side[o].astype(F32)
        for s in range(SLOTS):
            kvs[(o + 1) * SLOTS + s] = block[s : s + 1, :]

    sub = lax.broadcasted_iota(jnp.int32, (128, 128), 0)
    variate = (sub & 3).astype(F32)
    hot_rows = (sub & 63) < 12
    low_lanes = lax.broadcasted_iota(jnp.int32, (128, 128), 1) < 64
    ones = jnp.ones((16, 128), BF16)

    def visit(slots, js, fresh):
        tiles = []
        for n, slot in enumerate(slots):
            page = pg[pl.ds(pl.multiple_of(slot * PAGE, PAGE), PAGE), :]
            kvals = jnp.broadcast_to(kvs[slot], (128, 128))
            hot = jnp.where(hot_rows & (variate == kvals), 1.0, 0.0).T
            pair = page[:, 0:128].astype(F32)
            vals = page[:, 128:256].astype(F32).T.astype(BF16)
            for h in range(HEADS):
                both = (pair, hot) if h == 0 else (hot, pair)
                kaug = jnp.where(low_lanes, both[0], both[1]).astype(BF16)
                vaug = jnp.concatenate([vals[h * 64 : (h + 1) * 64, :], ones], axis=0)
                tiles.append((n, js[n], h, kaug, vaug))
        total = len(tiles)
        scores = {}
        weights = {}
        for i in range(total + 2):
            if i < total:
                n, j, h, kaug, _ = tiles[i]
                s = jnp.dot(kaug, qb[j, h], preferred_element_type=F32)
                scores[i] = s + causal[n] if fresh else s
            if 1 <= i <= total:
                n, j, h, _, _ = tiles[i - 1]
                s = scores.pop(i - 1)
                old = top[j, h]
                new = jnp.maximum(old, jnp.max(s, axis=0, keepdims=True))
                top[j, h] = new
                weights[i - 1] = (jnp.exp(s - new).astype(BF16), jnp.exp(old - new))
            if i >= 2:
                n, j, h, _, vaug = tiles[i - 2]
                p, keep = weights.pop(i - 2)
                acc[j, h] = acc[j, h] * keep + jnp.dot(vaug, p, preferred_element_type=F32)

    def body(i, carry):
        a = order[2 * i]
        b = order[2 * i + 1]
        visit([a, b], [owner[a], owner[b]], False)
        return carry

    lax.fori_loop(0, count // 2, body, 0)

    @pl.when(count % 2 == 1)
    def _():
        a = order[count - 1]
        visit([a], [owner[a]], False)

    def last(j, carry):
        visit([fresh_base + 2 * j, fresh_base + 2 * j + 1], [j, j], True)
        return carry

    lax.fori_loop(0, 2, last, 0)

    low64 = lax.broadcasted_iota(jnp.int32, (64, 128), 1) < 64
    low8 = lax.broadcasted_iota(jnp.int32, (8, 128), 1) < 64

    def send(zs, carry):
        for j in range(2):
            for yb in range(2):
                lanes = pl.ds(pl.multiple_of(zs * 256 + yb * 128, 128), 128)
                values = []
                parts = []
                for h in range(HEADS):
                    total = acc[j, h, 64:65, lanes]
                    values.append(acc[j, h, 0:64, lanes] * (1.0 / total))
                    lse = top[j, h, :, lanes] + jnp.log(total)
                    hi = lse.astype(BF16).astype(F32)
                    mid = (lse - hi).astype(BF16).astype(F32)
                    parts.append(
                        jnp.concatenate([hi, mid, lse - hi - mid, jnp.zeros((5, 128), F32)], axis=0)
                    )
                for zb in range(2):
                    p = (2 * j + yb) * NZ + zs * 2 + zb
                    if zb == 0:
                        body_rows = jnp.where(low64, values[0], pltpu.roll(values[1], 64, 1))
                        stat_rows = jnp.where(low8, parts[0], pltpu.roll(parts[1], 64, 1))
                    else:
                        body_rows = jnp.where(low64, pltpu.roll(values[0], 64, 1), values[1])
                        stat_rows = jnp.where(low8, pltpu.roll(parts[0], 64, 1), parts[1])
                    out[p, 0:64, :] = body_rows.astype(BF16)
                    out[p, 64:72, :] = stat_rows.astype(BF16)
        return carry

    lax.fori_loop(0, NH, send, 0)


def attend(idx, used, owner, bias, q, kv, pieces, app, own_vars, fresh_vars, qvar):
    return pl.pallas_call(
        attn_kernel,
        out_shape=jax.ShapeDtypeStruct((NY * NZ, 72, 128), BF16),
        in_specs=[smem()] * 4 + [vmem()] + [hbm()] * 9 + [vmem()] * 3,
        out_specs=vmem(),
        scratch_shapes=[
            pltpu.VMEM((NG * CACHED + 512, 256), BF16),
            pltpu.VMEM((2, HEADS, 128, 1024), BF16),
            pltpu.VMEM((2, HEADS, 1, 1024), F32),
            pltpu.VMEM((2, HEADS, 80, 1024), F32),
            pltpu.VMEM((7, 16, 128), BF16),
            pltpu.VMEM((NG * SLOTS + 4, 1, 128), F32),
            pltpu.VMEM((2, 128, 1024), F32),
            pltpu.SMEM((NG * SLOTS + 2,), jnp.int32),
            pltpu.SemaphoreType.DMA((17,)),
        ],
        compiler_params=params(56),
    )(idx, used, owner, bias, q, kv, *pieces, app, own_vars, fresh_vars, qvar)


def final_kernel(
    idx, parts, tokens, late, app_all, gain, hidden_out, logits_out, stats_out, app_out, wo, wh, head_in, sem
):
    group = idx[1] * 2 + idx[3]
    copies = [
        pltpu.make_async_copy(late.at[:, :, pl.ds(0, 32), :], wo, sem.at[0]),
        pltpu.make_async_copy(late.at[:, :, pl.ds(32, 8), :], wh, sem.at[1]),
    ]
    own = pl.ds(pl.multiple_of(group * ROWS, ROWS), ROWS)
    for g in range(NG):
        for half in range(2):
            copies.append(
                pltpu.make_async_copy(
                    app_all.at[g, own, pl.ds(half * 128, 128)],
                    app_out.at[:, pl.ds(half * 1024 + g * 128, 128)],
                    sem.at[2 + 2 * g + half],
                )
            )
    for c in copies:
        c.start()
    low64 = lax.broadcasted_iota(jnp.int32, (64, 128), 1) < 64
    merged = []
    for g in range(NG):
        sources = [(g // 2) * NZ + zs * 2 + g % 2 for zs in range(NH)]
        lses = []
        for p in sources:
            stat = parts[p, 64:72, :].astype(F32)
            lses.append(stat[0:1] + stat[1:2] + stat[2:3])
        best = lses[0]
        for v in lses[1:]:
            best = jnp.maximum(best, v)
        ws = [jnp.exp(v - best) for v in lses]
        total = ws[0]
        for w in ws[1:]:
            total = total + w
        inverse = 1.0 / total
        value = None
        for p, w in zip(sources, ws):
            term = parts[p, 0:64, :].astype(F32) * (w * inverse)
            value = term if value is None else value + term
        merged.append(value)
    chunks = []
    for g in range(0, NG, 2):
        turned = jnp.concatenate([merged[g], merged[g + 1]], axis=0).T
        upper = turned[0:64, :]
        lower = turned[64:128, :]
        chunks.append(jnp.where(low64, upper, pltpu.roll(lower, 64, 1)).astype(BF16))
        chunks.append(jnp.where(low64, pltpu.roll(upper, 64, 1), lower).astype(BF16))
    for c in copies:
        c.wait()
    total = tokens[...].astype(F32)
    for r in range(NR):
        total = total + dot_last(chunks[r], wo[r].reshape(1024, 128))
    hidden = total.astype(BF16)
    hidden_out[...] = hidden
    wide = hidden.astype(F32)
    square = wide * wide
    power = jnp.sum(square, axis=1, keepdims=True)
    head_in[...] = (wide * lax.rsqrt(power * (1.0 / 1024) + EPSILON) * gain[...]).astype(BF16)
    logits = None
    for r in range(NR):
        part = dot_last(head_in[:, r * 128 : (r + 1) * 128], wh[r].reshape(256, 128))
        logits = part if logits is None else logits + part
    logits_out[...] = logits.astype(BF16)
    energy = jnp.sum(power, axis=0, keepdims=True)
    peak = jnp.max(jnp.max(logits, axis=1, keepdims=True), axis=0, keepdims=True)
    row = lax.broadcasted_iota(jnp.int32, (8, 128), 0)
    tile = jnp.where(row == 0, energy, jnp.where(row == 1, peak, 0.0))
    for p in range(NY * NZ):
        stats_out[p * 8 : (p + 1) * 8, :] = tile


def finish(idx, parts, tokens, late, app_all, gain):
    return pl.pallas_call(
        final_kernel,
        out_shape=[
            jax.ShapeDtypeStruct((ROWS, 1024), BF16),
            jax.ShapeDtypeStruct((ROWS, 256), BF16),
            jax.ShapeDtypeStruct((NY * NZ * 8, 128), F32),
            jax.ShapeDtypeStruct((ROWS, 2048), BF16),
        ],
        in_specs=[smem(), vmem(), vmem(), hbm(), hbm(), vmem()],
        out_specs=[vmem()] * 4,
        scratch_shapes=[
            pltpu.VMEM((NR, NY * NZ, 32, 128), BF16),
            pltpu.VMEM((NR, NY * NZ, 8, 128), BF16),
            pltpu.VMEM((ROWS, 1024), BF16),
            pltpu.SemaphoreType.DMA((18,)),
        ],
        compiler_params=params(56),
    )(idx, parts, tokens, late, app_all, gain)


def stats_kernel(stats, norm_out, peak_out):
    half = NY * NZ * 4
    for j in range(2):
        block = stats[j * half : (j + 1) * half, :].reshape(NY * NZ // 2, 8, 128)
        norm_out[j] = jnp.sqrt(jnp.sum(block, axis=0))[0, 0]
        peak_out[j] = jnp.max(block, axis=0)[1, 0]


def gather_stats(stats):
    return pl.pallas_call(
        stats_kernel,
        out_shape=[jax.ShapeDtypeStruct((2,), F32)] * 2,
        in_specs=[vmem()],
        out_specs=[smem()] * 2,
        compiler_params=params(4),
    )(stats)


def slot_table(table_rows, pages_held, slot_ids):
    request_count, page_count = table_rows.shape
    matches = table_rows[:, :, None] == slot_ids[None, None, :]
    live = jnp.arange(page_count, dtype=jnp.int32)[None, :, None] < pages_held[:, None, None]
    hits = jnp.any(matches & live, axis=1)
    used = jnp.any(hits, axis=0).astype(jnp.int32)
    owner = jnp.sum(
        jnp.where(hits, jnp.arange(request_count, dtype=jnp.int32)[:, None], 0), axis=0
    )
    return used, owner


def q_target(p):
    group, block = p // 4, p % 4
    return (group // 2) * NZ + block * 2 + group % 2


def kv_target(p):
    head = p % 16
    group = head // 2
    return (group // 2) * NZ + (head % 2 + (2 if p >= 16 else 0)) * 2 + group % 2


def per_device(
    tokens,
    variate_ids,
    cache_pages,
    page_table,
    kv_cache,
    cache_variates,
    attn_gain,
    w_query,
    w_keyval,
    w_out,
    variate_bias,
    head_gain,
    w_head,
):
    r = lax.axis_index("req")
    y = lax.axis_index("y")
    z1 = lax.axis_index("z1")
    z0 = lax.axis_index("z0")
    idx = jnp.stack([r, y, z1, z0]).astype(jnp.int32)
    pg = ("y", "z1", "z0")

    q_cols = lax.ppermute(w_query.T, pg, [(p, q_target(p)) for p in range(NY * NZ)])
    kv_cols = lax.ppermute(w_keyval.T, pg, [(p, kv_target(p)) for p in range(NY * NZ)])

    kv_rows = kv_cache.reshape(CACHED, 2048)
    carved = carve(idx, kv_rows, cache_variates)
    pieces = [partner_permute(c, dy, dz) for c, (dy, dz) in zip(carved, STEPS[1:])]

    w_local = jnp.concatenate([q_cols, kv_cols, w_out.T, w_head.T], axis=0)
    w_z = lax.all_to_all(
        jnp.broadcast_to(w_local[None], (NZ, 136, 128)), ("z1", "z0"), 0, 0, tiled=True
    )
    w_z, pieces[0], pieces[3] = lax.optimization_barrier((w_z, pieces[0], pieces[3]))
    w_mine = lax.dynamic_index_in_dim(
        w_z[:, 0:96, :].reshape(NH, 2, 96, 128), z0, 1, keepdims=False
    )
    w_all = lax.all_to_all(
        jnp.broadcast_to(w_mine[None], (NR, NH, 96, 128)), "req", 0, 0, tiled=True
    )
    late = lax.all_gather(w_z[:, 96:136, :], ("req", "y"), axis=0).reshape(NR, NY * NZ, 40, 128)

    wide = tokens.astype(F32)
    power = jnp.mean(wide * wide, axis=-1, keepdims=True)
    normed = (wide * lax.rsqrt(power + EPSILON) * attn_gain).astype(BF16)
    pair = jnp.concatenate([normed, partner_permute(normed, 0, 1)], axis=0)
    toks = [pair] + [partner_permute(pair, dy, 0) for dy in range(1, NY)]
    toks[0], pieces[4] = lax.optimization_barrier((toks[0], pieces[4]))

    columns = jnp.transpose(variate_ids.reshape(NY, NH, 2 * ROWS), (1, 0, 2)).reshape(NH, 1, 512)
    fresh_vars = lax.dynamic_index_in_dim(columns, z1, 0, keepdims=False).reshape(4, 128)
    slot_ids = jnp.stack(
        [
            (((y + NY - dy) % NY) * NZ + z1 * 2 + (z0 + dz) % 2) * SLOTS + s
            for dy, dz in STEPS
            for s in range(SLOTS)
        ]
    ).astype(jnp.int32)
    used, owner = slot_table(page_table, cache_pages, slot_ids)

    lane = jnp.arange(512, dtype=jnp.int32)
    source = lane // ROWS
    positions = (
        jnp.where(source // 4 == 0, cache_pages[0], cache_pages[1]) * PAGE
        + (((source // 2) % 2) * NZ + z1 * 2 + source % 2) * ROWS
        + lane % ROWS
    )
    steps = jnp.arange(32, dtype=F32) / 32
    freqs = jnp.exp(-math.log(10000.0) * steps)
    angle = positions.astype(F32)[None, :] * freqs[:, None]

    q_copies, app = project(
        idx, toks, w_all.reshape(NR, NH * 96, 128), jnp.cos(angle), jnp.sin(angle)
    )
    app_all = lax.all_gather(app, ("y", "z0"), axis=0)
    q = lax.all_to_all(q_copies, "z1", 0, 0, tiled=True)
    sent = attend(
        idx, used, owner, variate_bias, q, kv_rows, pieces, app, cache_variates, fresh_vars, columns
    )
    sent, app_all, late = lax.optimization_barrier((sent, app_all, late))
    parts = lax.all_to_all(sent, pg, 0, 0, tiled=True)
    hidden, logits, stats, appended = finish(
        idx, parts, tokens, late, app_all, head_gain.reshape(1, -1)
    )
    norm, peak = gather_stats(lax.all_to_all(stats, pg, 0, 0, tiled=True))
    return hidden, appended, logits, norm, peak


def solution(mesh):
    grid = Mesh(mesh.devices.reshape(NR, NY, NH, 2), ("req", "y", "z1", "z0"))
    every = ("req", "y", "z1", "z0")
    pg = ("y", "z1", "z0")
    placed = (
        P(every, None),
        P("req"),
        P("req"),
        P("req", None),
        P(every, None, None),
        P(every, None),
        P(),
        P("req", pg),
        P("req", pg),
        P("req", pg),
        P(),
        P(),
        P("req", pg),
    )
    return jax.shard_map(
        per_device,
        mesh=grid,
        in_specs=placed,
        out_specs=(P(every, None), P(every, None), P(every, None), P("req"), P("req")),
        check_vma=False,
    )
```

```python
import math

import jax
import jax.numpy as jnp
from jax import lax
from jax.experimental import pallas as pl
from jax.experimental.pallas import tpu as pltpu
from jax.sharding import Mesh
from jax.sharding import PartitionSpec as P

PAGE = 128
EPSILON = 1e-05
NEGATIVE = -1e30
NY = 4
NZ = 8
NR = 8
SLOTS = 6
ROWS = 64
HEADS = 4
PIECE = SLOTS * 128 + 16 + 2 * ROWS
DH = 64
F32 = jnp.float32
BF16 = jnp.bfloat16


def shift(axis, size, step):
    return lambda value: lax.ppermute(
        value, axis, [(i, (i + step) % size) for i in range(size)]
    )


def vmem():
    return pl.BlockSpec(memory_space=pltpu.VMEM)


def smem():
    return pl.BlockSpec(memory_space=pltpu.SMEM)


def hbm():
    return pl.BlockSpec(memory_space=pltpu.HBM)


def params(mib):
    return pltpu.CompilerParams(vmem_limit_bytes=mib * 1024 * 1024)


def dot_last(a, b):
    return lax.dot_general(a, b, (((1,), (1,)), ((), ())), preferred_element_type=F32)


def carve_kernel(idx, kv, variates, normed, *refs):
    outs = refs[0:3]
    side, sem = refs[3:5]
    y = idx[1]
    rows = SLOTS * PAGE
    side[...] = jnp.zeros(side.shape, BF16)
    side[0:8, 0:128] = jnp.concatenate(
        [variates[...].astype(F32), jnp.zeros((2, 128), F32)], axis=0
    ).astype(BF16)
    copies = []
    for d in range(1, NY):
        yd = lax.rem(y + d, NY)
        for half in range(2):
            low = pl.multiple_of(half * 1024 + yd * 256, 256)
            copies.append(
                pltpu.make_async_copy(
                    kv.at[:, pl.ds(low, 256)],
                    outs[d - 1].at[pl.ds(0, rows), pl.ds(half * 256, 256)],
                    sem.at[2 * d - 2 + half],
                )
            )
    for c in copies:
        c.start()
    for d in range(1, NY):
        outs[d - 1][rows : rows + 16, :] = side[...]
        if d != 2:
            outs[d - 1][rows + 16 : rows + 80, :] = normed[:, 0:512]
            outs[d - 1][rows + 80 : rows + 144, :] = normed[:, 512:1024]
    for c in copies:
        c.wait()


def carve(idx, kv, variates, normed):
    return pl.pallas_call(
        carve_kernel,
        out_shape=[
            jax.ShapeDtypeStruct((PIECE if d != 2 else SLOTS * PAGE + 16, 512), BF16)
            for d in range(1, NY)
        ],
        in_specs=[smem(), hbm()] + [vmem()] * 2,
        out_specs=[vmem()] * 3,
        scratch_shapes=[pltpu.VMEM((16, 512), BF16), pltpu.SemaphoreType.DMA((6,))],
        compiler_params=params(56),
    )(idx, kv, variates, normed)


def qkv_kernel(idx, own, p1, opposite, p3, w_hbm, cos_ref, sin_ref, q_out, app_out, tok, w, acc, feats, sem):
    y = idx[1]
    base = SLOTS * PAGE + 16
    copies = [
        pltpu.make_async_copy(
            own, tok.at[pl.ds(pl.multiple_of(y * ROWS, ROWS), ROWS), :], sem.at[NR]
        ),
        pltpu.make_async_copy(
            opposite,
            tok.at[pl.ds(pl.multiple_of(lax.rem(y + 2, NY) * ROWS, ROWS), ROWS), :],
            sem.at[NR + 3],
        ),
    ]
    for d, piece in ((0, p1), (2, p3)):
        ys = lax.rem(y + NY - d - 1, NY)
        for half in range(2):
            copies.append(
                pltpu.make_async_copy(
                    piece.at[pl.ds(base + half * ROWS, ROWS)],
                    tok.at[
                        pl.ds(pl.multiple_of(ys * ROWS, ROWS), ROWS), pl.ds(half * 512, 512)
                    ],
                    sem.at[NR + 1 + 2 * d + half],
                )
            )
    blocks = [pltpu.make_async_copy(w_hbm.at[r], w.at[r], sem.at[r]) for r in range(NR)]
    for c in copies + blocks:
        c.start()
    for c in copies:
        c.wait()
    for r in range(NR):
        blocks[r].wait()
        part = dot_last(w[r], tok[:, r * 128 : (r + 1) * 128])
        if r == 0:
            acc[...] = part
        else:
            acc[...] += part
    cos = cos_ref[...]
    sin = sin_ref[...]

    def rounded(zs, low, high):
        return acc[zs * 96 + low : zs * 96 + high, :].astype(BF16).astype(F32)

    for h in range(HEADS):
        a = rounded(2 * h, 0, 32)
        b = rounded(2 * h + 1, 0, 32)
        first = ((a * cos - b * sin).astype(BF16).astype(F32) * 0.125).astype(BF16)
        second = ((b * cos + a * sin).astype(BF16).astype(F32) * 0.125).astype(BF16)
        for zs in range(NZ):
            q_out[zs, h * 64 : h * 64 + 32, :] = first
            q_out[zs, h * 64 + 32 : h * 64 + 64, :] = second
        a = rounded(h, 32, 64)
        b = rounded(h, 64, 96)
        feats[h * 64 : h * 64 + 32, :] = a * cos - b * sin
        feats[h * 64 + 32 : h * 64 + 64, :] = b * cos + a * sin
        feats[256 + h * 64 : 256 + h * 64 + 64, :] = acc[(HEADS + h) * 96 + 32 : (HEADS + h) * 96 + 96, :]
    app_out[:, 0:256] = feats[0:256, :].T.astype(BF16)
    app_out[:, 256:512] = feats[256:512, :].T.astype(BF16)


def project(idx, own, p1, opposite, p3, w, cos, sin):
    return pl.pallas_call(
        qkv_kernel,
        out_shape=[
            jax.ShapeDtypeStruct((NZ, 256, 256), BF16),
            jax.ShapeDtypeStruct((256, 512), BF16),
        ],
        in_specs=[smem()] + [hbm()] * 5 + [vmem()] * 2,
        out_specs=[vmem()] * 2,
        scratch_shapes=[
            pltpu.VMEM((256, 1024), BF16),
            pltpu.VMEM((NR, NZ * 96, 128), BF16),
            pltpu.VMEM((NZ * 96, 256), F32),
            pltpu.VMEM((512, 256), F32),
            pltpu.SemaphoreType.DMA((NR + 7,)),
        ],
        compiler_params=params(56),
    )(idx, own, p1, opposite, p3, w, cos, sin)


def attn_kernel(idx, used, owner, bias, *refs):
    q, kv, p1, p2, p3, app, own_vars, fresh_vars, qvar = refs[0:9]
    out = refs[9]
    pg, qb, top, acc, side, kvs, causal, sem = refs[10:18]
    y, z = idx[1], idx[2]
    rows = SLOTS * PAGE
    copies = []
    for half in range(2):
        low = pl.multiple_of(half * 1024 + y * 256, 256)
        copies.append(
            pltpu.make_async_copy(
                kv.at[:, pl.ds(low, 256)],
                pg.at[pl.ds(0, rows), pl.ds(half * 256, 256)],
                sem.at[half],
            )
        )
    for d, piece in enumerate((p1, p2, p3)):
        copies.append(
            pltpu.make_async_copy(
                piece.at[pl.ds(0, rows)], pg.at[pl.ds((d + 1) * rows, rows)], sem.at[2 + d]
            )
        )
        copies.append(
            pltpu.make_async_copy(
                piece.at[pl.ds(rows, 16), pl.ds(0, 128)], side.at[d], sem.at[5 + d]
            )
        )
    copies.append(pltpu.make_async_copy(app, pg.at[pl.ds(NY * rows, 256)], sem.at[8]))
    for c in copies:
        c.start()

    row16 = lax.broadcasted_iota(jnp.int32, (16, 128), 0)
    vsel = row16 & 3
    level = row16 >> 2
    zero = jnp.zeros((48, 128), BF16)

    def fill(zs, carry):
        lanes = pl.ds(pl.multiple_of(zs * 128, 128), 128)
        qv_row = qvar[zs]
        for j in range(2):
            same = jnp.broadcast_to(qv_row[:, j * 128 : (j + 1) * 128], (16, 128)) == vsel
            for h in range(HEADS):
                hh = y * HEADS + h
                b = jnp.where(same, bias[0, hh], bias[1, hh])
                hi = b.astype(BF16).astype(F32)
                mid = (b - hi).astype(BF16).astype(F32)
                lo = (b - hi - mid).astype(BF16).astype(F32)
                extra = jnp.where(
                    level == 0, hi, jnp.where(level == 1, mid, jnp.where(level == 2, lo, 0.0))
                ).astype(BF16)
                q_rows = q[zs, h * 64 : (h + 1) * 64, j * 128 : (j + 1) * 128]
                if h % 2 == 0:
                    qb[j, h, 0:64, lanes] = q_rows
                    qb[j, h, 64:80, lanes] = extra
                    qb[j, h, 80:128, lanes] = zero
                else:
                    qb[j, h, 0:16, lanes] = extra
                    qb[j, h, 16:64, lanes] = zero
                    qb[j, h, 64:128, lanes] = q_rows
        key_row = lax.broadcasted_iota(jnp.int32, (128, 128), 0)
        q_lane = lax.broadcasted_iota(jnp.int32, (128, 128), 1)
        key_pos = ((key_row >> 6) * NZ + z) * ROWS + (key_row & 63)
        q_pos = ((q_lane >> 6) * NZ + zs) * ROWS + (q_lane & 63)
        causal[:, lanes] = jnp.where(key_pos <= q_pos, 0.0, NEGATIVE)
        return carry

    lax.fori_loop(0, NZ, fill, 0)
    top[...] = jnp.full(top.shape, NEGATIVE, F32)
    acc[...] = jnp.zeros(acc.shape, F32)
    for s in range(SLOTS):
        kvs[s] = own_vars[s : s + 1, :].astype(F32)
    for j in range(2):
        kvs[NY * SLOTS + j] = fresh_vars[j : j + 1, :].astype(F32)
    for c in copies:
        c.wait()
    for d in range(3):
        block = side[d].astype(F32)
        for s in range(SLOTS):
            kvs[(d + 1) * SLOTS + s] = block[s : s + 1, :]

    sub = lax.broadcasted_iota(jnp.int32, (128, 128), 0)
    variate = (sub & 3).astype(F32)
    hot_rows = (sub & 63) < 12
    low_lanes = lax.broadcasted_iota(jnp.int32, (128, 128), 1) < 64
    ones = jnp.ones((16, 128), BF16)

    def visit(slot, j, fresh):
        page = pg[pl.ds(pl.multiple_of(slot * PAGE, PAGE), PAGE), :]
        kvals = jnp.broadcast_to(kvs[slot], (128, 128))
        hot = jnp.where(hot_rows & (variate == kvals), 1.0, 0.0).T
        keys = page[:, 0:256].astype(F32)
        vals = page[:, 256:512].astype(F32).T.astype(BF16)
        kaug = []
        vaug = []
        for h in range(HEADS):
            pair = keys[:, (h // 2) * 128 : (h // 2) * 128 + 128]
            both = (pair, hot) if h % 2 == 0 else (hot, pair)
            kaug.append(jnp.where(low_lanes, both[0], both[1]).astype(BF16))
            vaug.append(jnp.concatenate([vals[h * 64 : (h + 1) * 64, :], ones], axis=0))
        olds = [top[j, h] for h in range(HEADS)]
        scores = {}
        weights = {}
        for i in range(HEADS + 2):
            if i < HEADS:
                s = jnp.dot(kaug[i], qb[j, i], preferred_element_type=F32)
                scores[i] = s + causal[...] if fresh else s
            if 1 <= i <= HEADS:
                k = i - 1
                s = scores.pop(k)
                new = jnp.maximum(olds[k], jnp.max(s, axis=0, keepdims=True))
                weights[k] = (jnp.exp(s - new).astype(BF16), new, jnp.exp(olds[k] - new))
            if i >= 2:
                k = i - 2
                p, new, keep = weights.pop(k)
                top[j, k] = new
                acc[j, k] = acc[j, k] * keep + jnp.dot(vaug[k], p, preferred_element_type=F32)

    def body(slot, carry):
        @pl.when(used[slot] > 0)
        def _():
            visit(slot, owner[slot], False)

        return carry

    lax.fori_loop(0, NY * SLOTS, body, 0)

    def last(j, carry):
        visit(NY * SLOTS + j, j, True)
        return carry

    lax.fori_loop(0, 2, last, 0)

    low64 = lax.broadcasted_iota(jnp.int32, (64, 128), 1) < 64
    low8 = lax.broadcasted_iota(jnp.int32, (8, 128), 1) < 64

    def send(zs, carry):
        lanes = pl.ds(pl.multiple_of(zs * 128, 128), 128)
        for j in range(2):
            values = []
            parts = []
            for h in range(HEADS):
                total = acc[j, h, 64:65, lanes]
                values.append(acc[j, h, 0:64, lanes] * (1.0 / total))
                lse = top[j, h, :, lanes] + jnp.log(total)
                hi = lse.astype(BF16).astype(F32)
                mid = (lse - hi).astype(BF16).astype(F32)
                parts.append(jnp.concatenate([hi, mid, lse - hi - mid], axis=0))
            blank = jnp.zeros((2, 128), F32)
            stat_a = jnp.concatenate([parts[0], parts[1], blank], axis=0)
            stat_b = jnp.concatenate([parts[2], parts[3], blank], axis=0)
            for side_row in range(2):
                p = (2 * j + side_row) * NZ + zs

                def pick(left, right, mask):
                    if side_row == 0:
                        return jnp.where(mask, left, pltpu.roll(right, 64, 1)).astype(BF16)
                    return jnp.where(mask, pltpu.roll(left, 64, 1), right).astype(BF16)

                out[p, 0:64, :] = pick(values[0], values[2], low64)
                out[p, 64:128, :] = pick(values[1], values[3], low64)
                out[p, 128:136, :] = pick(stat_a, stat_b, low8)
        return carry

    lax.fori_loop(0, NZ, send, 0)


def attend(idx, used, owner, bias, q, kv, pieces, app, own_vars, fresh_vars, qvar):
    return pl.pallas_call(
        attn_kernel,
        out_shape=jax.ShapeDtypeStruct((NY * NZ, 136, 128), BF16),
        in_specs=[smem()] * 4 + [vmem()] + [hbm()] * 5 + [vmem()] * 3,
        out_specs=vmem(),
        scratch_shapes=[
            pltpu.VMEM((26 * PAGE, 512), BF16),
            pltpu.VMEM((2, HEADS, 128, 1024), BF16),
            pltpu.VMEM((2, HEADS, 1, 1024), F32),
            pltpu.VMEM((2, HEADS, 80, 1024), F32),
            pltpu.VMEM((3, 16, 128), BF16),
            pltpu.VMEM((26, 1, 128), F32),
            pltpu.VMEM((128, 1024), F32),
            pltpu.SemaphoreType.DMA((9,)),
        ],
        compiler_params=params(56),
    )(idx, used, owner, bias, q, kv, *pieces, app, own_vars, fresh_vars, qvar)


def final_kernel(idx, parts, tokens, late, app_all, gain, hidden_out, logits_out, stats_out, app_out, wo, wh, head_in, sem):
    copies = [
        pltpu.make_async_copy(late.at[:, :, pl.ds(0, 32), :], wo, sem.at[0]),
        pltpu.make_async_copy(late.at[:, :, pl.ds(32, 8), :], wh, sem.at[1]),
    ]
    own = pl.ds(pl.multiple_of(idx[1] * ROWS, ROWS), ROWS)
    for ys in range(NY):
        for half in range(2):
            copies.append(
                pltpu.make_async_copy(
                    app_all.at[ys, own, pl.ds(half * 256, 256)],
                    app_out.at[:, pl.ds(half * 1024 + ys * 256, 256)],
                    sem.at[2 + 2 * ys + half],
                )
            )
    for c in copies:
        c.start()
    chunks = []
    for ys in range(NY):
        lses = [[], []]
        for zs in range(NZ):
            stat = parts[ys * NZ + zs, 128:136, :].astype(F32)
            for k in range(2):
                lses[k].append(stat[3 * k : 3 * k + 1] + stat[3 * k + 1 : 3 * k + 2] + stat[3 * k + 2 : 3 * k + 3])
        merged = []
        for k in range(2):
            best = lses[k][0]
            for v in lses[k][1:]:
                best = jnp.maximum(best, v)
            ws = [jnp.exp(v - best) for v in lses[k]]
            total = ws[0]
            for w in ws[1:]:
                total = total + w
            inverse = 1.0 / total
            value = None
            for zs in range(NZ):
                term = parts[ys * NZ + zs, k * 64 : (k + 1) * 64, :].astype(F32) * (ws[zs] * inverse)
                value = term if value is None else value + term
            merged.append(value)
        turned = jnp.concatenate(merged, axis=0).T.astype(BF16)
        chunks.append(turned[0:64, :])
        chunks.append(turned[64:128, :])
    for c in copies:
        c.wait()
    total = tokens[...].astype(F32)
    for r in range(NR):
        total = total + dot_last(chunks[r], wo[r].reshape(1024, 128))
    hidden = total.astype(BF16)
    hidden_out[...] = hidden
    wide = hidden.astype(F32)
    square = wide * wide
    power = jnp.sum(square, axis=1, keepdims=True)
    head_in[...] = (wide * lax.rsqrt(power * (1.0 / 1024) + EPSILON) * gain[...]).astype(BF16)
    logits = None
    for r in range(NR):
        part = dot_last(head_in[:, r * 128 : (r + 1) * 128], wh[r].reshape(256, 128))
        logits = part if logits is None else logits + part
    logits_out[...] = logits.astype(BF16)
    energy = jnp.sum(power, axis=0, keepdims=True)
    peak = jnp.max(jnp.max(logits, axis=1, keepdims=True), axis=0, keepdims=True)
    row = lax.broadcasted_iota(jnp.int32, (8, 128), 0)
    tile = jnp.where(row == 0, energy, jnp.where(row == 1, peak, 0.0))
    for p in range(NY * NZ):
        stats_out[p * 8 : (p + 1) * 8, :] = tile


def finish(idx, parts, tokens, late, app_all, gain):
    return pl.pallas_call(
        final_kernel,
        out_shape=[
            jax.ShapeDtypeStruct((ROWS, 1024), BF16),
            jax.ShapeDtypeStruct((ROWS, 256), BF16),
            jax.ShapeDtypeStruct((NY * NZ * 8, 128), F32),
            jax.ShapeDtypeStruct((ROWS, 2048), BF16),
        ],
        in_specs=[smem(), vmem(), vmem(), hbm(), hbm(), vmem()],
        out_specs=[vmem()] * 4,
        scratch_shapes=[
            pltpu.VMEM((NR, NY * NZ, 32, 128), BF16),
            pltpu.VMEM((NR, NY * NZ, 8, 128), BF16),
            pltpu.VMEM((ROWS, 1024), BF16),
            pltpu.SemaphoreType.DMA((10,)),
        ],
        compiler_params=params(56),
    )(idx, parts, tokens, late, app_all, gain)


def stats_kernel(stats, norm_out, peak_out):
    half = NY * NZ * 4
    for j in range(2):
        block = stats[j * half : (j + 1) * half, :].reshape(NY * NZ // 2, 8, 128)
        norm_out[j] = jnp.sqrt(jnp.sum(block, axis=0))[0, 0]
        peak_out[j] = jnp.max(block, axis=0)[1, 0]


def gather_stats(stats):
    return pl.pallas_call(
        stats_kernel,
        out_shape=[jax.ShapeDtypeStruct((2,), F32)] * 2,
        in_specs=[vmem()],
        out_specs=[smem()] * 2,
        compiler_params=params(4),
    )(stats)


def slot_table(table_rows, pages_held, slot_ids):
    request_count, page_count = table_rows.shape
    matches = table_rows[:, :, None] == slot_ids[None, None, :]
    live = jnp.arange(page_count, dtype=jnp.int32)[None, :, None] < pages_held[:, None, None]
    hits = jnp.any(matches & live, axis=1)
    used = jnp.any(hits, axis=0).astype(jnp.int32)
    owner = jnp.sum(
        jnp.where(hits, jnp.arange(request_count, dtype=jnp.int32)[:, None], 0), axis=0
    )
    return used, owner


def kv_target(p):
    head = p % 16
    return (head // 4) * NZ + head % 4 + (4 if p >= 16 else 0)


def per_device(
    tokens,
    variate_ids,
    cache_pages,
    page_table,
    kv_cache,
    cache_variates,
    attn_gain,
    w_query,
    w_keyval,
    w_out,
    variate_bias,
    head_gain,
    w_head,
):
    r = lax.axis_index("req")
    y = lax.axis_index("y")
    z = lax.axis_index("z")
    idx = jnp.stack([r, y, z]).astype(jnp.int32)

    kv_cols = lax.ppermute(w_keyval.T, ("y", "z"), [(p, kv_target(p)) for p in range(NY * NZ)])

    kv_rows = kv_cache.reshape(SLOTS * PAGE, 2048)
    wide = tokens.astype(F32)
    power = jnp.mean(wide * wide, axis=-1, keepdims=True)
    own = (wide * lax.rsqrt(power + EPSILON) * attn_gain).astype(BF16)
    opposite = shift("y", NY, 2)(own)
    carved = carve(idx, kv_rows, cache_variates, own)
    carved, opposite, kv_cols = lax.optimization_barrier((carved, opposite, kv_cols))
    pieces = [shift("y", NY, d)(carved[d - 1]) for d in range(1, NY)]

    w_local = jnp.concatenate([w_query.T, kv_cols, w_out.T, w_head.T], axis=0)
    w_z = lax.all_to_all(
        jnp.broadcast_to(w_local[None], (NZ, 136, 128)), "z", 0, 0, tiled=True
    )
    w_z, pieces[0], pieces[2] = lax.optimization_barrier((w_z, pieces[0], pieces[2]))
    w_all = lax.all_to_all(
        jnp.broadcast_to(w_z[None, :, 0:96, :], (NR, NZ, 96, 128)), "req", 0, 0, tiled=True
    )
    late = lax.all_gather(w_z[:, 96:136, :], ("req", "y"), axis=0).reshape(NR, NY * NZ, 40, 128)

    columns = jnp.transpose(variate_ids.reshape(NY, NZ, ROWS), (1, 0, 2)).reshape(NZ, 1, 256)
    fresh_vars = lax.dynamic_index_in_dim(columns, z, 0, keepdims=False).reshape(2, 128)
    order = (y + NY - jnp.arange(NY, dtype=jnp.int32)) % NY
    slot_ids = (
        (order[:, None] * NZ + z) * SLOTS + jnp.arange(SLOTS, dtype=jnp.int32)[None, :]
    ).reshape(-1)
    used, owner = slot_table(page_table, cache_pages, slot_ids)

    lane = jnp.arange(256, dtype=jnp.int32)
    source = lane // ROWS
    positions = (
        jnp.where(source // 2 == 0, cache_pages[0], cache_pages[1]) * PAGE
        + ((source % 2) * NZ + z) * ROWS
        + lane % ROWS
    )
    steps = jnp.arange(32, dtype=F32) / 32
    freqs = jnp.exp(-math.log(10000.0) * steps)
    angle = positions.astype(F32)[None, :] * freqs[:, None]

    q_copies, app = project(
        idx, own, pieces[0], opposite, pieces[2], w_all.reshape(NR, NZ * 96, 128), jnp.cos(angle), jnp.sin(angle)
    )
    app_all = lax.all_gather(app, "y", axis=0)
    q = lax.all_to_all(q_copies, "z", 0, 0, tiled=True)
    q, late = lax.optimization_barrier((q, late))
    sent = attend(
        idx, used, owner, variate_bias, q, kv_rows, pieces, app, cache_variates, fresh_vars, columns
    )
    sent, app_all = lax.optimization_barrier((sent, app_all))
    parts = lax.all_to_all(sent, ("y", "z"), 0, 0, tiled=True)
    hidden, logits, stats, appended = finish(
        idx, parts, tokens, late, app_all, head_gain.reshape(1, -1)
    )
    norm, peak = gather_stats(lax.all_to_all(stats, ("y", "z"), 0, 0, tiled=True))
    return hidden, appended, logits, norm, peak


def solution(mesh):
    grid = Mesh(mesh.devices.reshape(NR, NY, NZ), ("req", "y", "z"))
    every = ("req", "y", "z")
    pg = ("y", "z")
    placed = (
        P(every, None),
        P("req"),
        P("req"),
        P("req", None),
        P(every, None, None),
        P(every, None),
        P(),
        P("req", pg),
        P("req", pg),
        P("req", pg),
        P(),
        P(),
        P("req", pg),
    )
    return jax.shard_map(
        per_device,
        mesh=grid,
        in_specs=placed,
        out_specs=(P(every, None), P(every, None), P(every, None), P("req"), P("req")),
        check_vma=False,
    )
```

```python
import math

import jax
import jax.numpy as jnp
from jax import lax
from jax.experimental import pallas as pl
from jax.experimental.pallas import tpu as pltpu
from jax.sharding import Mesh
from jax.sharding import PartitionSpec as P

PAGE = 128
EPSILON = 1e-05
NEGATIVE = -1e30
NY = 4
NZ = 8
NR = 8
SLOTS = 6
ROWS = 64
HEADS = 4
DH = 64
F32 = jnp.float32
BF16 = jnp.bfloat16


def shift(axis, size, step):
    return lambda value: lax.ppermute(
        value, axis, [(i, (i + step) % size) for i in range(size)]
    )


def vmem():
    return pl.BlockSpec(memory_space=pltpu.VMEM)


def smem():
    return pl.BlockSpec(memory_space=pltpu.SMEM)


def hbm():
    return pl.BlockSpec(memory_space=pltpu.HBM)


def params(mib):
    return pltpu.CompilerParams(vmem_limit_bytes=mib * 1024 * 1024)


def dot_last(a, b):
    return lax.dot_general(a, b, (((1,), (1,)), ((), ())), preferred_element_type=F32)


def carve_kernel(idx, kv, variates, *refs):
    outs = refs[0:3]
    side, sem = refs[3:5]
    y = idx[1]
    rows = SLOTS * PAGE
    side[...] = jnp.zeros(side.shape, BF16)
    side[0:8, 0:128] = jnp.concatenate(
        [variates[...].astype(F32), jnp.zeros((2, 128), F32)], axis=0
    ).astype(BF16)
    copies = []
    for d in range(1, NY):
        yd = lax.rem(y + d, NY)
        for half in range(2):
            low = pl.multiple_of(half * 1024 + yd * 256, 256)
            copies.append(
                pltpu.make_async_copy(
                    kv.at[:, pl.ds(low, 256)],
                    outs[d - 1].at[pl.ds(0, rows), pl.ds(half * 256, 256)],
                    sem.at[2 * d - 2 + half],
                )
            )
    for c in copies:
        c.start()
    for d in range(1, NY):
        outs[d - 1][rows : rows + 16, :] = side[...]
    for c in copies:
        c.wait()


def carve(idx, kv, variates):
    return pl.pallas_call(
        carve_kernel,
        out_shape=[jax.ShapeDtypeStruct((SLOTS * PAGE + 16, 512), BF16)] * 3,
        in_specs=[smem(), hbm(), vmem()],
        out_specs=[vmem()] * 3,
        scratch_shapes=[pltpu.VMEM((16, 512), BF16), pltpu.SemaphoreType.DMA((6,))],
        compiler_params=params(56),
    )(idx, kv, variates)


def qkv_kernel(idx, t0, t1, t2, t3, w_hbm, cos_ref, sin_ref, q_out, app_out, tok, w, acc, feats, sem):
    y = idx[1]
    copies = []
    for d, rows in enumerate((t0, t1, t2, t3)):
        low = pl.multiple_of(lax.rem(y + NY - d, NY) * ROWS, ROWS)
        copies.append(pltpu.make_async_copy(rows, tok.at[pl.ds(low, ROWS)], sem.at[NR + d]))
    blocks = [pltpu.make_async_copy(w_hbm.at[r], w.at[r], sem.at[r]) for r in range(NR)]
    for c in copies + blocks:
        c.start()
    for c in copies:
        c.wait()
    for r in range(NR):
        blocks[r].wait()
        part = dot_last(w[r], tok[:, r * 128 : (r + 1) * 128])
        if r == 0:
            acc[...] = part
        else:
            acc[...] += part
    cos = cos_ref[...]
    sin = sin_ref[...]

    def rounded(zs, low, high):
        return acc[zs * 96 + low : zs * 96 + high, :].astype(BF16).astype(F32)

    for h in range(HEADS):
        a = rounded(2 * h, 0, 32)
        b = rounded(2 * h + 1, 0, 32)
        first = ((a * cos - b * sin).astype(BF16).astype(F32) * 0.125).astype(BF16)
        second = ((b * cos + a * sin).astype(BF16).astype(F32) * 0.125).astype(BF16)
        for zs in range(NZ):
            q_out[zs, h * 64 : h * 64 + 32, :] = first
            q_out[zs, h * 64 + 32 : h * 64 + 64, :] = second
        a = rounded(h, 32, 64)
        b = rounded(h, 64, 96)
        feats[h * 64 : h * 64 + 32, :] = a * cos - b * sin
        feats[h * 64 + 32 : h * 64 + 64, :] = b * cos + a * sin
        feats[256 + h * 64 : 256 + h * 64 + 64, :] = acc[(HEADS + h) * 96 + 32 : (HEADS + h) * 96 + 96, :]
    app_out[:, 0:256] = feats[0:256, :].T.astype(BF16)
    app_out[:, 256:512] = feats[256:512, :].T.astype(BF16)


def project(idx, toks, w, cos, sin):
    return pl.pallas_call(
        qkv_kernel,
        out_shape=[
            jax.ShapeDtypeStruct((NZ, 256, 256), BF16),
            jax.ShapeDtypeStruct((256, 512), BF16),
        ],
        in_specs=[smem()] + [hbm()] * 5 + [vmem()] * 2,
        out_specs=[vmem()] * 2,
        scratch_shapes=[
            pltpu.VMEM((256, 1024), BF16),
            pltpu.VMEM((NR, NZ * 96, 128), BF16),
            pltpu.VMEM((NZ * 96, 256), F32),
            pltpu.VMEM((512, 256), F32),
            pltpu.SemaphoreType.DMA((NR + 4,)),
        ],
        compiler_params=params(56),
    )(idx, *toks, w, cos, sin)


def attn_kernel(idx, used, owner, bias, *refs):
    q, kv, p1, p2, p3, app, own_vars, fresh_vars, qvar = refs[0:9]
    out = refs[9]
    pg, qb, top, acc, side, kvs, causal, sem = refs[10:18]
    y, z = idx[1], idx[2]
    rows = SLOTS * PAGE
    copies = []
    for half in range(2):
        low = pl.multiple_of(half * 1024 + y * 256, 256)
        copies.append(
            pltpu.make_async_copy(
                kv.at[:, pl.ds(low, 256)],
                pg.at[pl.ds(0, rows), pl.ds(half * 256, 256)],
                sem.at[half],
            )
        )
    for d, piece in enumerate((p1, p2, p3)):
        copies.append(
            pltpu.make_async_copy(
                piece.at[pl.ds(0, rows)], pg.at[pl.ds((d + 1) * rows, rows)], sem.at[2 + d]
            )
        )
        copies.append(
            pltpu.make_async_copy(
                piece.at[pl.ds(rows, 16), pl.ds(0, 128)], side.at[d], sem.at[5 + d]
            )
        )
    copies.append(pltpu.make_async_copy(app, pg.at[pl.ds(NY * rows, 256)], sem.at[8]))
    for c in copies:
        c.start()

    row16 = lax.broadcasted_iota(jnp.int32, (16, 128), 0)
    vsel = row16 & 3
    level = row16 >> 2
    zero = jnp.zeros((48, 128), BF16)

    def fill(zs, carry):
        lanes = pl.ds(pl.multiple_of(zs * 128, 128), 128)
        qv_row = qvar[zs]
        for j in range(2):
            same = jnp.broadcast_to(qv_row[:, j * 128 : (j + 1) * 128], (16, 128)) == vsel
            for h in range(HEADS):
                hh = y * HEADS + h
                b = jnp.where(same, bias[0, hh], bias[1, hh])
                hi = b.astype(BF16).astype(F32)
                mid = (b - hi).astype(BF16).astype(F32)
                lo = (b - hi - mid).astype(BF16).astype(F32)
                extra = jnp.where(
                    level == 0, hi, jnp.where(level == 1, mid, jnp.where(level == 2, lo, 0.0))
                ).astype(BF16)
                q_rows = q[zs, h * 64 : (h + 1) * 64, j * 128 : (j + 1) * 128]
                if h % 2 == 0:
                    qb[j, h, 0:64, lanes] = q_rows
                    qb[j, h, 64:80, lanes] = extra
                    qb[j, h, 80:128, lanes] = zero
                else:
                    qb[j, h, 0:16, lanes] = extra
                    qb[j, h, 16:64, lanes] = zero
                    qb[j, h, 64:128, lanes] = q_rows
        key_row = lax.broadcasted_iota(jnp.int32, (128, 128), 0)
        q_lane = lax.broadcasted_iota(jnp.int32, (128, 128), 1)
        key_pos = ((key_row >> 6) * NZ + z) * ROWS + (key_row & 63)
        q_pos = ((q_lane >> 6) * NZ + zs) * ROWS + (q_lane & 63)
        causal[:, lanes] = jnp.where(key_pos <= q_pos, 0.0, NEGATIVE)
        return carry

    lax.fori_loop(0, NZ, fill, 0)
    top[...] = jnp.full(top.shape, NEGATIVE, F32)
    acc[...] = jnp.zeros(acc.shape, F32)
    for s in range(SLOTS):
        kvs[s] = own_vars[s : s + 1, :].astype(F32)
    for j in range(2):
        kvs[NY * SLOTS + j] = fresh_vars[j : j + 1, :].astype(F32)
    for c in copies:
        c.wait()
    for d in range(3):
        block = side[d].astype(F32)
        for s in range(SLOTS):
            kvs[(d + 1) * SLOTS + s] = block[s : s + 1, :]

    sub = lax.broadcasted_iota(jnp.int32, (128, 128), 0)
    variate = (sub & 3).astype(F32)
    hot_rows = (sub & 63) < 12
    low_lanes = lax.broadcasted_iota(jnp.int32, (128, 128), 1) < 64
    ones = jnp.ones((16, 128), BF16)

    def visit(slot, j, fresh):
        page = pg[pl.ds(pl.multiple_of(slot * PAGE, PAGE), PAGE), :]
        kvals = jnp.broadcast_to(kvs[slot], (128, 128))
        hot = jnp.where(hot_rows & (variate == kvals), 1.0, 0.0).T
        keys = page[:, 0:256].astype(F32)
        vals = page[:, 256:512].astype(F32).T.astype(BF16)
        kaug = []
        vaug = []
        for h in range(HEADS):
            pair = keys[:, (h // 2) * 128 : (h // 2) * 128 + 128]
            both = (pair, hot) if h % 2 == 0 else (hot, pair)
            kaug.append(jnp.where(low_lanes, both[0], both[1]).astype(BF16))
            vaug.append(jnp.concatenate([vals[h * 64 : (h + 1) * 64, :], ones], axis=0))
        olds = [top[j, h] for h in range(HEADS)]
        scores = {}
        weights = {}
        for i in range(HEADS + 2):
            if i < HEADS:
                s = jnp.dot(kaug[i], qb[j, i], preferred_element_type=F32)
                scores[i] = s + causal[...] if fresh else s
            if 1 <= i <= HEADS:
                k = i - 1
                s = scores.pop(k)
                new = jnp.maximum(olds[k], jnp.max(s, axis=0, keepdims=True))
                weights[k] = (jnp.exp(s - new).astype(BF16), new, jnp.exp(olds[k] - new))
            if i >= 2:
                k = i - 2
                p, new, keep = weights.pop(k)
                top[j, k] = new
                acc[j, k] = acc[j, k] * keep + jnp.dot(vaug[k], p, preferred_element_type=F32)

    def body(slot, carry):
        @pl.when(used[slot] > 0)
        def _():
            visit(slot, owner[slot], False)

        return carry

    lax.fori_loop(0, NY * SLOTS, body, 0)

    def last(j, carry):
        visit(NY * SLOTS + j, j, True)
        return carry

    lax.fori_loop(0, 2, last, 0)

    low64 = lax.broadcasted_iota(jnp.int32, (64, 128), 1) < 64
    low8 = lax.broadcasted_iota(jnp.int32, (8, 128), 1) < 64

    def send(zs, carry):
        lanes = pl.ds(pl.multiple_of(zs * 128, 128), 128)
        for j in range(2):
            values = []
            parts = []
            for h in range(HEADS):
                total = acc[j, h, 64:65, lanes]
                values.append(acc[j, h, 0:64, lanes] * (1.0 / total))
                lse = top[j, h, :, lanes] + jnp.log(total)
                hi = lse.astype(BF16).astype(F32)
                mid = (lse - hi).astype(BF16).astype(F32)
                parts.append(jnp.concatenate([hi, mid, lse - hi - mid], axis=0))
            blank = jnp.zeros((2, 128), F32)
            stat_a = jnp.concatenate([parts[0], parts[1], blank], axis=0)
            stat_b = jnp.concatenate([parts[2], parts[3], blank], axis=0)
            for side_row in range(2):
                p = (2 * j + side_row) * NZ + zs

                def pick(left, right, mask):
                    if side_row == 0:
                        return jnp.where(mask, left, pltpu.roll(right, 64, 1)).astype(BF16)
                    return jnp.where(mask, pltpu.roll(left, 64, 1), right).astype(BF16)

                out[p, 0:64, :] = pick(values[0], values[2], low64)
                out[p, 64:128, :] = pick(values[1], values[3], low64)
                out[p, 128:136, :] = pick(stat_a, stat_b, low8)
        return carry

    lax.fori_loop(0, NZ, send, 0)


def attend(idx, used, owner, bias, q, kv, pieces, app, own_vars, fresh_vars, qvar):
    return pl.pallas_call(
        attn_kernel,
        out_shape=jax.ShapeDtypeStruct((NY * NZ, 136, 128), BF16),
        in_specs=[smem()] * 4 + [vmem()] + [hbm()] * 5 + [vmem()] * 3,
        out_specs=vmem(),
        scratch_shapes=[
            pltpu.VMEM((26 * PAGE, 512), BF16),
            pltpu.VMEM((2, HEADS, 128, 1024), BF16),
            pltpu.VMEM((2, HEADS, 1, 1024), F32),
            pltpu.VMEM((2, HEADS, 80, 1024), F32),
            pltpu.VMEM((3, 16, 128), BF16),
            pltpu.VMEM((26, 1, 128), F32),
            pltpu.VMEM((128, 1024), F32),
            pltpu.SemaphoreType.DMA((9,)),
        ],
        compiler_params=params(56),
    )(idx, used, owner, bias, q, kv, *pieces, app, own_vars, fresh_vars, qvar)


def final_kernel(idx, parts, tokens, late, app_all, gain, hidden_out, logits_out, stats_out, app_out, wo, wh, head_in, sem):
    copies = [
        pltpu.make_async_copy(late.at[:, :, pl.ds(0, 32), :], wo, sem.at[0]),
        pltpu.make_async_copy(late.at[:, :, pl.ds(32, 8), :], wh, sem.at[1]),
    ]
    own = pl.ds(pl.multiple_of(idx[1] * ROWS, ROWS), ROWS)
    for ys in range(NY):
        for half in range(2):
            copies.append(
                pltpu.make_async_copy(
                    app_all.at[ys, own, pl.ds(half * 256, 256)],
                    app_out.at[:, pl.ds(half * 1024 + ys * 256, 256)],
                    sem.at[2 + 2 * ys + half],
                )
            )
    for c in copies:
        c.start()
    chunks = []
    for ys in range(NY):
        lses = [[], []]
        for zs in range(NZ):
            stat = parts[ys * NZ + zs, 128:136, :].astype(F32)
            for k in range(2):
                lses[k].append(stat[3 * k : 3 * k + 1] + stat[3 * k + 1 : 3 * k + 2] + stat[3 * k + 2 : 3 * k + 3])
        merged = []
        for k in range(2):
            best = lses[k][0]
            for v in lses[k][1:]:
                best = jnp.maximum(best, v)
            ws = [jnp.exp(v - best) for v in lses[k]]
            total = ws[0]
            for w in ws[1:]:
                total = total + w
            inverse = 1.0 / total
            value = None
            for zs in range(NZ):
                term = parts[ys * NZ + zs, k * 64 : (k + 1) * 64, :].astype(F32) * (ws[zs] * inverse)
                value = term if value is None else value + term
            merged.append(value)
        turned = jnp.concatenate(merged, axis=0).T.astype(BF16)
        chunks.append(turned[0:64, :])
        chunks.append(turned[64:128, :])
    for c in copies:
        c.wait()
    total = tokens[...].astype(F32)
    for r in range(NR):
        total = total + dot_last(chunks[r], wo[r].reshape(1024, 128))
    hidden = total.astype(BF16)
    hidden_out[...] = hidden
    wide = hidden.astype(F32)
    square = wide * wide
    power = jnp.sum(square, axis=1, keepdims=True)
    head_in[...] = (wide * lax.rsqrt(power * (1.0 / 1024) + EPSILON) * gain[...]).astype(BF16)
    logits = None
    for r in range(NR):
        part = dot_last(head_in[:, r * 128 : (r + 1) * 128], wh[r].reshape(256, 128))
        logits = part if logits is None else logits + part
    logits_out[...] = logits.astype(BF16)
    energy = jnp.sum(power, axis=0, keepdims=True)
    peak = jnp.max(jnp.max(logits, axis=1, keepdims=True), axis=0, keepdims=True)
    row = lax.broadcasted_iota(jnp.int32, (8, 128), 0)
    tile = jnp.where(row == 0, energy, jnp.where(row == 1, peak, 0.0))
    for p in range(NY * NZ):
        stats_out[p * 8 : (p + 1) * 8, :] = tile


def finish(idx, parts, tokens, late, app_all, gain):
    return pl.pallas_call(
        final_kernel,
        out_shape=[
            jax.ShapeDtypeStruct((ROWS, 1024), BF16),
            jax.ShapeDtypeStruct((ROWS, 256), BF16),
            jax.ShapeDtypeStruct((NY * NZ * 8, 128), F32),
            jax.ShapeDtypeStruct((ROWS, 2048), BF16),
        ],
        in_specs=[smem(), vmem(), vmem(), hbm(), hbm(), vmem()],
        out_specs=[vmem()] * 4,
        scratch_shapes=[
            pltpu.VMEM((NR, NY * NZ, 32, 128), BF16),
            pltpu.VMEM((NR, NY * NZ, 8, 128), BF16),
            pltpu.VMEM((ROWS, 1024), BF16),
            pltpu.SemaphoreType.DMA((10,)),
        ],
        compiler_params=params(56),
    )(idx, parts, tokens, late, app_all, gain)


def stats_kernel(stats, norm_out, peak_out):
    half = NY * NZ * 4
    for j in range(2):
        block = stats[j * half : (j + 1) * half, :].reshape(NY * NZ // 2, 8, 128)
        norm_out[j] = jnp.sqrt(jnp.sum(block, axis=0))[0, 0]
        peak_out[j] = jnp.max(block, axis=0)[1, 0]


def gather_stats(stats):
    return pl.pallas_call(
        stats_kernel,
        out_shape=[jax.ShapeDtypeStruct((2,), F32)] * 2,
        in_specs=[vmem()],
        out_specs=[smem()] * 2,
        compiler_params=params(4),
    )(stats)


def slot_table(table_rows, pages_held, slot_ids):
    request_count, page_count = table_rows.shape
    matches = table_rows[:, :, None] == slot_ids[None, None, :]
    live = jnp.arange(page_count, dtype=jnp.int32)[None, :, None] < pages_held[:, None, None]
    hits = jnp.any(matches & live, axis=1)
    used = jnp.any(hits, axis=0).astype(jnp.int32)
    owner = jnp.sum(
        jnp.where(hits, jnp.arange(request_count, dtype=jnp.int32)[:, None], 0), axis=0
    )
    return used, owner


def kv_target(p):
    head = p % 16
    return (head // 4) * NZ + head % 4 + (4 if p >= 16 else 0)


def per_device(
    tokens,
    variate_ids,
    cache_pages,
    page_table,
    kv_cache,
    cache_variates,
    attn_gain,
    w_query,
    w_keyval,
    w_out,
    variate_bias,
    head_gain,
    w_head,
):
    r = lax.axis_index("req")
    y = lax.axis_index("y")
    z = lax.axis_index("z")
    idx = jnp.stack([r, y, z]).astype(jnp.int32)

    kv_cols = lax.ppermute(w_keyval.T, ("y", "z"), [(p, kv_target(p)) for p in range(NY * NZ)])

    kv_rows = kv_cache.reshape(SLOTS * PAGE, 2048)
    wide = tokens.astype(F32)
    power = jnp.mean(wide * wide, axis=-1, keepdims=True)
    own = (wide * lax.rsqrt(power + EPSILON) * attn_gain).astype(BF16)
    toks = [own] + [shift("y", NY, d)(own) for d in range(1, NY)]
    carved = carve(idx, kv_rows, cache_variates)
    toks, kv_cols = lax.optimization_barrier((toks, kv_cols))
    pieces = [shift("y", NY, d)(carved[d - 1]) for d in range(1, NY)]

    w_local = jnp.concatenate([w_query.T, kv_cols, w_out.T, w_head.T], axis=0)
    w_z = lax.all_to_all(
        jnp.broadcast_to(w_local[None], (NZ, 136, 128)), "z", 0, 0, tiled=True
    )
    w_all = lax.all_to_all(
        jnp.broadcast_to(w_z[None, :, 0:96, :], (NR, NZ, 96, 128)), "req", 0, 0, tiled=True
    )

    toks[0], pieces[0] = lax.optimization_barrier((toks[0], pieces[0]))
    late = lax.all_gather(w_z[:, 96:136, :], ("req", "y"), axis=0).reshape(NR, NY * NZ, 40, 128)
    columns = jnp.transpose(variate_ids.reshape(NY, NZ, ROWS), (1, 0, 2)).reshape(NZ, 1, 256)
    fresh_vars = lax.dynamic_index_in_dim(columns, z, 0, keepdims=False).reshape(2, 128)
    order = (y + NY - jnp.arange(NY, dtype=jnp.int32)) % NY
    slot_ids = (
        (order[:, None] * NZ + z) * SLOTS + jnp.arange(SLOTS, dtype=jnp.int32)[None, :]
    ).reshape(-1)
    used, owner = slot_table(page_table, cache_pages, slot_ids)

    lane = jnp.arange(256, dtype=jnp.int32)
    source = lane // ROWS
    positions = (
        jnp.where(source // 2 == 0, cache_pages[0], cache_pages[1]) * PAGE
        + ((source % 2) * NZ + z) * ROWS
        + lane % ROWS
    )
    steps = jnp.arange(32, dtype=F32) / 32
    freqs = jnp.exp(-math.log(10000.0) * steps)
    angle = positions.astype(F32)[None, :] * freqs[:, None]

    q_copies, app = project(
        idx, toks, w_all.reshape(NR, NZ * 96, 128), jnp.cos(angle), jnp.sin(angle)
    )
    app_all = lax.all_gather(app, "y", axis=0)
    q = lax.all_to_all(q_copies, "z", 0, 0, tiled=True)
    q, late = lax.optimization_barrier((q, late))
    sent = attend(
        idx, used, owner, variate_bias, q, kv_rows, pieces, app, cache_variates, fresh_vars, columns
    )
    sent, app_all = lax.optimization_barrier((sent, app_all))
    parts = lax.all_to_all(sent, ("y", "z"), 0, 0, tiled=True)
    hidden, logits, stats, appended = finish(
        idx, parts, tokens, late, app_all, head_gain.reshape(1, -1)
    )
    norm, peak = gather_stats(lax.all_to_all(stats, ("y", "z"), 0, 0, tiled=True))
    return hidden, appended, logits, norm, peak


def solution(mesh):
    grid = Mesh(mesh.devices.reshape(NR, NY, NZ), ("req", "y", "z"))
    every = ("req", "y", "z")
    pg = ("y", "z")
    placed = (
        P(every, None),
        P("req"),
        P("req"),
        P("req", None),
        P(every, None, None),
        P(every, None),
        P(),
        P("req", pg),
        P("req", pg),
        P("req", pg),
        P(),
        P(),
        P("req", pg),
    )
    return jax.shard_map(
        per_device,
        mesh=grid,
        in_specs=placed,
        out_specs=(P(every, None), P(every, None), P(every, None), P("req"), P("req")),
        check_vma=False,
    )
```

```python
import functools
import math

import jax
import jax.numpy as jnp
from jax import lax
from jax.experimental import pallas as pl
from jax.experimental.pallas import tpu as pltpu
from jax.sharding import Mesh
from jax.sharding import PartitionSpec as P

PAGE = 128
EPSILON = 1e-05
NEGATIVE = -1e30
NY = 4
NZ = 8
NR = 8
SLOTS = 6
ROWS = 64
HEADS = 2
PIECE = SLOTS * 128 + 16 + 2 * ROWS
DH = 64
F32 = jnp.float32
BF16 = jnp.bfloat16


def shift(axis, size, step):
    return lambda value: lax.ppermute(
        value, axis, [(i, (i + step) % size) for i in range(size)]
    )


def vmem():
    return pl.BlockSpec(memory_space=pltpu.VMEM)


def smem():
    return pl.BlockSpec(memory_space=pltpu.SMEM)


def hbm():
    return pl.BlockSpec(memory_space=pltpu.HBM)


def params(mib):
    return pltpu.CompilerParams(vmem_limit_bytes=mib * 1024 * 1024)


def dot_last(a, b):
    return lax.dot_general(a, b, (((1,), (1,)), ((), ())), preferred_element_type=F32)


def carve_kernel(idx, kv, variates, tokens, gain, *refs):
    outs = refs[0:3]
    own = refs[3]
    side, sem = refs[4:6]
    y = idx[1]
    rows = SLOTS * PAGE
    side[...] = jnp.zeros(side.shape, BF16)
    side[0:8, 0:128] = jnp.concatenate(
        [variates[...].astype(F32), jnp.zeros((2, 128), F32)], axis=0
    ).astype(BF16)
    copies = []
    for d in range(1, NY):
        yd = lax.rem(y + d, NY)
        for half in range(2):
            low = pl.multiple_of(half * 1024 + yd * 256, 256)
            copies.append(
                pltpu.make_async_copy(
                    kv.at[:, pl.ds(low, 256)],
                    outs[d - 1].at[pl.ds(0, rows), pl.ds(half * 256, 256)],
                    sem.at[2 * d - 2 + half],
                )
            )
    for c in copies:
        c.start()
    wide = tokens[...].astype(F32)
    power = jnp.sum(wide * wide, axis=1, keepdims=True) * (1.0 / 1024)
    normed = (wide * lax.rsqrt(power + EPSILON) * gain[...]).astype(BF16)
    own[...] = normed
    for d in range(1, NY):
        outs[d - 1][rows : rows + 16, :] = side[...]
        if d != 2:
            outs[d - 1][rows + 16 : rows + 80, :] = normed[:, 0:512]
            outs[d - 1][rows + 80 : rows + 144, :] = normed[:, 512:1024]
    for c in copies:
        c.wait()


def carve(idx, kv, variates, tokens, gain):
    return pl.pallas_call(
        carve_kernel,
        out_shape=[
            jax.ShapeDtypeStruct((PIECE if d != 2 else SLOTS * PAGE + 16, 512), BF16)
            for d in range(1, NY)
        ]
        + [jax.ShapeDtypeStruct((ROWS, 1024), BF16)],
        in_specs=[smem(), hbm()] + [vmem()] * 3,
        out_specs=[vmem()] * 4,
        scratch_shapes=[pltpu.VMEM((16, 512), BF16), pltpu.SemaphoreType.DMA((6,))],
        compiler_params=params(56),
    )(idx, kv, variates, tokens, gain)


def qkv_kernel(idx, own, p1, opposite, p3, w_hbm, cos_ref, sin_ref, q_first, q_second, app_out, tok, w, acc, feats, sem):
    y = idx[1]
    base = SLOTS * PAGE + 16
    copies = [
        pltpu.make_async_copy(
            own, tok.at[pl.ds(pl.multiple_of(y * ROWS, ROWS), ROWS), :], sem.at[NR]
        ),
        pltpu.make_async_copy(
            opposite,
            tok.at[pl.ds(pl.multiple_of(lax.rem(y + 2, NY) * ROWS, ROWS), ROWS), :],
            sem.at[NR + 3],
        ),
    ]
    for d, piece in ((0, p1), (2, p3)):
        ys = lax.rem(y + NY - d - 1, NY)
        for half in range(2):
            copies.append(
                pltpu.make_async_copy(
                    piece.at[pl.ds(base + half * ROWS, ROWS)],
                    tok.at[
                        pl.ds(pl.multiple_of(ys * ROWS, ROWS), ROWS), pl.ds(half * 512, 512)
                    ],
                    sem.at[NR + 1 + 2 * d + half],
                )
            )
    blocks = [pltpu.make_async_copy(w_hbm.at[r], w.at[r], sem.at[r]) for r in range(NR)]
    for c in copies + blocks:
        c.start()
    for c in copies:
        c.wait()
    for r in range(NR):
        blocks[r].wait()
        part = dot_last(w[r], tok[:, r * 128 : (r + 1) * 128])
        if r == 0:
            acc[...] = part
        else:
            acc[...] += part
    cos = cos_ref[...]
    sin = sin_ref[...]

    def rounded(zs, low, high):
        return acc[zs * 96 + low : zs * 96 + high, :].astype(BF16).astype(F32)

    for h in range(4):
        a = rounded(2 * h, 0, 32)
        b = rounded(2 * h + 1, 0, 32)
        first = ((a * cos - b * sin).astype(BF16).astype(F32) * 0.125).astype(BF16)
        second = ((b * cos + a * sin).astype(BF16).astype(F32) * 0.125).astype(BF16)
        q_out = q_first if h < 2 else q_second
        low = (h % 2) * 64
        for zs in range(NZ):
            q_out[zs, low : low + 32, :] = first
            q_out[zs, low + 32 : low + 64, :] = second
        a = rounded(h, 32, 64)
        b = rounded(h, 64, 96)
        feats[h * 64 : h * 64 + 32, :] = a * cos - b * sin
        feats[h * 64 + 32 : h * 64 + 64, :] = b * cos + a * sin
        feats[256 + h * 64 : 256 + h * 64 + 64, :] = acc[(4 + h) * 96 + 32 : (4 + h) * 96 + 96, :]
    app_out[:, 0:256] = feats[0:256, :].T.astype(BF16)
    app_out[:, 256:512] = feats[256:512, :].T.astype(BF16)


def project(idx, own, p1, opposite, p3, w, cos, sin):
    return pl.pallas_call(
        qkv_kernel,
        out_shape=[
            jax.ShapeDtypeStruct((NZ, 128, 256), BF16),
            jax.ShapeDtypeStruct((NZ, 128, 256), BF16),
            jax.ShapeDtypeStruct((256, 512), BF16),
        ],
        in_specs=[smem()] + [hbm()] * 5 + [vmem()] * 2,
        out_specs=[vmem()] * 3,
        scratch_shapes=[
            pltpu.VMEM((256, 1024), BF16),
            pltpu.VMEM((NR, NZ * 96, 128), BF16),
            pltpu.VMEM((NZ * 96, 256), F32),
            pltpu.VMEM((512, 256), F32),
            pltpu.SemaphoreType.DMA((NR + 7,)),
        ],
        compiler_params=params(56),
    )(idx, own, p1, opposite, p3, w, cos, sin)


def attn_kernel(half, idx, used, owner, bias, *refs):
    q, kv, p1, p2, p3, app, own_vars, fresh_vars, qvar = refs[0:9]
    out = refs[9]
    pg, qb, top, acc, side, kvs, causal, order, sem = refs[10:19]
    y, z = idx[1], idx[2]
    rows = SLOTS * PAGE
    fresh_base = NY * SLOTS
    copies = []

    def fetch(source, target):
        copies.append(pltpu.make_async_copy(source, target, sem.at[len(copies)]))

    for side_col in range(2):
        cols = pl.ds(side_col * 128, 128)
        low = pl.multiple_of(side_col * 1024 + y * 256 + half * 128, 128)
        fetch(kv.at[:, pl.ds(low, 128)], pg.at[pl.ds(0, rows), cols])
        source_cols = pl.ds(side_col * 256 + half * 128, 128)
        for d, piece in enumerate((p1, p2, p3)):
            fetch(
                piece.at[pl.ds(0, rows), source_cols], pg.at[pl.ds((d + 1) * rows, rows), cols]
            )
        fetch(app.at[:, source_cols], pg.at[pl.ds(NY * rows, 256), cols])
    for d, piece in enumerate((p1, p2, p3)):
        fetch(piece.at[pl.ds(rows, 16), pl.ds(0, 128)], side.at[d])
    for c in copies:
        c.start()

    def collect(slot, count):
        order[count] = slot
        return count + used[slot]

    count = lax.fori_loop(0, fresh_base, collect, 0)

    row16 = lax.broadcasted_iota(jnp.int32, (16, 128), 0)
    vsel = row16 & 3
    level = row16 >> 2
    zero = jnp.zeros((48, 128), BF16)

    def fill(zs, carry):
        lanes = pl.ds(pl.multiple_of(zs * 128, 128), 128)
        qv_row = qvar[zs]
        for j in range(2):
            same = jnp.broadcast_to(qv_row[:, j * 128 : (j + 1) * 128], (16, 128)) == vsel
            for h in range(HEADS):
                hh = y * 4 + half * 2 + h
                b = jnp.where(same, bias[0, hh], bias[1, hh])
                hi = b.astype(BF16).astype(F32)
                mid = (b - hi).astype(BF16).astype(F32)
                lo = (b - hi - mid).astype(BF16).astype(F32)
                extra = jnp.where(
                    level == 0, hi, jnp.where(level == 1, mid, jnp.where(level == 2, lo, 0.0))
                ).astype(BF16)
                q_rows = q[zs, h * 64 : (h + 1) * 64, j * 128 : (j + 1) * 128]
                if h % 2 == 0:
                    qb[j, h, 0:64, lanes] = q_rows
                    qb[j, h, 64:80, lanes] = extra
                    qb[j, h, 80:128, lanes] = zero
                else:
                    qb[j, h, 0:16, lanes] = extra
                    qb[j, h, 16:64, lanes] = zero
                    qb[j, h, 64:128, lanes] = q_rows
        key_row = lax.broadcasted_iota(jnp.int32, (128, 128), 0)
        q_lane = lax.broadcasted_iota(jnp.int32, (128, 128), 1)
        key_pos = ((key_row >> 6) * NZ + z) * ROWS + (key_row & 63)
        q_pos = ((q_lane >> 6) * NZ + zs) * ROWS + (q_lane & 63)
        causal[:, lanes] = jnp.where(key_pos <= q_pos, 0.0, NEGATIVE)
        return carry

    lax.fori_loop(0, NZ, fill, 0)
    top[...] = jnp.full(top.shape, NEGATIVE, F32)
    acc[...] = jnp.zeros(acc.shape, F32)
    for s in range(SLOTS):
        kvs[s] = own_vars[s : s + 1, :].astype(F32)
    for j in range(2):
        kvs[NY * SLOTS + j] = fresh_vars[j : j + 1, :].astype(F32)
    for c in copies:
        c.wait()
    for d in range(3):
        block = side[d].astype(F32)
        for s in range(SLOTS):
            kvs[(d + 1) * SLOTS + s] = block[s : s + 1, :]

    sub = lax.broadcasted_iota(jnp.int32, (128, 128), 0)
    variate = (sub & 3).astype(F32)
    hot_rows = (sub & 63) < 12
    low_lanes = lax.broadcasted_iota(jnp.int32, (128, 128), 1) < 64
    ones = jnp.ones((16, 128), BF16)

    def visit(slots, js, fresh):
        tiles = []
        for n, slot in enumerate(slots):
            page = pg[pl.ds(pl.multiple_of(slot * PAGE, PAGE), PAGE), :]
            kvals = jnp.broadcast_to(kvs[slot], (128, 128))
            hot = jnp.where(hot_rows & (variate == kvals), 1.0, 0.0).T
            pair = page[:, 0:128].astype(F32)
            vals = page[:, 128:256].astype(F32).T.astype(BF16)
            for h in range(HEADS):
                both = (pair, hot) if h == 0 else (hot, pair)
                kaug = jnp.where(low_lanes, both[0], both[1]).astype(BF16)
                vaug = jnp.concatenate([vals[h * 64 : (h + 1) * 64, :], ones], axis=0)
                tiles.append((n, js[n], h, kaug, vaug))
        total = len(tiles)
        scores = {}
        weights = {}
        for i in range(total + 2):
            if i < total:
                n, j, h, kaug, _ = tiles[i]
                s = jnp.dot(kaug, qb[j, h], preferred_element_type=F32)
                scores[i] = s + causal[...] if fresh else s
            if 1 <= i <= total:
                n, j, h, _, _ = tiles[i - 1]
                s = scores.pop(i - 1)
                old = top[j, h]
                new = jnp.maximum(old, jnp.max(s, axis=0, keepdims=True))
                top[j, h] = new
                weights[i - 1] = (jnp.exp(s - new).astype(BF16), jnp.exp(old - new))
            if i >= 2:
                n, j, h, _, vaug = tiles[i - 2]
                p, keep = weights.pop(i - 2)
                acc[j, h] = acc[j, h] * keep + jnp.dot(vaug, p, preferred_element_type=F32)

    def body(i, carry):
        a = order[2 * i]
        b = order[2 * i + 1]
        visit([a, b], [owner[a], owner[b]], False)
        return carry

    lax.fori_loop(0, count // 2, body, 0)

    @pl.when(count % 2 == 1)
    def _():
        a = order[count - 1]
        visit([a], [owner[a]], False)

    visit([fresh_base, fresh_base + 1], [0, 1], True)

    low64 = lax.broadcasted_iota(jnp.int32, (64, 128), 1) < 64
    low8 = lax.broadcasted_iota(jnp.int32, (8, 128), 1) < 64

    def send(zs, carry):
        lanes = pl.ds(pl.multiple_of(zs * 128, 128), 128)
        for j in range(2):
            values = []
            parts = []
            for h in range(HEADS):
                total = acc[j, h, 64:65, lanes]
                values.append(acc[j, h, 0:64, lanes] * (1.0 / total))
                lse = top[j, h, :, lanes] + jnp.log(total)
                hi = lse.astype(BF16).astype(F32)
                mid = (lse - hi).astype(BF16).astype(F32)
                parts.append(
                    jnp.concatenate([hi, mid, lse - hi - mid, jnp.zeros((5, 128), F32)], axis=0)
                )
            for zb in range(2):
                p = (2 * j + zb) * NZ + zs
                if zb == 0:
                    body_rows = jnp.where(low64, values[0], pltpu.roll(values[1], 64, 1))
                    stat_rows = jnp.where(low8, parts[0], pltpu.roll(parts[1], 64, 1))
                else:
                    body_rows = jnp.where(low64, pltpu.roll(values[0], 64, 1), values[1])
                    stat_rows = jnp.where(low8, pltpu.roll(parts[0], 64, 1), parts[1])
                out[p, 0:64, :] = body_rows.astype(BF16)
                out[p, 64:72, :] = stat_rows.astype(BF16)
        return carry

    lax.fori_loop(0, NZ, send, 0)


def attend(half, idx, used, owner, bias, q, kv, pieces, app, own_vars, fresh_vars, qvar):
    return pl.pallas_call(
        functools.partial(attn_kernel, half),
        out_shape=jax.ShapeDtypeStruct((NY * NZ, 72, 128), BF16),
        in_specs=[smem()] * 4 + [vmem()] + [hbm()] * 5 + [vmem()] * 3,
        out_specs=vmem(),
        scratch_shapes=[
            pltpu.VMEM((26 * PAGE, 256), BF16),
            pltpu.VMEM((2, HEADS, 128, 1024), BF16),
            pltpu.VMEM((2, HEADS, 1, 1024), F32),
            pltpu.VMEM((2, HEADS, 80, 1024), F32),
            pltpu.VMEM((3, 16, 128), BF16),
            pltpu.VMEM((26, 1, 128), F32),
            pltpu.VMEM((128, 1024), F32),
            pltpu.SMEM((NY * SLOTS + 2,), jnp.int32),
            pltpu.SemaphoreType.DMA((13,)),
        ],
        compiler_params=params(56),
        cost_estimate=pl.CostEstimate(
            flops=7_000_000_000, bytes_accessed=6_000_000, transcendentals=7_000_000
        ),
    )(idx, used, owner, bias, q, kv, *pieces, app, own_vars, fresh_vars, qvar)


def final_kernel(idx, parts_a, parts_b, tokens, late, app_all, gain, hidden_out, logits_out, stats_out, app_out, wo, wh, head_in, sem):
    copies = [
        pltpu.make_async_copy(late.at[:, :, pl.ds(0, 32), :], wo, sem.at[0]),
        pltpu.make_async_copy(late.at[:, :, pl.ds(32, 8), :], wh, sem.at[1]),
    ]
    own = pl.ds(pl.multiple_of(idx[1] * ROWS, ROWS), ROWS)
    for ys in range(NY):
        for half in range(2):
            copies.append(
                pltpu.make_async_copy(
                    app_all.at[ys, own, pl.ds(half * 256, 256)],
                    app_out.at[:, pl.ds(half * 1024 + ys * 256, 256)],
                    sem.at[2 + 2 * ys + half],
                )
            )
    for c in copies:
        c.start()
    low64 = lax.broadcasted_iota(jnp.int32, (64, 128), 1) < 64
    merged = []
    for g in range(NR):
        parts = parts_a if g % 2 == 0 else parts_b
        sources = [(g // 2) * NZ + zs for zs in range(NZ)]
        lses = []
        for p in sources:
            stat = parts[p, 64:72, :].astype(F32)
            lses.append(stat[0:1] + stat[1:2] + stat[2:3])
        best = lses[0]
        for v in lses[1:]:
            best = jnp.maximum(best, v)
        ws = [jnp.exp(v - best) for v in lses]
        total = ws[0]
        for w in ws[1:]:
            total = total + w
        inverse = 1.0 / total
        value = None
        for p, w in zip(sources, ws):
            term = parts[p, 0:64, :].astype(F32) * (w * inverse)
            value = term if value is None else value + term
        merged.append(value)
    chunks = []
    for g in range(0, NR, 2):
        turned = jnp.concatenate([merged[g], merged[g + 1]], axis=0).T
        upper = turned[0:64, :]
        lower = turned[64:128, :]
        chunks.append(jnp.where(low64, upper, pltpu.roll(lower, 64, 1)).astype(BF16))
        chunks.append(jnp.where(low64, pltpu.roll(upper, 64, 1), lower).astype(BF16))
    for c in copies:
        c.wait()
    total = tokens[...].astype(F32)
    for r in range(NR):
        total = total + dot_last(chunks[r], wo[r].reshape(1024, 128))
    hidden = total.astype(BF16)
    hidden_out[...] = hidden
    wide = hidden.astype(F32)
    square = wide * wide
    power = jnp.sum(square, axis=1, keepdims=True)
    head_in[...] = (wide * lax.rsqrt(power * (1.0 / 1024) + EPSILON) * gain[...]).astype(BF16)
    logits = None
    for r in range(NR):
        part = dot_last(head_in[:, r * 128 : (r + 1) * 128], wh[r].reshape(256, 128))
        logits = part if logits is None else logits + part
    logits_out[...] = logits.astype(BF16)
    energy = jnp.sum(power, axis=0, keepdims=True)
    peak = jnp.max(jnp.max(logits, axis=1, keepdims=True), axis=0, keepdims=True)
    row = lax.broadcasted_iota(jnp.int32, (8, 128), 0)
    tile = jnp.where(row == 0, energy, jnp.where(row == 1, peak, 0.0))
    for p in range(NY * NZ):
        stats_out[p * 8 : (p + 1) * 8, :] = tile


def finish(idx, parts_a, parts_b, tokens, late, app_all, gain):
    return pl.pallas_call(
        final_kernel,
        out_shape=[
            jax.ShapeDtypeStruct((ROWS, 1024), BF16),
            jax.ShapeDtypeStruct((ROWS, 256), BF16),
            jax.ShapeDtypeStruct((NY * NZ * 8, 128), F32),
            jax.ShapeDtypeStruct((ROWS, 2048), BF16),
        ],
        in_specs=[smem(), vmem(), vmem(), vmem(), hbm(), hbm(), vmem()],
        out_specs=[vmem()] * 4,
        scratch_shapes=[
            pltpu.VMEM((NR, NY * NZ, 32, 128), BF16),
            pltpu.VMEM((NR, NY * NZ, 8, 128), BF16),
            pltpu.VMEM((ROWS, 1024), BF16),
            pltpu.SemaphoreType.DMA((10,)),
        ],
        compiler_params=params(56),
    )(idx, parts_a, parts_b, tokens, late, app_all, gain)


def stats_kernel(stats, norm_out, peak_out):
    half = NY * NZ * 4
    for j in range(2):
        block = stats[j * half : (j + 1) * half, :].reshape(NY * NZ // 2, 8, 128)
        norm_out[j] = jnp.sqrt(jnp.sum(block, axis=0))[0, 0]
        peak_out[j] = jnp.max(block, axis=0)[1, 0]


def gather_stats(stats):
    return pl.pallas_call(
        stats_kernel,
        out_shape=[jax.ShapeDtypeStruct((2,), F32)] * 2,
        in_specs=[vmem()],
        out_specs=[smem()] * 2,
        compiler_params=params(4),
    )(stats)


def slot_table(table_rows, pages_held, slot_ids):
    request_count, page_count = table_rows.shape
    matches = table_rows[:, :, None] == slot_ids[None, None, :]
    live = jnp.arange(page_count, dtype=jnp.int32)[None, :, None] < pages_held[:, None, None]
    hits = jnp.any(matches & live, axis=1)
    used = jnp.any(hits, axis=0).astype(jnp.int32)
    owner = jnp.sum(
        jnp.where(hits, jnp.arange(request_count, dtype=jnp.int32)[:, None], 0), axis=0
    )
    return used, owner


def kv_target(p):
    head = p % 16
    return (head // 4) * NZ + head % 4 + (4 if p >= 16 else 0)


def per_device(
    tokens,
    variate_ids,
    cache_pages,
    page_table,
    kv_cache,
    cache_variates,
    attn_gain,
    w_query,
    w_keyval,
    w_out,
    variate_bias,
    head_gain,
    w_head,
):
    r = lax.axis_index("req")
    y = lax.axis_index("y")
    z = lax.axis_index("z")
    idx = jnp.stack([r, y, z]).astype(jnp.int32)

    kv_cols = lax.ppermute(w_keyval.T, ("y", "z"), [(p, kv_target(p)) for p in range(NY * NZ)])

    kv_rows = kv_cache.reshape(SLOTS * PAGE, 2048)
    *carved, own = carve(idx, kv_rows, cache_variates, tokens, attn_gain.reshape(1, -1))
    pieces = [shift("y", NY, d)(carved[d - 1]) for d in range(1, NY)]
    opposite = shift("y", NY, 2)(own)

    w_local = jnp.concatenate([w_query.T, kv_cols, w_out.T, w_head.T], axis=0)
    w_z = lax.all_to_all(
        jnp.broadcast_to(w_local[None], (NZ, 136, 128)), "z", 0, 0, tiled=True
    )
    w_all = lax.all_to_all(
        jnp.broadcast_to(w_z[None, :, 0:96, :], (NR, NZ, 96, 128)), "req", 0, 0, tiled=True
    )
    late = lax.all_gather(w_z[:, 96:136, :], ("req", "y"), axis=0).reshape(NR, NY * NZ, 40, 128)

    columns = jnp.transpose(variate_ids.reshape(NY, NZ, ROWS), (1, 0, 2)).reshape(NZ, 1, 256)
    fresh_vars = lax.dynamic_index_in_dim(columns, z, 0, keepdims=False).reshape(2, 128)
    order = (y + NY - jnp.arange(NY, dtype=jnp.int32)) % NY
    slot_ids = (
        (order[:, None] * NZ + z) * SLOTS + jnp.arange(SLOTS, dtype=jnp.int32)[None, :]
    ).reshape(-1)
    used, owner = slot_table(page_table, cache_pages, slot_ids)

    lane = jnp.arange(256, dtype=jnp.int32)
    source = lane // ROWS
    positions = (
        jnp.where(source // 2 == 0, cache_pages[0], cache_pages[1]) * PAGE
        + ((source % 2) * NZ + z) * ROWS
        + lane % ROWS
    )
    steps = jnp.arange(32, dtype=F32) / 32
    freqs = jnp.exp(-math.log(10000.0) * steps)
    angle = positions.astype(F32)[None, :] * freqs[:, None]

    first_half, second_half, app = project(
        idx, own, pieces[0], opposite, pieces[2], w_all.reshape(NR, NZ * 96, 128), jnp.cos(angle), jnp.sin(angle)
    )
    app_all = lax.all_gather(app, "y", axis=0)
    shared = (kv_rows, pieces, app, cache_variates, fresh_vars, columns)
    q_a = lax.all_to_all(first_half, "z", 0, 0, tiled=True)
    q_a, late, second_half = lax.optimization_barrier((q_a, late, second_half))
    q_b = lax.all_to_all(second_half, "z", 0, 0, tiled=True)
    sent_a = attend(0, idx, used, owner, variate_bias, q_a, *shared)
    sent_a, q_b = lax.optimization_barrier((sent_a, q_b))
    parts_a = lax.all_to_all(sent_a, ("y", "z"), 0, 0, tiled=True)
    sent_b = attend(1, idx, used, owner, variate_bias, q_b, *shared)
    sent_b, parts_a, app_all = lax.optimization_barrier((sent_b, parts_a, app_all))
    parts_b = lax.all_to_all(sent_b, ("y", "z"), 0, 0, tiled=True)
    hidden, logits, stats, appended = finish(
        idx, parts_a, parts_b, tokens, late, app_all, head_gain.reshape(1, -1)
    )
    norm, peak = gather_stats(lax.all_to_all(stats, ("y", "z"), 0, 0, tiled=True))
    return hidden, appended, logits, norm, peak


def solution(mesh):
    grid = Mesh(mesh.devices.reshape(NR, NY, NZ), ("req", "y", "z"))
    every = ("req", "y", "z")
    pg = ("y", "z")
    placed = (
        P(every, None),
        P("req"),
        P("req"),
        P("req", None),
        P(every, None, None),
        P(every, None),
        P(),
        P("req", pg),
        P("req", pg),
        P("req", pg),
        P(),
        P(),
        P("req", pg),
    )
    return jax.shard_map(
        per_device,
        mesh=grid,
        in_specs=placed,
        out_specs=(P(every, None), P(every, None), P(every, None), P("req"), P("req")),
        check_vma=False,
    )
```

```python
import functools
import math

import jax
import jax.numpy as jnp
from jax import lax
from jax.experimental import pallas as pl
from jax.experimental.pallas import tpu as pltpu
from jax.sharding import Mesh
from jax.sharding import PartitionSpec as P

PAGE = 128
EPSILON = 1e-05
NEGATIVE = -1e30
NY = 4
NZ = 8
NR = 8
SLOTS = 6
ROWS = 64
HEADS = 2
PIECE = SLOTS * 128 + 16 + 2 * ROWS
DH = 64
F32 = jnp.float32
BF16 = jnp.bfloat16


def shift(axis, size, step):
    return lambda value: lax.ppermute(
        value, axis, [(i, (i + step) % size) for i in range(size)]
    )


def vmem():
    return pl.BlockSpec(memory_space=pltpu.VMEM)


def smem():
    return pl.BlockSpec(memory_space=pltpu.SMEM)


def hbm():
    return pl.BlockSpec(memory_space=pltpu.HBM)


def params(mib):
    return pltpu.CompilerParams(vmem_limit_bytes=mib * 1024 * 1024)


def dot_last(a, b):
    return lax.dot_general(a, b, (((1,), (1,)), ((), ())), preferred_element_type=F32)


def carve_kernel(idx, kv, variates, tokens, gain, *refs):
    outs = refs[0:3]
    own = refs[3]
    side, sem = refs[4:6]
    y = idx[1]
    rows = SLOTS * PAGE
    side[...] = jnp.zeros(side.shape, BF16)
    side[0:8, 0:128] = jnp.concatenate(
        [variates[...].astype(F32), jnp.zeros((2, 128), F32)], axis=0
    ).astype(BF16)
    copies = []
    for d in range(1, NY):
        yd = lax.rem(y + d, NY)
        for half in range(2):
            low = pl.multiple_of(half * 1024 + yd * 256, 256)
            copies.append(
                pltpu.make_async_copy(
                    kv.at[:, pl.ds(low, 256)],
                    outs[d - 1].at[pl.ds(0, rows), pl.ds(half * 256, 256)],
                    sem.at[2 * d - 2 + half],
                )
            )
    for c in copies:
        c.start()
    wide = tokens[...].astype(F32)
    power = jnp.sum(wide * wide, axis=1, keepdims=True) * (1.0 / 1024)
    normed = (wide * lax.rsqrt(power + EPSILON) * gain[...]).astype(BF16)
    own[...] = normed
    for d in range(1, NY):
        outs[d - 1][rows : rows + 16, :] = side[...]
        if d != 2:
            outs[d - 1][rows + 16 : rows + 80, :] = normed[:, 0:512]
            outs[d - 1][rows + 80 : rows + 144, :] = normed[:, 512:1024]
    for c in copies:
        c.wait()


def carve(idx, kv, variates, tokens, gain):
    return pl.pallas_call(
        carve_kernel,
        out_shape=[
            jax.ShapeDtypeStruct((PIECE if d != 2 else SLOTS * PAGE + 16, 512), BF16)
            for d in range(1, NY)
        ]
        + [jax.ShapeDtypeStruct((ROWS, 1024), BF16)],
        in_specs=[smem(), hbm()] + [vmem()] * 3,
        out_specs=[vmem()] * 4,
        scratch_shapes=[pltpu.VMEM((16, 512), BF16), pltpu.SemaphoreType.DMA((6,))],
        compiler_params=params(56),
    )(idx, kv, variates, tokens, gain)


def qkv_kernel(idx, own, p1, opposite, p3, w_hbm, cos_ref, sin_ref, q_first, q_second, app_out, tok, w, acc, feats, sem):
    y = idx[1]
    base = SLOTS * PAGE + 16
    copies = [
        pltpu.make_async_copy(
            own, tok.at[pl.ds(pl.multiple_of(y * ROWS, ROWS), ROWS), :], sem.at[NR]
        ),
        pltpu.make_async_copy(
            opposite,
            tok.at[pl.ds(pl.multiple_of(lax.rem(y + 2, NY) * ROWS, ROWS), ROWS), :],
            sem.at[NR + 3],
        ),
    ]
    for d, piece in ((0, p1), (2, p3)):
        ys = lax.rem(y + NY - d - 1, NY)
        for half in range(2):
            copies.append(
                pltpu.make_async_copy(
                    piece.at[pl.ds(base + half * ROWS, ROWS)],
                    tok.at[
                        pl.ds(pl.multiple_of(ys * ROWS, ROWS), ROWS), pl.ds(half * 512, 512)
                    ],
                    sem.at[NR + 1 + 2 * d + half],
                )
            )
    blocks = [pltpu.make_async_copy(w_hbm.at[r], w.at[r], sem.at[r]) for r in range(NR)]
    for c in copies + blocks:
        c.start()
    for c in copies:
        c.wait()
    for r in range(NR):
        blocks[r].wait()
        part = dot_last(w[r], tok[:, r * 128 : (r + 1) * 128])
        if r == 0:
            acc[...] = part
        else:
            acc[...] += part
    cos = cos_ref[...]
    sin = sin_ref[...]

    def rounded(zs, low, high):
        return acc[zs * 96 + low : zs * 96 + high, :].astype(BF16).astype(F32)

    for h in range(4):
        a = rounded(2 * h, 0, 32)
        b = rounded(2 * h + 1, 0, 32)
        first = ((a * cos - b * sin).astype(BF16).astype(F32) * 0.125).astype(BF16)
        second = ((b * cos + a * sin).astype(BF16).astype(F32) * 0.125).astype(BF16)
        q_out = q_first if h < 2 else q_second
        low = (h % 2) * 64
        for zs in range(NZ):
            q_out[zs, low : low + 32, :] = first
            q_out[zs, low + 32 : low + 64, :] = second
        a = rounded(h, 32, 64)
        b = rounded(h, 64, 96)
        feats[h * 64 : h * 64 + 32, :] = a * cos - b * sin
        feats[h * 64 + 32 : h * 64 + 64, :] = b * cos + a * sin
        feats[256 + h * 64 : 256 + h * 64 + 64, :] = acc[(4 + h) * 96 + 32 : (4 + h) * 96 + 96, :]
    app_out[:, 0:256] = feats[0:256, :].T.astype(BF16)
    app_out[:, 256:512] = feats[256:512, :].T.astype(BF16)


def project(idx, own, p1, opposite, p3, w, cos, sin):
    return pl.pallas_call(
        qkv_kernel,
        out_shape=[
            jax.ShapeDtypeStruct((NZ, 128, 256), BF16),
            jax.ShapeDtypeStruct((NZ, 128, 256), BF16),
            jax.ShapeDtypeStruct((256, 512), BF16),
        ],
        in_specs=[smem()] + [hbm()] * 5 + [vmem()] * 2,
        out_specs=[vmem()] * 3,
        scratch_shapes=[
            pltpu.VMEM((256, 1024), BF16),
            pltpu.VMEM((NR, NZ * 96, 128), BF16),
            pltpu.VMEM((NZ * 96, 256), F32),
            pltpu.VMEM((512, 256), F32),
            pltpu.SemaphoreType.DMA((NR + 7,)),
        ],
        compiler_params=params(56),
    )(idx, own, p1, opposite, p3, w, cos, sin)


def attn_kernel(half, idx, used, owner, bias, *refs):
    q, kv, p1, p2, p3, app, own_vars, fresh_vars, qvar = refs[0:9]
    out = refs[9]
    pg, qb, top, acc, side, kvs, causal, order, sem = refs[10:19]
    y, z = idx[1], idx[2]
    rows = SLOTS * PAGE
    fresh_base = NY * SLOTS
    copies = []

    def fetch(source, target):
        copies.append(pltpu.make_async_copy(source, target, sem.at[len(copies)]))

    for side_col in range(2):
        cols = pl.ds(side_col * 128, 128)
        low = pl.multiple_of(side_col * 1024 + y * 256 + half * 128, 128)
        fetch(kv.at[:, pl.ds(low, 128)], pg.at[pl.ds(0, rows), cols])
        source_cols = pl.ds(side_col * 256 + half * 128, 128)
        for d, piece in enumerate((p1, p2, p3)):
            fetch(
                piece.at[pl.ds(0, rows), source_cols], pg.at[pl.ds((d + 1) * rows, rows), cols]
            )
        fetch(app.at[:, source_cols], pg.at[pl.ds(NY * rows, 256), cols])
    for d, piece in enumerate((p1, p2, p3)):
        fetch(piece.at[pl.ds(rows, 16), pl.ds(0, 128)], side.at[d])
    for c in copies:
        c.start()

    def collect(slot, count):
        order[count] = slot
        return count + used[slot]

    count = lax.fori_loop(0, fresh_base, collect, 0)

    row16 = lax.broadcasted_iota(jnp.int32, (16, 128), 0)
    vsel = row16 & 3
    level = row16 >> 2
    zero = jnp.zeros((48, 128), BF16)

    def fill(zs, carry):
        lanes = pl.ds(pl.multiple_of(zs * 128, 128), 128)
        qv_row = qvar[zs]
        for j in range(2):
            same = jnp.broadcast_to(qv_row[:, j * 128 : (j + 1) * 128], (16, 128)) == vsel
            for h in range(HEADS):
                hh = y * 4 + half * 2 + h
                b = jnp.where(same, bias[0, hh], bias[1, hh])
                hi = b.astype(BF16).astype(F32)
                mid = (b - hi).astype(BF16).astype(F32)
                lo = (b - hi - mid).astype(BF16).astype(F32)
                extra = jnp.where(
                    level == 0, hi, jnp.where(level == 1, mid, jnp.where(level == 2, lo, 0.0))
                ).astype(BF16)
                q_rows = q[zs, h * 64 : (h + 1) * 64, j * 128 : (j + 1) * 128]
                if h % 2 == 0:
                    qb[j, h, 0:64, lanes] = q_rows
                    qb[j, h, 64:80, lanes] = extra
                    qb[j, h, 80:128, lanes] = zero
                else:
                    qb[j, h, 0:16, lanes] = extra
                    qb[j, h, 16:64, lanes] = zero
                    qb[j, h, 64:128, lanes] = q_rows
        key_row = lax.broadcasted_iota(jnp.int32, (128, 128), 0)
        q_lane = lax.broadcasted_iota(jnp.int32, (128, 128), 1)
        key_pos = ((key_row >> 6) * NZ + z) * ROWS + (key_row & 63)
        q_pos = ((q_lane >> 6) * NZ + zs) * ROWS + (q_lane & 63)
        causal[:, lanes] = jnp.where(key_pos <= q_pos, 0.0, NEGATIVE)
        return carry

    lax.fori_loop(0, NZ, fill, 0)
    top[...] = jnp.full(top.shape, NEGATIVE, F32)
    acc[...] = jnp.zeros(acc.shape, F32)
    for s in range(SLOTS):
        kvs[s] = own_vars[s : s + 1, :].astype(F32)
    for j in range(2):
        kvs[NY * SLOTS + j] = fresh_vars[j : j + 1, :].astype(F32)
    for c in copies:
        c.wait()
    for d in range(3):
        block = side[d].astype(F32)
        for s in range(SLOTS):
            kvs[(d + 1) * SLOTS + s] = block[s : s + 1, :]

    sub = lax.broadcasted_iota(jnp.int32, (128, 128), 0)
    variate = (sub & 3).astype(F32)
    hot_rows = (sub & 63) < 12
    low_lanes = lax.broadcasted_iota(jnp.int32, (128, 128), 1) < 64
    ones = jnp.ones((16, 128), BF16)

    def visit(slots, js, fresh):
        tiles = []
        for n, slot in enumerate(slots):
            page = pg[pl.ds(pl.multiple_of(slot * PAGE, PAGE), PAGE), :]
            kvals = jnp.broadcast_to(kvs[slot], (128, 128))
            hot = jnp.where(hot_rows & (variate == kvals), 1.0, 0.0).T
            pair = page[:, 0:128].astype(F32)
            vals = page[:, 128:256].astype(F32).T.astype(BF16)
            for h in range(HEADS):
                both = (pair, hot) if h == 0 else (hot, pair)
                kaug = jnp.where(low_lanes, both[0], both[1]).astype(BF16)
                vaug = jnp.concatenate([vals[h * 64 : (h + 1) * 64, :], ones], axis=0)
                tiles.append((n, js[n], h, kaug, vaug))
        total = len(tiles)
        scores = {}
        weights = {}
        for i in range(total + 2):
            if i < total:
                n, j, h, kaug, _ = tiles[i]
                s = jnp.dot(kaug, qb[j, h], preferred_element_type=F32)
                scores[i] = s + causal[...] if fresh else s
            if 1 <= i <= total:
                n, j, h, _, _ = tiles[i - 1]
                s = scores.pop(i - 1)
                old = top[j, h]
                new = jnp.maximum(old, jnp.max(s, axis=0, keepdims=True))
                top[j, h] = new
                weights[i - 1] = (jnp.exp(s - new).astype(BF16), jnp.exp(old - new))
            if i >= 2:
                n, j, h, _, vaug = tiles[i - 2]
                p, keep = weights.pop(i - 2)
                acc[j, h] = acc[j, h] * keep + jnp.dot(vaug, p, preferred_element_type=F32)

    def body(i, carry):
        a = order[2 * i]
        b = order[2 * i + 1]
        visit([a, b], [owner[a], owner[b]], False)
        return carry

    lax.fori_loop(0, count // 2, body, 0)

    @pl.when(count % 2 == 1)
    def _():
        a = order[count - 1]
        visit([a], [owner[a]], False)

    visit([fresh_base, fresh_base + 1], [0, 1], True)

    low64 = lax.broadcasted_iota(jnp.int32, (64, 128), 1) < 64
    low8 = lax.broadcasted_iota(jnp.int32, (8, 128), 1) < 64

    def send(zs, carry):
        lanes = pl.ds(pl.multiple_of(zs * 128, 128), 128)
        for j in range(2):
            values = []
            parts = []
            for h in range(HEADS):
                total = acc[j, h, 64:65, lanes]
                values.append(acc[j, h, 0:64, lanes] * (1.0 / total))
                lse = top[j, h, :, lanes] + jnp.log(total)
                hi = lse.astype(BF16).astype(F32)
                mid = (lse - hi).astype(BF16).astype(F32)
                parts.append(
                    jnp.concatenate([hi, mid, lse - hi - mid, jnp.zeros((5, 128), F32)], axis=0)
                )
            for zb in range(2):
                p = (2 * j + zb) * NZ + zs
                if zb == 0:
                    body_rows = jnp.where(low64, values[0], pltpu.roll(values[1], 64, 1))
                    stat_rows = jnp.where(low8, parts[0], pltpu.roll(parts[1], 64, 1))
                else:
                    body_rows = jnp.where(low64, pltpu.roll(values[0], 64, 1), values[1])
                    stat_rows = jnp.where(low8, pltpu.roll(parts[0], 64, 1), parts[1])
                out[p, 0:64, :] = body_rows.astype(BF16)
                out[p, 64:72, :] = stat_rows.astype(BF16)
        return carry

    lax.fori_loop(0, NZ, send, 0)


def attend(half, idx, used, owner, bias, q, kv, pieces, app, own_vars, fresh_vars, qvar):
    return pl.pallas_call(
        functools.partial(attn_kernel, half),
        out_shape=jax.ShapeDtypeStruct((NY * NZ, 72, 128), BF16),
        in_specs=[smem()] * 4 + [vmem()] + [hbm()] * 5 + [vmem()] * 3,
        out_specs=vmem(),
        scratch_shapes=[
            pltpu.VMEM((26 * PAGE, 256), BF16),
            pltpu.VMEM((2, HEADS, 128, 1024), BF16),
            pltpu.VMEM((2, HEADS, 1, 1024), F32),
            pltpu.VMEM((2, HEADS, 80, 1024), F32),
            pltpu.VMEM((3, 16, 128), BF16),
            pltpu.VMEM((26, 1, 128), F32),
            pltpu.VMEM((128, 1024), F32),
            pltpu.SMEM((NY * SLOTS + 2,), jnp.int32),
            pltpu.SemaphoreType.DMA((13,)),
        ],
        compiler_params=params(56),
        cost_estimate=pl.CostEstimate(
            flops=7_000_000_000, bytes_accessed=6_000_000, transcendentals=7_000_000
        ),
    )(idx, used, owner, bias, q, kv, *pieces, app, own_vars, fresh_vars, qvar)


def merged_chunks(parts):
    low64 = lax.broadcasted_iota(jnp.int32, (64, 128), 1) < 64
    merged = []
    for ys in range(NY):
        sources = [ys * NZ + zs for zs in range(NZ)]
        lses = []
        for p in sources:
            stat = parts[p, 64:72, :].astype(F32)
            lses.append(stat[0:1] + stat[1:2] + stat[2:3])
        best = lses[0]
        for v in lses[1:]:
            best = jnp.maximum(best, v)
        ws = [jnp.exp(v - best) for v in lses]
        total = ws[0]
        for w in ws[1:]:
            total = total + w
        inverse = 1.0 / total
        value = None
        for p, w in zip(sources, ws):
            term = parts[p, 0:64, :].astype(F32) * (w * inverse)
            value = term if value is None else value + term
        merged.append(value)
    chunks = []
    for g in range(0, NY, 2):
        turned = jnp.concatenate([merged[g], merged[g + 1]], axis=0).T
        upper = turned[0:64, :]
        lower = turned[64:128, :]
        chunks.append(jnp.where(low64, upper, pltpu.roll(lower, 64, 1)).astype(BF16))
        chunks.append(jnp.where(low64, pltpu.roll(upper, 64, 1), lower).astype(BF16))
    return chunks


def half_kernel(idx, parts, tokens, late, app_all, total_out, app_out, wo, sem):
    own = pl.ds(pl.multiple_of(idx[1] * ROWS, ROWS), ROWS)
    copies = []
    for ys in range(NY):
        copies.append(
            pltpu.make_async_copy(
                late.at[2 * ys, :, pl.ds(0, 32), :], wo.at[ys], sem.at[8 + ys]
            )
        )
        for half in range(2):
            copies.append(
                pltpu.make_async_copy(
                    app_all.at[ys, own, pl.ds(half * 256, 256)],
                    app_out.at[:, pl.ds(half * 1024 + ys * 256, 256)],
                    sem.at[2 * ys + half],
                )
            )
    for c in copies:
        c.start()
    chunks = merged_chunks(parts)
    for c in copies:
        c.wait()
    total = tokens[...].astype(F32)
    for ys in range(NY):
        total = total + dot_last(chunks[ys], wo[ys].reshape(1024, 128))
    total_out[...] = total


def half_finish(idx, parts, tokens, late, app_all):
    return pl.pallas_call(
        half_kernel,
        out_shape=[
            jax.ShapeDtypeStruct((ROWS, 1024), F32),
            jax.ShapeDtypeStruct((ROWS, 2048), BF16),
        ],
        in_specs=[smem(), vmem(), vmem(), hbm(), hbm()],
        out_specs=[vmem()] * 2,
        scratch_shapes=[
            pltpu.VMEM((NY, NY * NZ, 32, 128), BF16),
            pltpu.SemaphoreType.DMA((12,)),
        ],
        compiler_params=params(56),
        cost_estimate=pl.CostEstimate(
            flops=500_000_000, bytes_accessed=3_000_000, transcendentals=4096
        ),
    )(idx, parts, tokens, late, app_all)


def final_kernel(parts, first, late, gain, hidden_out, logits_out, stats_out, wo, wh, head_in, sem):
    copies = [
        pltpu.make_async_copy(late.at[2 * ys + 1, :, pl.ds(0, 32), :], wo.at[ys], sem.at[ys])
        for ys in range(NY)
    ] + [pltpu.make_async_copy(late.at[:, :, pl.ds(32, 8), :], wh, sem.at[NY])]
    for c in copies:
        c.start()
    chunks = merged_chunks(parts)
    for c in copies:
        c.wait()
    total = first[...]
    for ys in range(NY):
        total = total + dot_last(chunks[ys], wo[ys].reshape(1024, 128))
    hidden = total.astype(BF16)
    hidden_out[...] = hidden
    wide = hidden.astype(F32)
    square = wide * wide
    power = jnp.sum(square, axis=1, keepdims=True)
    head_in[...] = (wide * lax.rsqrt(power * (1.0 / 1024) + EPSILON) * gain[...]).astype(BF16)
    logits = None
    for r in range(NR):
        part = dot_last(head_in[:, r * 128 : (r + 1) * 128], wh[r].reshape(256, 128))
        logits = part if logits is None else logits + part
    logits_out[...] = logits.astype(BF16)
    energy = jnp.sum(power, axis=0, keepdims=True)
    peak = jnp.max(jnp.max(logits, axis=1, keepdims=True), axis=0, keepdims=True)
    row = lax.broadcasted_iota(jnp.int32, (8, 128), 0)
    tile = jnp.where(row == 0, energy, jnp.where(row == 1, peak, 0.0))
    for p in range(NY * NZ):
        stats_out[p * 8 : (p + 1) * 8, :] = tile


def finish(parts, first, late, gain):
    return pl.pallas_call(
        final_kernel,
        out_shape=[
            jax.ShapeDtypeStruct((ROWS, 1024), BF16),
            jax.ShapeDtypeStruct((ROWS, 256), BF16),
            jax.ShapeDtypeStruct((NY * NZ * 8, 128), F32),
        ],
        in_specs=[vmem(), vmem(), hbm(), vmem()],
        out_specs=[vmem()] * 3,
        scratch_shapes=[
            pltpu.VMEM((NY, NY * NZ, 32, 128), BF16),
            pltpu.VMEM((NR, NY * NZ, 8, 128), BF16),
            pltpu.VMEM((ROWS, 1024), BF16),
            pltpu.SemaphoreType.DMA((5,)),
        ],
        compiler_params=params(56),
    )(parts, first, late, gain)


def stats_kernel(stats, norm_out, peak_out):
    half = NY * NZ * 4
    for j in range(2):
        block = stats[j * half : (j + 1) * half, :].reshape(NY * NZ // 2, 8, 128)
        norm_out[j] = jnp.sqrt(jnp.sum(block, axis=0))[0, 0]
        peak_out[j] = jnp.max(block, axis=0)[1, 0]


def gather_stats(stats):
    return pl.pallas_call(
        stats_kernel,
        out_shape=[jax.ShapeDtypeStruct((2,), F32)] * 2,
        in_specs=[vmem()],
        out_specs=[smem()] * 2,
        compiler_params=params(4),
    )(stats)


def slot_table(table_rows, pages_held, slot_ids):
    request_count, page_count = table_rows.shape
    matches = table_rows[:, :, None] == slot_ids[None, None, :]
    live = jnp.arange(page_count, dtype=jnp.int32)[None, :, None] < pages_held[:, None, None]
    hits = jnp.any(matches & live, axis=1)
    used = jnp.any(hits, axis=0).astype(jnp.int32)
    owner = jnp.sum(
        jnp.where(hits, jnp.arange(request_count, dtype=jnp.int32)[:, None], 0), axis=0
    )
    return used, owner


def kv_target(p):
    head = p % 16
    return (head // 4) * NZ + head % 4 + (4 if p >= 16 else 0)


def per_device(
    tokens,
    variate_ids,
    cache_pages,
    page_table,
    kv_cache,
    cache_variates,
    attn_gain,
    w_query,
    w_keyval,
    w_out,
    variate_bias,
    head_gain,
    w_head,
):
    r = lax.axis_index("req")
    y = lax.axis_index("y")
    z = lax.axis_index("z")
    idx = jnp.stack([r, y, z]).astype(jnp.int32)

    kv_cols = lax.ppermute(w_keyval.T, ("y", "z"), [(p, kv_target(p)) for p in range(NY * NZ)])

    kv_rows = kv_cache.reshape(SLOTS * PAGE, 2048)
    *carved, own = carve(idx, kv_rows, cache_variates, tokens, attn_gain.reshape(1, -1))
    pieces = [shift("y", NY, d)(carved[d - 1]) for d in range(1, NY)]
    opposite = shift("y", NY, 2)(own)

    w_local = jnp.concatenate([w_query.T, kv_cols, w_out.T, w_head.T], axis=0)
    w_z = lax.all_to_all(
        jnp.broadcast_to(w_local[None], (NZ, 136, 128)), "z", 0, 0, tiled=True
    )
    w_all = lax.all_to_all(
        jnp.broadcast_to(w_z[None, :, 0:96, :], (NR, NZ, 96, 128)), "req", 0, 0, tiled=True
    )
    late = lax.all_gather(w_z[:, 96:136, :], ("req", "y"), axis=0).reshape(NR, NY * NZ, 40, 128)

    columns = jnp.transpose(variate_ids.reshape(NY, NZ, ROWS), (1, 0, 2)).reshape(NZ, 1, 256)
    fresh_vars = lax.dynamic_index_in_dim(columns, z, 0, keepdims=False).reshape(2, 128)
    order = (y + NY - jnp.arange(NY, dtype=jnp.int32)) % NY
    slot_ids = (
        (order[:, None] * NZ + z) * SLOTS + jnp.arange(SLOTS, dtype=jnp.int32)[None, :]
    ).reshape(-1)
    used, owner = slot_table(page_table, cache_pages, slot_ids)

    lane = jnp.arange(256, dtype=jnp.int32)
    source = lane // ROWS
    positions = (
        jnp.where(source // 2 == 0, cache_pages[0], cache_pages[1]) * PAGE
        + ((source % 2) * NZ + z) * ROWS
        + lane % ROWS
    )
    steps = jnp.arange(32, dtype=F32) / 32
    freqs = jnp.exp(-math.log(10000.0) * steps)
    angle = positions.astype(F32)[None, :] * freqs[:, None]

    first_half, second_half, app = project(
        idx, own, pieces[0], opposite, pieces[2], w_all.reshape(NR, NZ * 96, 128), jnp.cos(angle), jnp.sin(angle)
    )
    app_all = lax.all_gather(app, "y", axis=0)
    shared = (kv_rows, pieces, app, cache_variates, fresh_vars, columns)
    q_a = lax.all_to_all(first_half, "z", 0, 0, tiled=True)
    q_a, late, second_half = lax.optimization_barrier((q_a, late, second_half))
    q_b = lax.all_to_all(second_half, "z", 0, 0, tiled=True)
    sent_a = attend(0, idx, used, owner, variate_bias, q_a, *shared)
    sent_a, q_b = lax.optimization_barrier((sent_a, q_b))
    parts_a = lax.all_to_all(sent_a, ("y", "z"), 0, 0, tiled=True)
    sent_b = attend(1, idx, used, owner, variate_bias, q_b, *shared)
    sent_b, parts_a, app_all = lax.optimization_barrier((sent_b, parts_a, app_all))
    parts_b = lax.all_to_all(sent_b, ("y", "z"), 0, 0, tiled=True)
    first, appended = half_finish(idx, parts_a, tokens, late, app_all)
    hidden, logits, stats = finish(parts_b, first, late, head_gain.reshape(1, -1))
    norm, peak = gather_stats(lax.all_to_all(stats, ("y", "z"), 0, 0, tiled=True))
    return hidden, appended, logits, norm, peak


def solution(mesh):
    grid = Mesh(mesh.devices.reshape(NR, NY, NZ), ("req", "y", "z"))
    every = ("req", "y", "z")
    pg = ("y", "z")
    placed = (
        P(every, None),
        P("req"),
        P("req"),
        P("req", None),
        P(every, None, None),
        P(every, None),
        P(),
        P("req", pg),
        P("req", pg),
        P("req", pg),
        P(),
        P(),
        P("req", pg),
    )
    return jax.shard_map(
        per_device,
        mesh=grid,
        in_specs=placed,
        out_specs=(P(every, None), P(every, None), P(every, None), P("req"), P("req")),
        check_vma=False,
    )
```
